256 devices in a mesh: rows: 64 (over z, y, core), pairs: 4 (over x).
Axes of the slice: x: 4, y: 4, z: 8, core: 2. Of those that a mesh axis runs over, the one named last changes fastest.
Arguments:
- latent: float32 [131072, 128], P('rows'), may hold values from -2.5 to 2.5
- left_block: int32 [64, 4, 64, 2], P('rows', 'pairs'), may hold values from 0 to 15, as said below
- right_block: int32 [64, 4, 64, 2], P('rows', 'pairs'), may hold values from 0 to 15
- slot_kind: int32 [64, 4, 64, 2], P('rows', 'pairs'), may hold values from 0 to 2, as said below
- edge_cols: int32 [64, 4, 64, 2, 8, 128], P('rows', 'pairs'), may hold values from 0 to 127
Outputs:
- latent_grad: float32 [131072, 128], P(('rows', 'pairs'))
The draws below stay inside these ranges and needn't reach their ends.
Inputs may be any that keep to these rules, and one draw needn't show every extreme that they name: `slot_kind`: exactly the slots whose third index s is lower than the first index r hold 0; every other slot holds 1 or 2. On slots whose third index equals the first, left_block <= right_block, so that every listed pair has its left block at or before its right block.
All inputs are finite; a program needn't handle non-finite values.
Results may differ from the reference program's by a relative error of at most 0.0003.
Values sent between devices are 32-bit elements; how exact they have to be, the bound alone decides.
A program may use at most 128 MiB of HBM per device.

```python
import jax
import jax.numpy as jnp
from jax import lax

DL = 128
BLOCK = 128
BLK_DEV = 16
CAP = 2
NBR = 8
NODES = 131072
N_ROWS = 64
N_PAIRS = 4


def slot_tables(base_key):
    shape = (N_ROWS, N_PAIRS, N_ROWS, CAP)
    source = lax.broadcasted_iota(jnp.int32, shape, 0)
    destination = lax.broadcasted_iota(jnp.int32, shape, 2)
    first = jax.random.randint(jax.random.fold_in(base_key, 11), shape, 0, BLK_DEV)
    second = jax.random.randint(jax.random.fold_in(base_key, 12), shape, 0, BLK_DEV)
    same = source == destination
    left_ids = jnp.where(same, jnp.minimum(first, second), first)
    right_ids = jnp.where(same, jnp.maximum(first, second), second)
    kinds = jax.random.randint(jax.random.fold_in(base_key, 13), shape, 1, 3)
    kinds = jnp.where(destination >= source, kinds, 0)
    return (left_ids.astype(jnp.int32), right_ids.astype(jnp.int32), kinds.astype(jnp.int32))


def draw_left_block(key, part):
    return slot_tables(key)[0]


def draw_right_block(key, part):
    return slot_tables(key)[1]


def draw_slot_kind(key, part):
    return slot_tables(key)[2]


def draw_edge_cols(key, part):
    shape = (N_ROWS, N_PAIRS, N_ROWS, CAP, NBR, BLOCK)
    return jax.random.randint(jax.random.fold_in(key, 14), shape, 0, BLOCK).astype(jnp.int32)


def level_of(key, dims, cuts, smallest, high):
    factor_of, own = 1.0, jax.random.fold_in(key, 6)
    for position, blocks in cuts:
        steps = jnp.exp(jax.random.uniform(jax.random.fold_in(own, position), (blocks,), jnp.float32, smallest / len(cuts), high / len(cuts)))
        factor_of = factor_of * jnp.repeat(steps, dims[position] // blocks).reshape([-1 if axis == position else 1 for axis in range(len(dims))])
    return factor_of


def scatter_about(own_key, shape, scale, bound, pieces=(), kind=jnp.bfloat16):
    entries = scale * jax.random.normal(own_key, shape, jnp.float32)
    if pieces:
        entries = entries * level_of(own_key, shape, pieces, -0.22, 0.18)
    return jnp.clip(entries, -bound, bound).astype(kind)


def setup_inputs(seed: int = 0) -> dict:
    keys = jax.random.split(jax.random.key(seed), 6)
    latent = scatter_about(keys[0], (NODES, DL), 0.35, 2.5, ((0, 64),), jnp.float32)
    left_block = draw_left_block(jax.random.fold_in(keys[5], 71), 0)
    right_block = draw_right_block(jax.random.fold_in(keys[5], 71), 0)
    slot_kind = draw_slot_kind(jax.random.fold_in(keys[5], 71), 0)
    edge_cols = draw_edge_cols(jax.random.fold_in(keys[5], 71), 0)
    return dict(latent=latent, left_block=left_block, right_block=right_block, slot_kind=slot_kind, edge_cols=edge_cols)


def residual(left_rows, right_rows, slot_kinds, edge_ids):
    scores = jnp.einsum('...id,...jd->...ij', left_rows, right_rows, precision=lax.Precision.HIGHEST)
    columns = lax.broadcasted_iota(jnp.int32, scores.shape, scores.ndim - 1)
    target_hit = jnp.zeros(scores.shape, jnp.bool_)
    for which in range(edge_ids.shape[-2]):
        target_hit = target_hit | (edge_ids[..., which, :, None] == columns)
    positive = (slot_kinds == 2)[..., None, None]
    target = jnp.where(target_hit & positive, jnp.ones_like(scores), jnp.zeros_like(scores))
    live = (slot_kinds > 0)[..., None, None]
    return jnp.where(live, jax.nn.sigmoid(scores) - target, jnp.zeros_like(scores))


def reference(latent, left_block, right_block, slot_kind, edge_cols):
    blocks = latent.reshape(N_ROWS * BLK_DEV, BLOCK, DL)

    def one_source(gradient, source):
        left_ids = left_block[source] + source * BLK_DEV
        destination = lax.broadcasted_iota(jnp.int32, left_ids.shape, 1)
        right_ids = right_block[source] + destination * BLK_DEV
        left_rows = blocks[left_ids]
        right_rows = blocks[right_ids]
        residue = residual(left_rows, right_rows, slot_kind[source], edge_cols[source])
        left_grad = jnp.einsum('...ij,...jd->...id', residue, right_rows, precision=lax.Precision.HIGHEST)
        right_grad = jnp.einsum('...ij,...id->...jd', residue, left_rows, precision=lax.Precision.HIGHEST)
        gradient = gradient.at[left_ids.reshape(-1)].add(left_grad.reshape(-1, BLOCK, DL))
        gradient = gradient.at[right_ids.reshape(-1)].add(right_grad.reshape(-1, BLOCK, DL))
        return gradient, None

    gradient, _ = lax.scan(one_source, jnp.zeros(blocks.shape, latent.dtype), jnp.arange(N_ROWS, dtype=jnp.int32))
    return gradient.reshape(NODES, DL)
```

```python
import jax
import jax.numpy as jnp
from jax import lax
from jax.experimental import pallas as pl
from jax.experimental.pallas import tpu as pltpu
from jax.sharding import Mesh
from jax.sharding import PartitionSpec as P

NZ, NY, NC, NX = 8, 4, 2, 4
BLOCKS = 16
QUARTER = 4
TILE = 128
NBR = 8
OWN = NY * BLOCKS
MOVED = NZ * NC * QUARTER
ALL = OWN + MOVED
ROWSET = NZ * NC
CAND = NX * NY * ROWSET
GROUP = 2

NT = (((1,), (1,)), ((), ()))
NN = (((1,), (0,)), ((), ()))


def mm(a, b, dims):
    return lax.dot_general(a, b, dims, preferred_element_type=jnp.float32)


def halves(a):
    high = a.astype(jnp.bfloat16)
    low = (a - high.astype(jnp.float32)).astype(jnp.bfloat16)
    return high, low


def pair_step(left, right, edges, hit_scale):
    lh, ll = halves(left)
    rh, rl = halves(right)
    scores = mm(
        jnp.concatenate([rh, rl], axis=1), jnp.concatenate([lh, lh], axis=1), NT
    ) + mm(rh, ll, NT)
    rows = lax.broadcasted_iota(jnp.int32, (TILE, TILE), 0)
    hit = rows == edges[0:1, :]
    for k in range(1, NBR):
        hit = hit | (rows == edges[k : k + 1, :])
    res = (1.0 / (1.0 + jnp.exp(-scores)) - jnp.where(hit, 1.0, 0.0)) * hit_scale
    rest = res.T
    th, tl = halves(res)
    uh, ul = halves(rest)
    grad_right = mm(
        jnp.concatenate([th, tl], axis=1), jnp.concatenate([lh, lh], axis=0), NN
    ) + mm(th, ll, NN)
    grad_left = mm(
        jnp.concatenate([uh, ul], axis=1), jnp.concatenate([rh, rh], axis=0), NN
    ) + mm(uh, rl, NN)
    return grad_left, grad_right


def compute_kernel(left_ref, right_ref, kind_ref, own_ref, moved_ref, edge_ref,
                   og_ref, mg_ref, blk, grad, ebuf, list_l, list_r, list_e, list_k, sem, esem):
    x = lax.axis_index("x")
    copy_a = pltpu.make_async_copy(own_ref, blk.at[pl.ds(0, OWN)], sem.at[0])
    copy_b = pltpu.make_async_copy(moved_ref, blk.at[pl.ds(OWN, MOVED)], sem.at[1])
    copy_a.start()
    copy_b.start()

    def scan(i, count):
        lb, rb, kind = left_ref[i], right_ref[i], kind_ref[i]
        first = i < CAND
        j = jnp.where(first, i, i - CAND)
        yo = jnp.where(first, lax.rem(j // ROWSET, NY), lax.rem(j, NY))
        zc = jnp.where(first, lax.rem(j, ROWSET), lax.rem(j // NY, ROWSET))
        own_block = jnp.where(first, lb, rb)
        moved_block = jnp.where(first, rb, lb)
        here = moved_block - x * QUARTER
        own_at = yo * BLOCKS + own_block
        moved_at = OWN + zc * QUARTER + here
        list_l[count] = jnp.where(first, own_at, moved_at)
        list_r[count] = jnp.where(first, moved_at, own_at)
        list_e[count] = i
        list_k[count] = kind
        take = (kind > 0) & (here >= 0) & (here < QUARTER)
        return count + jnp.where(take, 1, 0)

    count = lax.fori_loop(0, 2 * CAND, scan, 0)
    for k in range(GROUP):
        list_l[count + k] = ALL
        list_r[count + k] = ALL
        list_e[count + k] = 0
        list_k[count + k] = 0

    def clear(i, carry):
        grad[i] = jnp.zeros((TILE, TILE), jnp.float32)
        return carry

    lax.fori_loop(0, ALL + 1, clear, 0)
    blk[ALL] = jnp.zeros((TILE, TILE), jnp.float32)
    steps = (count + GROUP - 1) // GROUP

    def fetch(step, slot):
        return [
            pltpu.make_async_copy(
                edge_ref.at[list_e[step * GROUP + k]], ebuf.at[slot, k], esem.at[slot, k]
            )
            for k in range(GROUP)
        ]

    copy_a.wait()
    copy_b.wait()

    @pl.when(steps > 0)
    def _():
        for c in fetch(0, 0):
            c.start()

    def work(step, carry):
        slot = lax.rem(step, 2)

        @pl.when(step + 1 < steps)
        def _():
            for c in fetch(step + 1, 1 - slot):
                c.start()

        for c in fetch(step, slot):
            c.wait()
        results = []
        for k in range(GROUP):
            at = step * GROUP + k
            li, ri, kind = list_l[at], list_r[at], list_k[at]
            edges = jnp.where(kind == 2, ebuf[slot, k], -1)
            scale = jnp.where(kind > 0, 1.0, 0.0)
            results.append((li, ri) + pair_step(blk[li], blk[ri], edges, scale))
        for li, ri, gl, gr in results:
            grad[li] += gl
            grad[ri] += gr
        return carry

    lax.fori_loop(0, steps, work, 0)
    out_a = pltpu.make_async_copy(grad.at[pl.ds(0, OWN)], og_ref, sem.at[0])
    out_b = pltpu.make_async_copy(grad.at[pl.ds(OWN, MOVED)], mg_ref, sem.at[1])
    out_a.start()
    out_b.start()
    out_a.wait()
    out_b.wait()


def compute(left, right, kind, own, moved, edges):
    smem = pl.BlockSpec(memory_space=pltpu.SMEM)
    hbm = pl.BlockSpec(memory_space=pl.ANY)
    return pl.pallas_call(
        compute_kernel,
        out_shape=(
            jax.ShapeDtypeStruct((OWN, TILE, TILE), jnp.float32),
            jax.ShapeDtypeStruct((MOVED, TILE, TILE), jnp.float32),
        ),
        in_specs=[smem, smem, smem, hbm, hbm, hbm],
        out_specs=(hbm, hbm),
        scratch_shapes=[
            pltpu.VMEM((ALL + 1, TILE, TILE), jnp.float32),
            pltpu.VMEM((ALL + 1, TILE, TILE), jnp.float32),
            pltpu.VMEM((2, GROUP, NBR, TILE), jnp.int32),
            pltpu.SMEM((2 * CAND + GROUP,), jnp.int32),
            pltpu.SMEM((2 * CAND + GROUP,), jnp.int32),
            pltpu.SMEM((2 * CAND + GROUP,), jnp.int32),
            pltpu.SMEM((2 * CAND + GROUP,), jnp.int32),
            pltpu.SemaphoreType.DMA((2,)),
            pltpu.SemaphoreType.DMA((2, GROUP)),
        ],
        compiler_params=pltpu.CompilerParams(vmem_limit_bytes=40 << 20),
        name="slot_gradients",
    )(left, right, kind, own, moved, edges)


def route(values):
    rest = values.shape[2:]
    first = values[:, 0].reshape((NZ, NY, NC) + rest)
    first = jnp.moveaxis(first, 1, 0).reshape((NY * ROWSET,) + rest)
    first = lax.all_to_all(first, "y", 0, 0, tiled=True)
    second = values[:, 1].reshape((NZ, NY, NC) + rest)
    second = jnp.moveaxis(second, 2, 1).reshape((ROWSET * NY,) + rest)
    second = lax.all_to_all(second, ("z", "core"), 0, 0, tiled=True)
    both = jnp.stack([first, second])
    return lax.all_gather(both, "x", axis=1, tiled=False)


def body(latent, left_block, right_block, slot_kind, edge_cols):
    x = lax.axis_index("x")
    blocks = latent.reshape(BLOCKS, TILE, TILE)
    own = lax.all_gather(blocks, "y", axis=0, tiled=True)
    quarter = lax.dynamic_slice_in_dim(blocks, x * QUARTER, QUARTER, 0)
    moved = lax.all_gather(quarter, ("z", "core"), axis=0, tiled=True)
    edges = route(edge_cols[0, 0]).reshape(2 * CAND, NBR, TILE)
    meta = jnp.stack([left_block[0, 0], right_block[0, 0], slot_kind[0, 0]], axis=-1)
    meta = route(meta).reshape(2 * CAND, 3)
    og, mg = compute(meta[:, 0], meta[:, 1], meta[:, 2], own, moved, edges)
    og = lax.psum_scatter(og, ("y", "x"), scatter_dimension=0, tiled=True)
    mg = lax.psum_scatter(mg, ("z", "core"), scatter_dimension=0, tiled=True)
    return (og + mg).reshape(QUARTER * TILE, TILE)


def solution(mesh):
    fine = Mesh(mesh.devices.reshape(NZ, NY, NC, NX), ("z", "y", "core", "x"))
    rows = ("z", "y", "core")
    return jax.shard_map(
        body,
        mesh=fine,
        in_specs=(
            P(rows, None),
            P(rows, "x", None, None),
            P(rows, "x", None, None),
            P(rows, "x", None, None),
            P(rows, "x", None, None, None, None),
        ),
        out_specs=P(("z", "y", "core", "x"), None),
        check_vma=False,
    )
```

```python
import functools

import jax
import jax.numpy as jnp
from jax import lax
from jax.experimental import pallas as pl
from jax.experimental.pallas import tpu as pltpu
from jax.sharding import Mesh
from jax.sharding import PartitionSpec as P

NZ, NY, NC, NX = 8, 4, 2, 4
BLOCKS = 16
QUARTER = 4
TILE = 128
NBR = 8
OWN = NY * BLOCKS
MOVED = NZ * NC * QUARTER
ALL = OWN + MOVED
PLANES = NZ + 1
CAND = PLANES * NY * NC
META = NY + NZ * NC
GROUP = 2
MESH = pl.DeviceIdType.MESH

NT = (((1,), (1,)), ((), ()))
NN = (((1,), (0,)), ((), ()))


def position():
    return tuple(lax.axis_index(name) for name in ("z", "y", "core", "x"))


def step_of(value, by, size):
    return lax.rem(value + (by + size), size)


class Copies:
    def __init__(self, send_sems, recv_sems):
        self.send_sems, self.recv_sems = send_sems, recv_sems
        self.index = {}
        self.sent = []

    def sems(self, name):
        at = self.index.setdefault(name, len(self.index))
        return self.send_sems.at[at], self.recv_sems.at[at]

    def make(self, name, src, dst, device):
        send, recv = self.sems(name)
        return pltpu.make_async_remote_copy(
            src_ref=src, dst_ref=dst, send_sem=send, recv_sem=recv,
            device_id=device, device_id_type=MESH,
        )

    def start(self, name, src, dst, device, when=None):
        copy = self.make(name, src, dst, device)
        self.sent.append((copy, when))
        if when is None:
            copy.start()
        else:
            pl.when(when)(copy.start)

    def arrived(self, name, landed, device, when=None):
        copy = self.make(name, landed, landed, device)
        if when is None:
            copy.wait_recv()
        else:
            pl.when(when)(copy.wait_recv)

    def drain(self):
        for copy, when in self.sent:
            if when is None:
                copy.wait_send()
            else:
                pl.when(when)(copy.wait_send)


GATHER_SEMS = 128


def gather_kernel(lat, edges, first_meta, second_meta, own, moved, edge, meta,
                  send_sems, recv_sems, local_sems):
    z, y, c, x = position()
    other = 1 - c
    ys = [step_of(y, d, NY) for d in range(NY)]
    yd = {1: ys[1], -1: ys[3], 2: ys[2]}
    xd = {1: step_of(x, 1, NX), -1: step_of(x, -1, NX)}
    zd = {d: step_of(z, d, NZ) for d in range(-4, NZ)}
    cp = Copies(send_sems, recv_sems)
    cs = [c, other]

    barrier = pltpu.get_barrier_semaphore()
    peers = [{"y": ys[d]} for d in (1, 2, 3)] + [{"x": xd[1]}, {"x": xd[-1]}]
    peers += [{"z": zd[dz], "core": cs[dc]} for dz in range(NZ) for dc in range(NC) if dz or dc]
    for peer in peers:
        pl.semaphore_signal(barrier, inc=1, device_id=peer, device_id_type=MESH)

    local = []

    def here(src, dst, when=None):
        copy = pltpu.make_async_copy(src, dst, local_sems.at[len(local)])
        local.append((copy, when))
        if when is None:
            copy.start()
        else:
            pl.when(when)(copy.start)

    for zp in range(NZ):
        here(edges.at[zp, y, :, 0], edge.at[x, zp, y], zp >= z)
    here(edges.at[z, :, c, 1], edge.at[x, NZ, :, c])
    here(first_meta.at[y], meta.at[x, y])
    here(second_meta.at[z, c], meta.at[x, NY + z * NC + c])

    pl.semaphore_wait(barrier, len(peers))

    for d in (1, 2, 3):
        for zp in range(NZ):
            cp.start(("e0", d, zp), edges.at[zp, ys[d], :, 0], edge.at[x, zp, y], {"y": ys[d]}, zp >= z)
        cp.start(("m0", d), first_meta.at[ys[d]], meta.at[x, y], {"y": ys[d]})
    for dz in range(NZ):
        for dc in range(NC):
            if dz or dc:
                zs, cc = zd[dz], cs[dc]
                plane = NZ if dz == 0 else z
                cp.start(("e1", dz, dc), edges.at[zs, :, cc, 1], edge.at[x, plane, :, c],
                         {"z": zs, "core": cc}, zs >= z)
                cp.start(("m1", dz, dc), second_meta.at[zs, cc], meta.at[x, NY + z * NC + c],
                         {"z": zs, "core": cc})

    pieces = {0: pl.ds(8, 4), 1: pl.ds(12, 4)}

    def zsend(sign, step, sub):
        origin = zd[-(step - 1)] if sign > 0 else zd[step - 1]
        if step == 1:
            src = lat.at[pl.ds(x * QUARTER + 2 * sub, 2)]
        else:
            src = moved.at[origin, c, pl.ds(2 * sub, 2)]
        cp.start(("z", sign, step, sub), src, moved.at[origin, c, pl.ds(2 * sub, 2)], {"z": zd[sign]})

    def zgot(sign, step, sub):
        origin = zd[-step] if sign > 0 else zd[step]
        cp.arrived(("z", sign, step, sub), moved.at[origin, c, pl.ds(2 * sub, 2)], {"z": zd[-sign]})

    def to_core(key, origin, src):
        cp.start(("core", key), src, moved.at[origin, c], {"core": other})

    for s in (1, -1):
        cp.start(("yx", s), lat.at[pl.ds(2 * x, 2)], own.at[y, pl.ds(2 * x, 2)], {"y": yd[s]})
    for sub in (0, 1):
        for s in (1, -1):
            zsend(s, 1, sub if s > 0 else 1 - sub)
    for half in (0, 1):
        for s in (1, -1):
            h = half if s > 0 else 1 - half
            cp.start(("yd", s, h), lat.at[pieces[h]], own.at[y, pieces[h]], {"y": yd[s]})
    to_core(0, z, lat.at[pl.ds(x * QUARTER, QUARTER)])

    for d in (1, 2, 3):
        src = ys[NY - d]
        for zp in range(NZ):
            cp.arrived(("e0", d, zp), edge.at[x, zp, src], {"y": src}, zp >= z)
        cp.arrived(("m0", d), meta.at[x, src], {"y": src})
    for dz in range(NZ):
        for dc in range(NC):
            if dz or dc:
                zr, cr = zd[(NZ - dz) % NZ], cs[dc]
                plane = NZ if dz == 0 else zr
                cp.arrived(("e1", dz, dc), edge.at[x, plane, :, cr], {"z": zr, "core": cr}, zr <= z)
                cp.arrived(("m1", dz, dc), meta.at[x, NY + zr * NC + cr], {"z": zr, "core": cr})
    for copy, when in local:
        if when is None:
            copy.wait()
        else:
            pl.when(when)(copy.wait)
    parts = {0: pl.ds(0, 5), 1: pl.ds(5, 4)}
    for s in (1, -1):
        cp.start(("xm", s), meta.at[x], meta.at[x], {"x": xd[s]})
    for half in (0, 1):
        for s in (1, -1):
            h = half if s > 0 else 1 - half
            cp.start(("xe", s, h), edge.at[x, parts[h]], edge.at[x, parts[h]], {"x": xd[s]})

    def xsend(key, row):
        for half in (0, 1):
            for s in (1, -1):
                at = 2 * x + (half if s > 0 else 1 - half)
                cp.start(("xo", key, s, half), own.at[row, pl.ds(at, 1)], own.at[row, pl.ds(at, 1)], {"x": xd[s]})

    def xgot(key, row, half, relay):
        for s in (1, -1):
            origin = xd[-s]
            at = 2 * origin + (half if s > 0 else 1 - half)
            cp.arrived(("xo", key, s, half), own.at[row, pl.ds(at, 1)], {"x": origin})
            if relay:
                cp.start(("xr", key, s), own.at[row, pl.ds(at, 1)], own.at[row, pl.ds(at, 1)], {"x": xd[s]})

    for s in (1, -1):
        row = yd[-s]
        cp.arrived(("yx", s), own.at[row, pl.ds(2 * x, 2)], {"y": row})
        at = 2 * x + (0 if s > 0 else 1)
        cp.start(("yxr", s), own.at[row, pl.ds(at, 1)], own.at[row, pl.ds(at, 1)], {"y": yd[s]})
    xsend(1, yd[1])
    xsend(-1, yd[-1])

    def zround(step):
        for k in (0, 1):
            for s in (1, -1):
                sub = k if s > 0 else 1 - k
                if step == 4 and k == 1:
                    continue
                zgot(s, step, sub)
                if step < 3 or (step == 3 and k == 0):
                    zsend(s, step + 1, sub)
        for s in (1, -1):
            origin = zd[-s * step] if step < 4 else zd[4]
            if step < 4:
                to_core((s, step), origin, moved.at[origin, c])
            elif s == 1:
                to_core((s, step), origin, moved.at[origin, c])

    zround(1)
    for s in (1, -1):
        h = 0 if s > 0 else 1
        row = yd[-s]
        cp.arrived(("yd", s, h), own.at[row, pieces[h]], {"y": row})
        cp.start(("ydr", s), own.at[row, pieces[h]], own.at[row, pieces[h]], {"y": yd[s]})
    for s in (1, -1):
        at = 2 * x + (0 if s > 0 else 1)
        cp.arrived(("yxr", s), own.at[yd[2], pl.ds(at, 1)], {"y": yd[-s]})
    xsend(2, yd[2])
    for s in (1, -1):
        h = 0 if s > 0 else 1
        src = xd[-s]
        cp.arrived(("xm", s), meta.at[src], {"x": src})
        if s > 0:
            cp.start(("xmr", s), meta.at[src], meta.at[src], {"x": xd[s]})
        cp.arrived(("xe", s, h), edge.at[src, parts[h]], {"x": src})
        cp.start(("xer", s), edge.at[src, parts[h]], edge.at[src, parts[h]], {"x": xd[s]})
    zround(2)
    for key in (1, -1):
        xgot(key, yd[key], 0, True)
    zround(3)
    xgot(2, yd[2], 0, True)
    zround(4)

    across = step_of(x, 2, NX)
    for s in (1, -1):
        h = 1 if s > 0 else 0
        row = yd[-s]
        cp.arrived(("yd", s, h), own.at[row, pieces[h]], {"y": row})
        cp.arrived(("ydr", s), own.at[yd[2], pieces[1 - h]], {"y": yd[-s]})
        src = xd[-s]
        cp.arrived(("xe", s, h), edge.at[src, parts[h]], {"x": src})
        cp.arrived(("xer", s), edge.at[across, parts[1 - h]], {"x": src})
        if s > 0:
            cp.arrived(("xmr", s), meta.at[across], {"x": src})
    for key in (1, -1, 2):
        xgot(key, yd[key], 1, False)
        for s in (1, -1):
            at = 2 * across + (0 if s > 0 else 1)
            cp.arrived(("xr", key, s), own.at[yd[key], pl.ds(at, 1)], {"x": xd[-s]})
    cp.arrived(("core", 0), moved.at[z, other], {"core": other})
    for step in (1, 2, 3):
        for s in (1, -1):
            cp.arrived(("core", (s, step)), moved.at[zd[-s * step], other], {"core": other})
    cp.arrived(("core", (1, 4)), moved.at[zd[4], other], {"core": other})
    cp.drain()


def gather(lat, edges, first_meta, second_meta):
    hbm = pl.BlockSpec(memory_space=pl.ANY)
    return pl.pallas_call(
        gather_kernel,
        out_shape=(
            jax.ShapeDtypeStruct((NY, BLOCKS, TILE, TILE), jnp.float32),
            jax.ShapeDtypeStruct((NZ, NC, QUARTER, TILE, TILE), jnp.float32),
            jax.ShapeDtypeStruct((NX, PLANES, NY, NC, NBR, TILE), jnp.int32),
            jax.ShapeDtypeStruct((NX, META, 1, TILE), jnp.int32),
        ),
        in_specs=[hbm] * 4,
        out_specs=(hbm,) * 4,
        scratch_shapes=[
            pltpu.SemaphoreType.DMA((GATHER_SEMS,)),
            pltpu.SemaphoreType.DMA((GATHER_SEMS,)),
            pltpu.SemaphoreType.DMA((12,)),
        ],
        compiler_params=pltpu.CompilerParams(collective_id=0, has_side_effects=True),
        name="gather_rows",
    )(lat, edges, first_meta, second_meta)


def mm(a, b, dims):
    return lax.dot_general(a, b, dims, preferred_element_type=jnp.float32)


def halves(a):
    high = a.astype(jnp.bfloat16)
    low = (a - high.astype(jnp.float32)).astype(jnp.bfloat16)
    return high, low


def pair_step(left, right, edges, hit_scale):
    lh, ll = halves(left)
    rh, rl = halves(right)
    scores = mm(
        jnp.concatenate([rh, rl], axis=1), jnp.concatenate([lh, lh], axis=1), NT
    ) + mm(rh, ll, NT)
    rows = lax.broadcasted_iota(jnp.int32, (TILE, TILE), 0)
    hit = rows == edges[0:1, :]
    for k in range(1, NBR):
        hit = hit | (rows == edges[k : k + 1, :])
    res = (1.0 / (1.0 + jnp.exp(-scores)) - jnp.where(hit, 1.0, 0.0)) * hit_scale
    rest = res.T
    th, tl = halves(res)
    uh, ul = halves(rest)
    grad_right = mm(
        jnp.concatenate([th, tl], axis=1), jnp.concatenate([lh, lh], axis=0), NN
    ) + mm(th, ll, NN)
    grad_left = mm(
        jnp.concatenate([uh, ul], axis=1), jnp.concatenate([rh, rh], axis=0), NN
    ) + mm(uh, rl, NN)
    return grad_left, grad_right


def compute_kernel(meta_ref, lat_ref, own_ref, moved_ref, edge_ref, og_ref, mg_ref,
                   blk, grad, ebuf, list_l, list_r, list_e, list_k, sem):
    z, y, c, x = position()
    ins = [pltpu.make_async_copy(edge_ref, ebuf, sem.at[0]),
           pltpu.make_async_copy(lat_ref, blk.at[pl.ds(y * BLOCKS, BLOCKS)], sem.at[1]),
           pltpu.make_async_copy(
               lat_ref.at[pl.ds(x * QUARTER, QUARTER)],
               blk.at[pl.ds(OWN + (z * NC + c) * QUARTER, QUARTER)], sem.at[2])]
    for d in range(1, NY):
        row = step_of(y, d, NY)
        ins.append(pltpu.make_async_copy(
            own_ref.at[row], blk.at[pl.ds(row * BLOCKS, BLOCKS)], sem.at[2 + d]))
    for d in range(1, NZ * NC):
        row = step_of(z * NC + c, d, NZ * NC)
        ins.append(pltpu.make_async_copy(
            moved_ref.at[row], blk.at[pl.ds(OWN + row * QUARTER, QUARTER)], sem.at[5 + d]))
    for copy in ins:
        copy.start()

    low = x * QUARTER
    me = y * NC

    def scan(j, count):
        q, plane = j // PLANES, lax.rem(j, PLANES)
        last = plane == NZ
        first = (plane >= z) & (plane < NZ)
        same = (plane == z) | last
        at = jnp.where(last, z, plane)
        base = q * META * TILE
        for yo in range(NY):
            for cc in range(NC):
                zc = at * NC + cc
                where = base + jnp.where(first, yo * TILE + zc, (NY + zc) * TILE + yo)
                stride = jnp.where(first, NZ * NC, NY)
                lb, rb, kind = meta_ref[where], meta_ref[where + stride], meta_ref[where + 2 * stride]
                own_block = jnp.where(first, lb, rb)
                here = jnp.where(first, rb, lb) - low
                own_at = yo * BLOCKS + own_block
                moved_at = OWN + zc * QUARTER + here
                list_l[count] = jnp.where(first, own_at, moved_at)
                list_r[count] = jnp.where(first, moved_at, own_at)
                list_e[count] = j * (NY * NC) + yo * NC + cc
                list_k[count] = kind
                order = (me + cc) - (yo * NC + c)
                order = jnp.where(last, -order, order)
                live = jnp.logical_not(same) | (order >= 0)
                take = live & (here >= 0) & (here < QUARTER)
                count = count + jnp.where(take, 1, 0)
        return count

    count = lax.fori_loop(0, NX * PLANES, scan, 0)
    for k in range(GROUP):
        list_l[count + k] = ALL
        list_r[count + k] = ALL
        list_e[count + k] = 0
        list_k[count + k] = 0

    def clear(i, carry):
        grad[i] = jnp.zeros((TILE, TILE), jnp.float32)
        return carry

    lax.fori_loop(0, ALL + 1, clear, 0)
    blk[ALL] = jnp.zeros((TILE, TILE), jnp.float32)
    steps = (count + GROUP - 1) // GROUP
    for copy in ins:
        copy.wait()

    def work(step, carry):
        results = []
        for k in range(GROUP):
            at = step * GROUP + k
            li, ri, kind = list_l[at], list_r[at], list_k[at]
            edges = jnp.where(kind == 2, ebuf[list_e[at]], -1)
            scale = jnp.where(kind > 0, 1.0, 0.0)
            results.append((li, ri) + pair_step(blk[li], blk[ri], edges, scale))
        for li, ri, gl, gr in results:
            grad[li] += gl
            grad[ri] += gr
        return carry

    lax.fori_loop(0, steps, work, 0)
    outs = [pltpu.make_async_copy(grad.at[pl.ds(0, OWN)], og_ref, sem.at[0]),
            pltpu.make_async_copy(grad.at[pl.ds(OWN, MOVED)], mg_ref, sem.at[1])]
    for copy in outs:
        copy.start()
    for copy in outs:
        copy.wait()


def compute(meta, lat, own, moved, edges):
    smem = pl.BlockSpec(memory_space=pltpu.SMEM)
    hbm = pl.BlockSpec(memory_space=pl.ANY)
    slots = NX * CAND + GROUP
    return pl.pallas_call(
        compute_kernel,
        out_shape=(
            jax.ShapeDtypeStruct((OWN, TILE, TILE), jnp.float32),
            jax.ShapeDtypeStruct((MOVED, TILE, TILE), jnp.float32),
        ),
        in_specs=[smem, hbm, hbm, hbm, hbm],
        out_specs=(hbm, hbm),
        scratch_shapes=[
            pltpu.VMEM((ALL + 1, TILE, TILE), jnp.float32),
            pltpu.VMEM((ALL + 1, TILE, TILE), jnp.float32),
            pltpu.VMEM((NX * CAND, NBR, TILE), jnp.int32),
            pltpu.SMEM((slots,), jnp.int32),
            pltpu.SMEM((slots,), jnp.int32),
            pltpu.SMEM((slots,), jnp.int32),
            pltpu.SMEM((slots,), jnp.int32),
            pltpu.SemaphoreType.DMA((24,)),
        ],
        compiler_params=pltpu.CompilerParams(vmem_limit_bytes=40 << 20),
        name="slot_gradients",
    )(meta.reshape(NX * META * TILE), lat, own,
      moved.reshape(NZ * NC, QUARTER, TILE, TILE), edges.reshape(NX * CAND, NBR, TILE))


class Ring:
    def __init__(self, cp, name, axis, at, part, far, near, made):
        self.cp, self.name, self.axis, self.part = cp, name, axis, part
        self.far, self.near, self.made = far, near, made
        self.at = {d: step_of(at, d, 4) for d in (-1, 0, 1, 2)}

    def to(self, sign):
        return {self.axis: self.at[sign]}

    def begin(self):
        for k, s in enumerate((1, -1)):
            self.cp.start((self.name, "far", s), self.part(self.at[2], k), self.far.at[k], self.to(s))
        for k, s in enumerate((1, -1)):
            h = 1 - k
            self.cp.start((self.name, "near", s, h), self.part(self.at[s], h), self.near.at[k, h], self.to(s))

    def pass_on(self):
        for k, s in enumerate((1, -1)):
            self.cp.arrived((self.name, "far", s), self.far.at[k], self.to(-s))
            self.made[k] = self.part(self.at[s], k)[...] + self.far[k]
            self.cp.start((self.name, "near", s, k), self.made.at[k], self.near.at[k, k], self.to(s))

    def total(self, half):
        for k, s in enumerate((1, -1)):
            self.cp.arrived((self.name, "near", s, half), self.near.at[k, half], self.to(-s))
        return self.part(self.at[0], half)[...] + self.near[0, half] + self.near[1, half]


REDUCE_SEMS = 64


def reduce_kernel(og, mg, out, a_far, a_near, a_made, a_sum, b_far, b_near, b_made, b_sum,
                  c_far, c_near, c_made, d_far, d_near, d_made,
                  partner, z_in, z_out, send_sems, recv_sems):
    z, y, c, x = position()
    other = 1 - c
    zd = {d: step_of(z, d, NZ) for d in range(-4, 5)}
    cp = Copies(send_sems, recv_sems)

    barrier = pltpu.get_barrier_semaphore()
    peers = [{"y": step_of(y, 1, NY)}, {"y": step_of(y, -1, NY)}, {"x": step_of(x, 1, NX)},
             {"x": step_of(x, -1, NX)}, {"z": zd[1]}, {"z": zd[-1]}, {"core": other}]
    for peer in peers:
        pl.semaphore_signal(barrier, inc=1, device_id=peer, device_id_type=MESH)
    pl.semaphore_wait(barrier, len(peers))

    a = Ring(cp, "a", "y", y, lambda dest, h: og.at[dest, pl.ds(2 * h, 2), pl.ds(0, 2)], a_far, a_near, a_made)
    b = Ring(cp, "b", "x", x, lambda dest, h: og.at[pl.ds(2 * h, 2), dest, pl.ds(2, 2)], b_far, b_near, b_made)
    order = [4, 3, -3, 2, -2, 1, -1, 0]
    for d in order:
        cp.start(("p", d), mg.at[zd[d], other], partner.at[zd[d]], {"core": other})
    a.begin()
    b.begin()

    slot = {}
    for s in (1, -1):
        for d in (4, 3, 2, 1):
            for sub in (0, 1):
                if d < 4 or sub == (0 if s > 0 else 1):
                    slot[s, d, sub] = len(slot)

    def mine(d, sub):
        return mg[zd[d], c, pl.ds(2 * sub, 2)] + partner[zd[d], pl.ds(2 * sub, 2)]

    def zsend(s, d, sub, received):
        at = slot[s, d, sub]
        value = mine(s * d if d < 4 else 4, sub)
        if received:
            value = value + z_in[slot[s, d + 1, sub]]
        z_out[at] = value
        cp.start(("z", s, d, sub), z_out.at[at], z_in.at[at], {"z": zd[s]})

    def zgot(s, d, sub):
        cp.arrived(("z", s, d, sub), z_in.at[slot[s, d, sub]], {"z": zd[-s]})

    def from_core(d):
        cp.arrived(("p", d), partner.at[zd[d]], {"core": other})

    lead = {1: 0, -1: 1}
    from_core(4)
    for s in (1, -1):
        zsend(s, 4, lead[s], False)
    for s in (1, -1):
        from_core(3 * s)
        zsend(s, 3, 1 - lead[s], False)
    from_core(2)
    from_core(-2)
    for s in (1, -1):
        zgot(s, 4, lead[s])
        zsend(s, 3, lead[s], True)
    a.pass_on()
    b.pass_on()
    for s in (1, -1):
        zgot(s, 3, 1 - lead[s])
        zsend(s, 2, 1 - lead[s], True)
    for s in (1, -1):
        zgot(s, 3, lead[s])
        zsend(s, 2, lead[s], True)
    from_core(1)
    from_core(-1)
    from_core(0)
    for s in (1, -1):
        zgot(s, 2, 1 - lead[s])
        zsend(s, 1, 1 - lead[s], True)
    for h in (1, 0):
        a_sum[pl.ds(2 * h, 2)] = a.total(h)
        b_sum[pl.ds(2 * h, 2)] = b.total(h)
    second_a = Ring(cp, "c", "x", x, lambda dest, h: a_sum.at[dest, pl.ds(h, 1)], c_far, c_near, c_made)
    second_b = Ring(cp, "d", "y", y, lambda dest, h: b_sum.at[dest, pl.ds(h, 1)], d_far, d_near, d_made)
    second_a.begin()
    second_b.begin()
    for s in (1, -1):
        zgot(s, 2, lead[s])
        zsend(s, 1, lead[s], True)
    second_a.pass_on()
    second_b.pass_on()
    for sub in (0, 1):
        zgot(1, 1, sub)
        zgot(-1, 1, sub)
        value = mine(0, sub) + z_in[slot[1, 1, sub]] + z_in[slot[-1, 1, sub]]
        ring = second_a if sub == 0 else second_b
        for h in (0, 1):
            out[2 * sub + h] = value[h] + ring.total(h)[0]
    cp.drain()


def reduce(og, mg):
    vmem = pl.BlockSpec(memory_space=pltpu.VMEM)
    tile = (TILE, TILE)
    f32 = jnp.float32

    def ring(blocks):
        return [pltpu.VMEM((2,) + blocks + tile, f32), pltpu.VMEM((2, 2) + blocks + tile, f32),
                pltpu.VMEM((2,) + blocks + tile, f32)]

    first, second = (2, 2), (1,)
    return pl.pallas_call(
        reduce_kernel,
        out_shape=jax.ShapeDtypeStruct((QUARTER,) + tile, f32),
        in_specs=[vmem, vmem],
        out_specs=vmem,
        scratch_shapes=ring(first) + [pltpu.VMEM((4, 2) + tile, f32)]
        + ring(first) + [pltpu.VMEM((4, 2) + tile, f32)]
        + ring(second) + ring(second)
        + [
            pltpu.VMEM((NZ, QUARTER) + tile, f32),
            pltpu.VMEM((14, 2) + tile, f32),
            pltpu.VMEM((14, 2) + tile, f32),
            pltpu.SemaphoreType.DMA((REDUCE_SEMS,)),
            pltpu.SemaphoreType.DMA((REDUCE_SEMS,)),
        ],
        compiler_params=pltpu.CompilerParams(
            collective_id=1, has_side_effects=True, vmem_limit_bytes=40 << 20
        ),
        name="reduce_rows",
    )(og.reshape((NY, NX, QUARTER) + tile), mg.reshape((NZ, NC, QUARTER) + tile))


def body(latent, left_block, right_block, slot_kind, edge_cols):
    lat = latent.reshape(BLOCKS, TILE, TILE)
    edges = edge_cols.reshape(NZ, NY, NC, 2, NBR, TILE)
    ids = jnp.stack([left_block, right_block, slot_kind]).reshape(3, NZ, NY, NC, 2)
    first = jnp.transpose(ids[..., 0], (2, 0, 1, 3)).reshape(NY, 1, 3 * NZ * NC)
    second = jnp.transpose(ids[..., 1], (1, 3, 0, 2)).reshape(NZ, NC, 1, 3 * NY)
    first = jnp.pad(first, ((0, 0), (0, 0), (0, TILE - 3 * NZ * NC)))
    second = jnp.pad(second, ((0, 0), (0, 0), (0, 0), (0, TILE - 3 * NY)))
    own, moved, edge, meta = gather(lat, edges, first, second)
    og, mg = compute(meta, lat, own, moved, edge)
    out = reduce(og, mg)
    return out.reshape(QUARTER * TILE, TILE)


def solution(mesh):
    fine = Mesh(mesh.devices.reshape(NZ, NY, NC, NX), ("z", "y", "core", "x"))
    rows = ("z", "y", "core")
    return jax.shard_map(
        body,
        mesh=fine,
        in_specs=(
            P(rows, None),
            P(rows, "x", None, None),
            P(rows, "x", None, None),
            P(rows, "x", None, None),
            P(rows, "x", None, None, None, None),
        ),
        out_specs=P(("z", "y", "core", "x"), None),
        check_vma=False,
    )
```

```python
import functools

import jax
import jax.numpy as jnp
from jax import lax
from jax.experimental import pallas as pl
from jax.experimental.pallas import tpu as pltpu
from jax.sharding import Mesh
from jax.sharding import PartitionSpec as P

NZ, NY, NC, NX = 8, 4, 2, 4
BLOCKS = 16
QUARTER = 4
TILE = 128
NBR = 8
OWN = NY * BLOCKS
MOVED = NZ * NC * QUARTER
ALL = OWN + MOVED
PLANES = NZ + 1
CAND = PLANES * NY * NC
META = NY + NZ * NC
PARTS = ALL // 16
TRASH = ALL
GROUP = 2
MESH = pl.DeviceIdType.MESH
GATHER_VMEM, SLOT_VMEM, REDUCE_VMEM = 54 << 20, 24 << 20, 28 << 20

NT = (((1,), (1,)), ((), ()))
NN = (((1,), (0,)), ((), ()))


def position():
    return tuple(lax.axis_index(name) for name in ("z", "y", "core", "x"))


def step_of(value, by, size):
    return lax.rem(value + (by + size), size)


class Copies:
    def __init__(self, send_sems, recv_sems):
        self.send_sems, self.recv_sems = send_sems, recv_sems
        self.index = {}
        self.sent = []

    def sems(self, name):
        at = self.index.setdefault(name, len(self.index))
        return self.send_sems.at[at], self.recv_sems.at[at]

    def make(self, name, src, dst, device):
        send, recv = self.sems(name)
        return pltpu.make_async_remote_copy(
            src_ref=src, dst_ref=dst, send_sem=send, recv_sem=recv,
            device_id=device, device_id_type=MESH,
        )

    def start(self, name, src, dst, device, when=None):
        copy = self.make(name, src, dst, device)
        self.sent.append((copy, when))
        if when is None:
            copy.start()
        else:
            pl.when(when)(copy.start)

    def arrived(self, name, landed, device, when=None):
        copy = self.make(name, landed, landed, device)
        if when is None:
            copy.wait_recv()
        else:
            pl.when(when)(copy.wait_recv)

    def drain(self):
        for copy, when in self.sent:
            if when is None:
                copy.wait_send()
            else:
                pl.when(when)(copy.wait_send)


GATHER_SEMS = 128
IDS = 2


def gather_kernel(lat, edges, ids, high, low, edge, meta, land,
                  send_sems, recv_sems, local_sems):
    z, y, c, x = position()
    other = 1 - c
    ys = [step_of(y, d, NY) for d in range(NY)]
    yd = {1: ys[1], -1: ys[3], 2: ys[2]}
    xd = {1: step_of(x, 1, NX), -1: step_of(x, -1, NX), 2: step_of(x, 2, NX)}
    zd = {d: step_of(z, d, NZ) for d in range(-4, NZ)}
    cp = Copies(send_sems, recv_sems)
    cs = [c, other]

    barrier = pltpu.get_barrier_semaphore()
    peers = [{"y": ys[d]} for d in (1, 2, 3)] + [{"x": xd[1]}, {"x": xd[-1]}]
    peers += [{"z": zd[dz], "core": cs[dc]} for dz in range(NZ) for dc in range(NC) if dz or dc]
    for peer in peers:
        pl.semaphore_signal(barrier, inc=1, device_id=peer, device_id_type=MESH)

    local = []

    def here(src, dst, when=None):
        copy = pltpu.make_async_copy(src, dst, local_sems.at[len(local)])
        local.append((copy, when))
        if when is None:
            copy.start()
        else:
            pl.when(when)(copy.start)

    def moved_at(zz, cc):
        return PARTS // 2 + zz // 2, lax.rem(zz, 2) * NC + cc

    for zp in range(NZ):
        here(edges.at[zp, y, :, 0], edge.at[x, zp, y], zp >= z)
    here(edges.at[z, :, c, 1], edge.at[x, NZ, :, c])
    here(ids.at[0], meta.at[x, y])
    here(ids.at[1], meta.at[x, NY + z * NC + c])
    edge_local = len(local)
    here(lat, land.at[y])
    here(lat.at[x], land.at[moved_at(z, c)])

    pl.semaphore_wait(barrier, len(peers))

    def quarter_of(row, at, count):
        return land.at[row, at // 4, pl.ds(lax.rem(at, 4), count)]

    def moved_sub(zz, cc, sub):
        p, s = moved_at(zz, cc)
        return land.at[p, s, pl.ds(2 * sub, 2)]

    def zsend(sign, step, sub):
        origin = zd[-(step - 1)] if sign > 0 else zd[step - 1]
        dst = moved_sub(origin, c, sub)
        src = lat.at[x, pl.ds(2 * sub, 2)] if step == 1 else dst
        cp.start(("z", sign, step, sub), src, dst, {"z": zd[sign]})

    def zgot(sign, step, sub):
        origin = zd[-step] if sign > 0 else zd[step]
        cp.arrived(("z", sign, step, sub), moved_sub(origin, c, sub), {"z": zd[-sign]})

    def to_core(key, origin, src):
        cp.start(("core", key), src, land.at[moved_at(origin, c)], {"core": other})

    def split(part, sub):
        def one(j, carry):
            value = land[part, sub, j]
            top = value.astype(jnp.bfloat16)
            high[part * 16 + sub * 4 + j] = top
            low[part * 16 + sub * 4 + j] = (value - top.astype(jnp.float32)).astype(jnp.bfloat16)
            return carry

        lax.fori_loop(0, 4, one, 0)

    lead = {1: 0, -1: 1}

    for s in (1, -1):
        at = 2 * x
        cp.start(("yx", s), lat.at[at // 4, pl.ds(lax.rem(at, 4), 2)], quarter_of(y, at, 2), {"y": yd[s]})
    for s in (1, -1):
        zsend(s, 1, lead[s])
    for d in (1, 2, 3):
        for zp in range(NZ):
            cp.start(("e0", d, zp), edges.at[zp, ys[d], :, 0], edge.at[x, zp, y], {"y": ys[d]}, zp >= z)
        cp.start(("m0", d), ids.at[0], meta.at[x, y], {"y": ys[d]})
    for dz in range(NZ):
        for dc in range(NC):
            if dz or dc:
                zs, cc = zd[dz], cs[dc]
                plane = NZ if dz == 0 else z
                cp.start(("e1", dz, dc), edges.at[zs, :, cc, 1], edge.at[x, plane, :, c],
                         {"z": zs, "core": cc}, zs >= z)
                cp.start(("m1", dz, dc), ids.at[1], meta.at[x, NY + z * NC + c],
                         {"z": zs, "core": cc})
    for s in (1, -1):
        h = lead[s]
        cp.start(("yd", s, h), lat.at[2 + h], land.at[y, 2 + h], {"y": yd[s]})
    for s in (1, -1):
        zsend(s, 1, 1 - lead[s])
    to_core(0, z, lat.at[x])

    def xsend(key, row, half):
        for s in (1, -1):
            at = 2 * x + (half if s > 0 else 1 - half)
            ref = quarter_of(row, at, 1)
            cp.start(("xo", key, s, half), ref, ref, {"x": xd[s]})

    def xgot(key, row, half, relay):
        for s in (1, -1):
            origin = xd[-s]
            ref = quarter_of(row, 2 * origin + (half if s > 0 else 1 - half), 1)
            cp.arrived(("xo", key, s, half), ref, {"x": origin})
            if relay:
                cp.start(("xr", key, s), ref, ref, {"x": xd[s]})

    def zstep(step, k):
        for s in (1, -1):
            sub = lead[s] if k == 0 else 1 - lead[s]
            zgot(s, step, sub)
            if step < 3 or (step == 3 and k == 0):
                zsend(s, step + 1, sub)

    def zdone(step):
        for s in (1, -1):
            if step < 4 or s == 1:
                origin = zd[-s * step] if step < 4 else zd[4]
                to_core((s, step), origin, land.at[moved_at(origin, c)])

    for s in (1, -1):
        row = yd[-s]
        cp.arrived(("yx", s), quarter_of(row, 2 * x, 2), {"y": row})
        ref = quarter_of(row, 2 * x + lead[s], 1)
        cp.start(("yxr", s), ref, ref, {"y": yd[s]})
    for s in (1, -1):
        h = 1 - lead[s]
        cp.start(("yd", s, h), lat.at[2 + h], land.at[y, 2 + h], {"y": yd[s]})
    xsend(1, yd[1], 0)
    xsend(-1, yd[-1], 0)
    zstep(1, 0)

    for copy, when in local[:edge_local]:
        if when is None:
            copy.wait()
        else:
            pl.when(when)(copy.wait)
    for d in (1, 2, 3):
        src = ys[NY - d]
        for zp in range(NZ):
            cp.arrived(("e0", d, zp), edge.at[x, zp, src], {"y": src}, zp >= z)
        cp.arrived(("m0", d), meta.at[x, src], {"y": src})
    for dz in range(NZ):
        for dc in range(NC):
            if dz or dc:
                zr, cr = zd[(NZ - dz) % NZ], cs[dc]
                plane = NZ if dz == 0 else zr
                cp.arrived(("e1", dz, dc), edge.at[x, plane, :, cr], {"z": zr, "core": cr}, zr <= z)
                cp.arrived(("m1", dz, dc), meta.at[x, NY + zr * NC + cr], {"z": zr, "core": cr})
    pieces = {0: pl.ds(0, 5), 1: pl.ds(5, 4)}
    for s in (1, -1):
        cp.start(("xm", s), meta.at[x], meta.at[x], {"x": xd[s]})
    for s in (1, -1):
        h = lead[s]
        cp.start(("xe", s, h), edge.at[x, pieces[h]], edge.at[x, pieces[h]], {"x": xd[s]})

    zstep(1, 1)
    zdone(1)
    for s in (1, -1):
        h, row = lead[s], yd[-s]
        cp.arrived(("yd", s, h), land.at[row, 2 + h], {"y": row})
        cp.start(("ydr", s), land.at[row, 2 + h], land.at[row, 2 + h], {"y": yd[s]})
    zstep(2, 0)
    for s in (1, -1):
        ref = quarter_of(yd[2], 2 * x + lead[s], 1)
        cp.arrived(("yxr", s), ref, {"y": yd[-s]})
    xsend(2, yd[2], 0)
    for key in (1, -1):
        xgot(key, yd[key], 0, True)
    for copy, when in local[edge_local:]:
        copy.wait()
    zstep(2, 1)
    zdone(2)
    for s in (1, -1):
        h = 1 - lead[s]
        cp.start(("xe", s, h), edge.at[x, pieces[h]], edge.at[x, pieces[h]], {"x": xd[s]})
    for key in (1, -1, 2):
        xsend(key, yd[key], 1)
    for sub in range(4):
        split(y, sub)
    split(*moved_at(z, c))
    zstep(3, 0)
    for s in (1, -1):
        h, src = lead[s], xd[-s]
        cp.arrived(("xm", s), meta.at[src], {"x": src})
        if s > 0:
            cp.start(("xmr", s), meta.at[src], meta.at[src], {"x": xd[s]})
        cp.arrived(("xe", s, h), edge.at[src, pieces[h]], {"x": src})
        cp.start(("xer", s), edge.at[src, pieces[h]], edge.at[src, pieces[h]], {"x": xd[s]})
    xgot(2, yd[2], 0, True)
    zstep(3, 1)
    zdone(3)
    cp.arrived(("core", 0), land.at[moved_at(z, other)], {"core": other})
    split(*moved_at(z, other))
    for step in (1, 2):
        for s in (1, -1):
            origin = zd[-s * step]
            cp.arrived(("core", (s, step)), land.at[moved_at(origin, other)], {"core": other})
            split(*moved_at(origin, other))
            split(*moved_at(origin, c))
    for s in (1, -1):
        h, row = 1 - lead[s], yd[-s]
        cp.arrived(("yd", s, h), land.at[row, 2 + h], {"y": row})
        for sub in (2, 3):
            split(row, sub)
    zstep(4, 0)
    zdone(4)
    for s in (1, -1):
        origin = zd[-s * 3]
        cp.arrived(("core", (s, 3)), land.at[moved_at(origin, other)], {"core": other})
        split(*moved_at(origin, other))
        split(*moved_at(origin, c))
    split(*moved_at(zd[4], c))
    for s in (1, -1):
        h, src = 1 - lead[s], xd[-s]
        cp.arrived(("ydr", s), land.at[yd[2], 2 + lead[s]], {"y": yd[-s]})
        split(yd[2], 2 + lead[s])
    for key in (1, -1, 2):
        xgot(key, yd[key], 1, False)
        for s in (1, -1):
            ref = quarter_of(yd[key], 2 * xd[2] + lead[s], 1)
            cp.arrived(("xr", key, s), ref, {"x": xd[-s]})
        for sub in (0, 1):
            split(yd[key], sub)
    for s in (1, -1):
        h, src = 1 - lead[s], xd[-s]
        cp.arrived(("xe", s, h), edge.at[src, pieces[h]], {"x": src})
        cp.arrived(("xer", s), edge.at[xd[2], pieces[1 - h]], {"x": src})
        if s > 0:
            cp.arrived(("xmr", s), meta.at[xd[2]], {"x": src})
    cp.arrived(("core", (1, 4)), land.at[moved_at(zd[4], other)], {"core": other})
    split(*moved_at(zd[4], other))
    cp.drain()


def gather(lat, edges, ids):
    hbm = pl.BlockSpec(memory_space=pltpu.HBM)
    vmem = pl.BlockSpec(memory_space=pltpu.VMEM)
    return pl.pallas_call(
        gather_kernel,
        out_shape=(
            jax.ShapeDtypeStruct((ALL + 1, TILE, TILE), jnp.bfloat16),
            jax.ShapeDtypeStruct((ALL + 1, TILE, TILE), jnp.bfloat16),
            jax.ShapeDtypeStruct((NX, PLANES, NY, NC, NBR, TILE), jnp.int32),
            jax.ShapeDtypeStruct((NX, META, IDS, 1, TILE), jnp.int32),
        ),
        in_specs=[hbm] * 3,
        out_specs=(vmem,) * 4,
        scratch_shapes=[
            pltpu.VMEM((PARTS, 4, 4, TILE, TILE), jnp.float32),
            pltpu.SemaphoreType.DMA((GATHER_SEMS,)),
            pltpu.SemaphoreType.DMA((GATHER_SEMS,)),
            pltpu.SemaphoreType.DMA((16,)),
        ],
        compiler_params=pltpu.CompilerParams(
            collective_id=0, has_side_effects=True, vmem_limit_bytes=GATHER_VMEM
        ),
        name="gather_rows",
    )(lat.reshape(4, 4, TILE, TILE), edges, ids)


def mm(a, b, dims):
    return lax.dot_general(a, b, dims, preferred_element_type=jnp.float32)


def three(a, b, axis):
    return jnp.concatenate([a, b, a], axis=axis)


def three_other(a, b, axis):
    return jnp.concatenate([a, a, b], axis=axis)


def residue(left, right, edges, positive):
    scores = mm(three(right[0], right[1], 1), three_other(left[0], left[1], 1), NT)
    bit = jnp.where(positive, lax.shift_left(jnp.ones_like(edges), edges & 31), 0)
    word = edges >> 5
    rows = lax.broadcasted_iota(jnp.int32, (NBR, TILE), 0)
    words, tests = [], []
    for w in range(4):
        have = jnp.where(word == w, bit, 0)
        for shift in (4, 2, 1):
            have = have | pltpu.roll(have, shift, 0)
        words += [have] * 4
        tests.append(lax.shift_left(jnp.ones_like(edges), rows + 8 * w))
    hit = (jnp.concatenate(words, axis=0) & jnp.concatenate(tests * 4, axis=0)) != 0
    value = 1.0 / (1.0 + jnp.exp(-scores)) - jnp.where(hit, 1.0, 0.0)
    top = value.astype(jnp.bfloat16)
    return top, (value - top.astype(jnp.float32)).astype(jnp.bfloat16)


def compute_kernel(meta_ref, high, low, edge, grad, slots, held):
    z, y, c, x = position()
    span = IDS * TILE
    half = TILE // 2

    def entry(own_block, moved_block, yo, zc, flip, kind, where):
        own_at = yo * BLOCKS + own_block
        moved_at = OWN + zc * QUARTER + (moved_block - x * QUARTER)
        left, right = (moved_at, own_at) if flip else (own_at, moved_at)
        both = left + right * 256 + where * 65536
        return both + jnp.where(kind == 2, 1 << 28, 0)

    def put(value, take, count):
        slots[count] = value
        return count + jnp.where(take, 1, 0)

    def clear(at):
        grad[at // 4, lax.rem(at, 4)] = jnp.zeros((4, TILE, TILE), jnp.float32)

    def first(q, count):
        def plane(zz, count):
            clear(q * PLANES + zz)
            for yo in range(NY):
                for cc in range(NC):
                    at = (q * META + yo) * span + zz * (NY * NC) + y * NC + cc
                    lb, rb, kind = meta_ref[at], meta_ref[at + half], meta_ref[at + TILE]
                    live = zz * (NY * NC) + y * NC + cc >= z * (NY * NC) + yo * NC + c
                    where = (q * PLANES + zz) * (NY * NC) + yo * NC + cc
                    value = entry(lb, rb, yo, zz * NC + cc, False, kind, where)
                    count = put(value, live & (rb // QUARTER == x), count)
            return count

        return lax.fori_loop(z, NZ, plane, count)

    def second(q, count):
        def plane(zz, count):
            to = jnp.where(zz == z, NZ, zz)
            clear(q * PLANES + to)
            for cc in range(NC):
                for yo in range(NY):
                    at = (q * META + NY + zz * NC + cc) * span + z * (NY * NC) + yo * NC + c
                    lb, rb, kind = meta_ref[at], meta_ref[at + half], meta_ref[at + TILE]
                    live = zz * (NY * NC) + y * NC + cc <= z * (NY * NC) + yo * NC + c
                    where = (q * PLANES + to) * (NY * NC) + yo * NC + cc
                    value = entry(rb, lb, yo, zz * NC + cc, True, kind, where)
                    count = put(value, live & (lb // QUARTER == x), count)
            return count

        return lax.fori_loop(0, z + 1, plane, count)

    nothing = TRASH + TRASH * 256
    for k in range(GROUP):
        slots[k] = nothing
    count = lax.fori_loop(0, NX, first, GROUP)
    count = lax.fori_loop(0, NX, second, count)
    for k in range(2 * GROUP):
        slots[count + k] = nothing
    steps = (count - GROUP + GROUP - 1) // GROUP

    def parts(value):
        return value & 255, (value >> 8) & 255, (value >> 16) & 4095, value >> 28

    def block(at):
        return high[at], low[at]

    def add(at, value):
        p, s, j = at // 16, lax.rem(at // 4, 4), lax.rem(at, 4)
        grad[p, s, j] += value

    def work(step, carry):
        done = []
        for k in range(GROUP):
            li, ri, _, _ = parts(slots[step * GROUP + k])
            top, rest = held[k, 0], held[k, 1]
            left, right = block(li), block(ri)
            gr = mm(three(top, rest, 1), three_other(left[0], left[1], 0), NN)
            gl = mm(three(top.T, rest.T, 1), three_other(right[0], right[1], 0), NN)
            done.append((li, ri, gl, gr))
        for k in range(GROUP):
            li, ri, where, positive = parts(slots[(step + 1) * GROUP + k])
            top, rest = residue(block(li), block(ri), edge[where], positive > 0)
            held[k, 0] = top
            held[k, 1] = rest
        for li, ri, gl, gr in done:
            add(li, gl)
            add(ri, gr)
        return carry

    lax.fori_loop(0, steps + 1, work, 0)


def compute(meta, high, low, edges):
    smem = pl.BlockSpec(memory_space=pltpu.SMEM)
    vmem = pl.BlockSpec(memory_space=pltpu.VMEM)
    return pl.pallas_call(
        compute_kernel,
        out_shape=jax.ShapeDtypeStruct((PARTS + 1, 4, 4, TILE, TILE), jnp.float32),
        in_specs=[smem, vmem, vmem, vmem],
        out_specs=vmem,
        scratch_shapes=[
            pltpu.SMEM((NX * CAND + 3 * GROUP,), jnp.int32),
            pltpu.VMEM((GROUP, 2, TILE, TILE), jnp.bfloat16),
        ],
        compiler_params=pltpu.CompilerParams(vmem_limit_bytes=SLOT_VMEM),
        name="slot_gradients",
    )(meta.reshape(NX * META * IDS * TILE), high, low,
      edges.reshape(NX * CAND, NBR, TILE))


class Ring:
    def __init__(self, cp, name, axis, at, part, far, near, made):
        self.cp, self.name, self.axis, self.part = cp, name, axis, part
        self.far, self.near, self.made = far, near, made
        self.at = {d: step_of(at, d, 4) for d in (-1, 0, 1, 2)}

    def to(self, sign):
        return {self.axis: self.at[sign]}

    def begin(self):
        for k, s in enumerate((1, -1)):
            self.cp.start((self.name, "far", s), self.part(self.at[2], k), self.far.at[k], self.to(s))
        for k, s in enumerate((1, -1)):
            h = 1 - k
            self.cp.start((self.name, "near", s, h), self.part(self.at[s], h), self.near.at[k, h], self.to(s))

    def pass_on(self):
        for k, s in enumerate((1, -1)):
            self.cp.arrived((self.name, "far", s), self.far.at[k], self.to(-s))
            self.made[k] = self.part(self.at[s], k)[...] + self.far[k]
            self.cp.start((self.name, "near", s, k), self.made.at[k], self.near.at[k, k], self.to(s))

    def total(self, half):
        for k, s in enumerate((1, -1)):
            self.cp.arrived((self.name, "near", s, half), self.near.at[k, half], self.to(-s))
        return self.part(self.at[0], half)[...] + self.near[0, half] + self.near[1, half]


REDUCE_SEMS = 64


def reduce_kernel(grad, out, a_far, a_near, a_made, a_sum, b_far, b_near, b_made, b_sum,
                  c_far, c_near, c_made, d_far, d_near, d_made,
                  partner, z_in, z_out, send_sems, recv_sems):
    z, y, c, x = position()
    other = 1 - c
    zd = {d: step_of(z, d, NZ) for d in range(-4, 5)}
    cp = Copies(send_sems, recv_sems)

    barrier = pltpu.get_barrier_semaphore()
    peers = [{"y": step_of(y, 1, NY)}, {"y": step_of(y, -1, NY)}, {"x": step_of(x, 1, NX)},
             {"x": step_of(x, -1, NX)}, {"z": zd[1]}, {"z": zd[-1]}, {"core": other}]
    for peer in peers:
        pl.semaphore_signal(barrier, inc=1, device_id=peer, device_id_type=MESH)
    pl.semaphore_wait(barrier, len(peers))

    a = Ring(cp, "a", "y", y, lambda dest, h: grad.at[dest, pl.ds(2 * h, 2), pl.ds(0, 2)], a_far, a_near, a_made)
    b = Ring(cp, "b", "x", x, lambda dest, h: grad.at[pl.ds(2 * h, 2), dest, pl.ds(2, 2)], b_far, b_near, b_made)

    def moved_at(d, cc):
        return PARTS // 2 + zd[d] // 2, lax.rem(zd[d], 2) * NC + cc

    order = [4, 3, -3, 2, -2, 1, -1, 0]
    for d in order:
        cp.start(("p", d), grad.at[moved_at(d, other)], partner.at[zd[d]], {"core": other})
    a.begin()
    b.begin()

    slot = {}
    for s in (1, -1):
        for d in (4, 3, 2, 1):
            for sub in (0, 1):
                if d < 4 or sub == (0 if s > 0 else 1):
                    slot[s, d, sub] = len(slot)

    def mine(d, sub):
        p, s = moved_at(d, c)
        return grad[p, s, pl.ds(2 * sub, 2)] + partner[zd[d], pl.ds(2 * sub, 2)]

    def zsend(s, d, sub, received):
        at = slot[s, d, sub]
        value = mine(s * d if d < 4 else 4, sub)
        if received:
            value = value + z_in[slot[s, d + 1, sub]]
        z_out[at] = value
        cp.start(("z", s, d, sub), z_out.at[at], z_in.at[at], {"z": zd[s]})

    def zgot(s, d, sub):
        cp.arrived(("z", s, d, sub), z_in.at[slot[s, d, sub]], {"z": zd[-s]})

    def from_core(d):
        cp.arrived(("p", d), partner.at[zd[d]], {"core": other})

    lead = {1: 0, -1: 1}
    from_core(4)
    for s in (1, -1):
        zsend(s, 4, lead[s], False)
    for s in (1, -1):
        from_core(3 * s)
        zsend(s, 3, 1 - lead[s], False)
    from_core(2)
    from_core(-2)
    for s in (1, -1):
        zgot(s, 4, lead[s])
        zsend(s, 3, lead[s], True)
    a.pass_on()
    b.pass_on()
    for s in (1, -1):
        zgot(s, 3, 1 - lead[s])
        zsend(s, 2, 1 - lead[s], True)
    for s in (1, -1):
        zgot(s, 3, lead[s])
        zsend(s, 2, lead[s], True)
    from_core(1)
    from_core(-1)
    from_core(0)
    for s in (1, -1):
        zgot(s, 2, 1 - lead[s])
        zsend(s, 1, 1 - lead[s], True)
    for h in (1, 0):
        a_sum[pl.ds(2 * h, 2)] = a.total(h)
        b_sum[pl.ds(2 * h, 2)] = b.total(h)
    second_a = Ring(cp, "c", "x", x, lambda dest, h: a_sum.at[dest, pl.ds(h, 1)], c_far, c_near, c_made)
    second_b = Ring(cp, "d", "y", y, lambda dest, h: b_sum.at[dest, pl.ds(h, 1)], d_far, d_near, d_made)
    second_a.begin()
    second_b.begin()
    for s in (1, -1):
        zgot(s, 2, lead[s])
        zsend(s, 1, lead[s], True)
    second_a.pass_on()
    second_b.pass_on()
    for sub in (0, 1):
        zgot(1, 1, sub)
        zgot(-1, 1, sub)
        value = mine(0, sub) + z_in[slot[1, 1, sub]] + z_in[slot[-1, 1, sub]]
        ring = second_a if sub == 0 else second_b
        for h in (0, 1):
            out[2 * sub + h] = value[h] + ring.total(h)[0]
    cp.drain()


def reduce(grad):
    vmem = pl.BlockSpec(memory_space=pltpu.VMEM)
    tile = (TILE, TILE)
    f32 = jnp.float32

    def ring(blocks):
        return [pltpu.VMEM((2,) + blocks + tile, f32), pltpu.VMEM((2, 2) + blocks + tile, f32),
                pltpu.VMEM((2,) + blocks + tile, f32)]

    first, second = (2, 2), (1,)
    return pl.pallas_call(
        reduce_kernel,
        out_shape=jax.ShapeDtypeStruct((QUARTER,) + tile, f32),
        in_specs=[vmem],
        out_specs=vmem,
        scratch_shapes=ring(first) + [pltpu.VMEM((4, 2) + tile, f32)]
        + ring(first) + [pltpu.VMEM((4, 2) + tile, f32)]
        + ring(second) + ring(second)
        + [
            pltpu.VMEM((NZ, QUARTER) + tile, f32),
            pltpu.VMEM((14, 2) + tile, f32),
            pltpu.VMEM((14, 2) + tile, f32),
            pltpu.SemaphoreType.DMA((REDUCE_SEMS,)),
            pltpu.SemaphoreType.DMA((REDUCE_SEMS,)),
        ],
        compiler_params=pltpu.CompilerParams(
            collective_id=1, has_side_effects=True, vmem_limit_bytes=REDUCE_VMEM
        ),
        name="reduce_rows",
    )(grad)


def body(latent, left_block, right_block, slot_kind, edge_cols):
    lat = latent.reshape(BLOCKS, TILE, TILE)
    edges = edge_cols.reshape(NZ, NY, NC, 2, NBR, TILE)
    lb, rb, kind = [v[0, 0].T.reshape(2, 1, 1, 2 * TILE // 4) for v in (left_block, right_block, slot_kind)]
    top = jnp.concatenate([lb, rb], axis=3)
    rest = jnp.pad(kind, ((0, 0), (0, 0), (0, 0), (0, TILE // 2)))
    ids = jnp.concatenate([top, rest], axis=1)
    high, low, edge, meta = gather(lat, edges, ids)
    grad = compute(meta, high, low, edge)
    out = reduce(grad)
    return out.reshape(QUARTER * TILE, TILE)


def solution(mesh):
    fine = Mesh(mesh.devices.reshape(NZ, NY, NC, NX), ("z", "y", "core", "x"))
    rows = ("z", "y", "core")
    return jax.shard_map(
        body,
        mesh=fine,
        in_specs=(
            P(rows, None),
            P(rows, "x", None, None),
            P(rows, "x", None, None),
            P(rows, "x", None, None),
            P(rows, "x", None, None, None, None),
        ),
        out_specs=P(("z", "y", "core", "x"), None),
        check_vma=False,
    )
```

```python
import functools

import jax
import jax.numpy as jnp
from jax import lax
from jax.experimental import pallas as pl
from jax.experimental.pallas import tpu as pltpu
from jax.sharding import Mesh
from jax.sharding import PartitionSpec as P

NZ, NY, NC, NX = 8, 4, 2, 4
BLOCKS = 16
QUARTER = 4
TILE = 128
NBR = 8
OWN = NY * BLOCKS
MOVED = NZ * NC * QUARTER
ALL = OWN + MOVED
PLANES = NZ + 1
CAND = PLANES * NY * NC
META = NY + NZ * NC
PARTS = ALL // 16
TRASH = ALL
GROUP = 4
MESH = pl.DeviceIdType.MESH
GATHER_VMEM, SLOT_VMEM, REDUCE_VMEM = 32 << 20, 24 << 20, 28 << 20

NT = (((1,), (1,)), ((), ()))
NN = (((1,), (0,)), ((), ()))


def position():
    return tuple(lax.axis_index(name) for name in ("z", "y", "core", "x"))


def step_of(value, by, size):
    return lax.rem(value + (by + size), size)


class Copies:
    def __init__(self, send_sems, recv_sems):
        self.send_sems, self.recv_sems = send_sems, recv_sems
        self.index = {}
        self.sent = []

    def sems(self, name):
        at = self.index.setdefault(name, len(self.index))
        return self.send_sems.at[at], self.recv_sems.at[at]

    def make(self, name, src, dst, device):
        send, recv = self.sems(name)
        return pltpu.make_async_remote_copy(
            src_ref=src, dst_ref=dst, send_sem=send, recv_sem=recv,
            device_id=device, device_id_type=MESH,
        )

    def start(self, name, src, dst, device, when=None):
        copy = self.make(name, src, dst, device)
        self.sent.append((copy, when))
        if when is None:
            copy.start()
        else:
            pl.when(when)(copy.start)

    def arrived(self, name, landed, device, when=None):
        copy = self.make(name, landed, landed, device)
        if when is None:
            copy.wait_recv()
        else:
            pl.when(when)(copy.wait_recv)

    def drain(self):
        for copy, when in self.sent:
            if when is None:
                copy.wait_send()
            else:
                pl.when(when)(copy.wait_send)


GATHER_SEMS = 128
IDS = 3


def entries(meta, entry, z, y, c, x):
    step = NY * NC

    def one(q, carry):
        def write(rows, own_ids, moved_ids, kinds, yo, zc, plane, flip, live):
            cc = zc & 1
            own_at = yo * BLOCKS + own_ids
            moved_at = OWN + zc * QUARTER + moved_ids - x * QUARTER
            left, right = (moved_at, own_at) if flip else (own_at, moved_at)
            where = (q * PLANES + plane) * step + yo * NC + cc
            value = left + right * 256 + where * 65536 + jnp.where(kinds == 2, 1 << 28, 0)
            take = live & ((moved_ids >> 2) == x)
            entry[q, rows] = jnp.where(take, value, -1)

        shape = (NY, 1, TILE)
        s = lax.broadcasted_iota(jnp.int32, shape, 2) & (NZ * step - 1)
        yo = lax.broadcasted_iota(jnp.int32, shape, 0)
        rows = pl.ds(0, NY)
        lb, rb, kind = [meta[q, rows, v] for v in range(IDS)]
        live = s >= z * step + yo * NC + c
        write(rows, lb, rb, kind, yo, (s >> 3) * NC + (s & 1), s >> 3, False, live)

        shape = (NZ * NC, 1, TILE)
        s = lax.broadcasted_iota(jnp.int32, shape, 2) & (NZ * step - 1)
        zc = lax.broadcasted_iota(jnp.int32, shape, 0)
        rows = pl.ds(NY, NZ * NC)
        lb, rb, kind = [meta[q, rows, v] for v in range(IDS)]
        zz = zc >> 1
        live = zz * step + y * NC + (zc & 1) <= s
        write(rows, rb, lb, kind, (s >> 1) & 3, zc, jnp.where(zz == z, NZ, zz), True, live)
        return carry

    lax.fori_loop(0, NX, one, 0)


def gather_kernel(lat, edges, ids, high, low, edge, entry, land, meta,
                  send_sems, recv_sems, local_sems):
    z, y, c, x = position()
    other = 1 - c
    ys = [step_of(y, d, NY) for d in range(NY)]
    yd = {1: ys[1], -1: ys[3], 2: ys[2]}
    xd = {1: step_of(x, 1, NX), -1: step_of(x, -1, NX), 2: step_of(x, 2, NX)}
    zd = {d: step_of(z, d, NZ) for d in range(-4, NZ)}
    cp = Copies(send_sems, recv_sems)
    cs = [c, other]

    barrier = pltpu.get_barrier_semaphore()
    peers = [{"y": ys[d]} for d in (1, 2, 3)] + [{"x": xd[1]}, {"x": xd[-1]}]
    peers += [{"z": zd[dz], "core": cs[dc]} for dz in range(NZ) for dc in range(NC) if dz or dc]
    for peer in peers:
        pl.semaphore_signal(barrier, inc=1, device_id=peer, device_id_type=MESH)

    local = []

    def here(src, dst, when=None):
        copy = pltpu.make_async_copy(src, dst, local_sems.at[len(local)])
        local.append((copy, when))
        if when is None:
            copy.start()
        else:
            pl.when(when)(copy.start)

    def moved_at(zz, cc):
        return PARTS // 2 + zz // 2, lax.rem(zz, 2) * NC + cc

    for zp in range(NZ):
        here(edges.at[zp, y, :, 0], edge.at[x, zp, y], zp >= z)
    here(edges.at[z, :, c, 1], edge.at[x, NZ, :, c])
    here(ids.at[0], meta.at[x, y])
    here(ids.at[1], meta.at[x, NY + z * NC + c])
    edge_local = len(local)
    here(lat, land.at[y])
    here(lat.at[x], land.at[moved_at(z, c)])

    pl.semaphore_wait(barrier, len(peers))

    def quarter_of(row, at, count):
        return land.at[row, at // 4, pl.ds(lax.rem(at, 4), count)]

    def moved_sub(zz, cc, sub):
        p, s = moved_at(zz, cc)
        return land.at[p, s, pl.ds(2 * sub, 2)]

    def zsend(sign, step, sub):
        origin = zd[-(step - 1)] if sign > 0 else zd[step - 1]
        dst = moved_sub(origin, c, sub)
        src = lat.at[x, pl.ds(2 * sub, 2)] if step == 1 else dst
        cp.start(("z", sign, step, sub), src, dst, {"z": zd[sign]})

    def zgot(sign, step, sub):
        origin = zd[-step] if sign > 0 else zd[step]
        cp.arrived(("z", sign, step, sub), moved_sub(origin, c, sub), {"z": zd[-sign]})

    def to_core(key, origin, src):
        cp.start(("core", key), src, land.at[moved_at(origin, c)], {"core": other})

    def split(part, sub):
        def one(j, carry):
            value = land[part, sub, j]
            top = value.astype(jnp.bfloat16)
            high[part * 16 + sub * 4 + j] = top
            low[part * 16 + sub * 4 + j] = (value - top.astype(jnp.float32)).astype(jnp.bfloat16)
            return carry

        lax.fori_loop(0, 4, one, 0)

    lead = {1: 0, -1: 1}

    for s in (1, -1):
        at = 2 * x
        cp.start(("yx", s), lat.at[at // 4, pl.ds(lax.rem(at, 4), 2)], quarter_of(y, at, 2), {"y": yd[s]})
    for d in (1, 2, 3):
        for zp in range(NZ):
            cp.start(("e0", d, zp), edges.at[zp, ys[d], :, 0], edge.at[x, zp, y], {"y": ys[d]}, zp >= z)
        cp.start(("m0", d), ids.at[0], meta.at[x, y], {"y": ys[d]})
    for dz in range(NZ):
        for dc in range(NC):
            if dz or dc:
                zs, cc = zd[dz], cs[dc]
                plane = NZ if dz == 0 else z
                cp.start(("e1", dz, dc), edges.at[zs, :, cc, 1], edge.at[x, plane, :, c],
                         {"z": zs, "core": cc}, zs >= z)
                cp.start(("m1", dz, dc), ids.at[1], meta.at[x, NY + z * NC + c],
                         {"z": zs, "core": cc})
    for s in (1, -1):
        zsend(s, 1, lead[s])
    for s in (1, -1):
        h = lead[s]
        cp.start(("yd", s, h), lat.at[2 + h], land.at[y, 2 + h], {"y": yd[s]})
    for s in (1, -1):
        zsend(s, 1, 1 - lead[s])
    to_core(0, z, lat.at[x])

    def xsend(key, row, half):
        for s in (1, -1):
            at = 2 * x + (half if s > 0 else 1 - half)
            ref = quarter_of(row, at, 1)
            cp.start(("xo", key, s, half), ref, ref, {"x": xd[s]})

    def xgot(key, row, half, relay):
        for s in (1, -1):
            origin = xd[-s]
            ref = quarter_of(row, 2 * origin + (half if s > 0 else 1 - half), 1)
            cp.arrived(("xo", key, s, half), ref, {"x": origin})
            if relay:
                cp.start(("xr", key, s), ref, ref, {"x": xd[s]})

    def zstep(step, k):
        for s in (1, -1):
            sub = lead[s] if k == 0 else 1 - lead[s]
            zgot(s, step, sub)
            if step < 3 or (step == 3 and k == 0):
                zsend(s, step + 1, sub)

    def zdone(step):
        for s in (1, -1):
            if step < 4 or s == 1:
                origin = zd[-s * step] if step < 4 else zd[4]
                to_core((s, step), origin, land.at[moved_at(origin, c)])

    for s in (1, -1):
        row = yd[-s]
        cp.arrived(("yx", s), quarter_of(row, 2 * x, 2), {"y": row})
        ref = quarter_of(row, 2 * x + lead[s], 1)
        cp.start(("yxr", s), ref, ref, {"y": yd[s]})
    for s in (1, -1):
        h = 1 - lead[s]
        cp.start(("yd", s, h), lat.at[2 + h], land.at[y, 2 + h], {"y": yd[s]})
    for half in (0, 1):
        for key in (1, -1):
            xsend(key, yd[key], half)
    zstep(1, 0)

    for copy, when in local[:edge_local]:
        if when is None:
            copy.wait()
        else:
            pl.when(when)(copy.wait)
    for d in (1, 2, 3):
        src = ys[NY - d]
        for zp in range(NZ):
            cp.arrived(("e0", d, zp), edge.at[x, zp, src], {"y": src}, zp >= z)
        cp.arrived(("m0", d), meta.at[x, src], {"y": src})
    for dz in range(NZ):
        for dc in range(NC):
            if dz or dc:
                zr, cr = zd[(NZ - dz) % NZ], cs[dc]
                plane = NZ if dz == 0 else zr
                cp.arrived(("e1", dz, dc), edge.at[x, plane, :, cr], {"z": zr, "core": cr}, zr <= z)
                cp.arrived(("m1", dz, dc), meta.at[x, NY + zr * NC + cr], {"z": zr, "core": cr})
    pieces = {0: pl.ds(0, 5), 1: pl.ds(5, 4)}
    for s in (1, -1):
        cp.start(("xm", s), meta.at[x], meta.at[x], {"x": xd[s]})
    for k in (0, 1):
        for s in (1, -1):
            h = lead[s] if k == 0 else 1 - lead[s]
            cp.start(("xe", s, h), edge.at[x, pieces[h]], edge.at[x, pieces[h]], {"x": xd[s]})

    zstep(1, 1)
    zdone(1)
    for s in (1, -1):
        h, row = lead[s], yd[-s]
        cp.arrived(("yd", s, h), land.at[row, 2 + h], {"y": row})
        cp.start(("ydr", s), land.at[row, 2 + h], land.at[row, 2 + h], {"y": yd[s]})
    zstep(2, 0)
    for s in (1, -1):
        ref = quarter_of(yd[2], 2 * x + lead[s], 1)
        cp.arrived(("yxr", s), ref, {"y": yd[-s]})
    for half in (0, 1):
        xsend(2, yd[2], half)
    for key in (1, -1):
        xgot(key, yd[key], 0, True)
    for copy, when in local[edge_local:]:
        copy.wait()
    zstep(2, 1)
    zdone(2)
    for sub in range(4):
        split(y, sub)
    split(*moved_at(z, c))
    zstep(3, 0)
    for s in (1, -1):
        h, src = lead[s], xd[-s]
        cp.arrived(("xm", s), meta.at[src], {"x": src})
        if s > 0:
            cp.start(("xmr", s), meta.at[src], meta.at[src], {"x": xd[s]})
        cp.arrived(("xe", s, h), edge.at[src, pieces[h]], {"x": src})
        cp.start(("xer", s), edge.at[src, pieces[h]], edge.at[src, pieces[h]], {"x": xd[s]})
    xgot(2, yd[2], 0, True)
    zstep(3, 1)
    zdone(3)
    cp.arrived(("core", 0), land.at[moved_at(z, other)], {"core": other})
    split(*moved_at(z, other))
    for step in (1, 2):
        for s in (1, -1):
            origin = zd[-s * step]
            cp.arrived(("core", (s, step)), land.at[moved_at(origin, other)], {"core": other})
            split(*moved_at(origin, other))
            split(*moved_at(origin, c))
    for s in (1, -1):
        h, row = 1 - lead[s], yd[-s]
        cp.arrived(("yd", s, h), land.at[row, 2 + h], {"y": row})
        for sub in (2, 3):
            split(row, sub)
    zstep(4, 0)
    zdone(4)
    for s in (1, -1):
        origin = zd[-s * 3]
        cp.arrived(("core", (s, 3)), land.at[moved_at(origin, other)], {"core": other})
        split(*moved_at(origin, other))
        split(*moved_at(origin, c))
    split(*moved_at(zd[4], c))
    for s in (1, -1):
        h, src = 1 - lead[s], xd[-s]
        cp.arrived(("ydr", s), land.at[yd[2], 2 + lead[s]], {"y": yd[-s]})
        split(yd[2], 2 + lead[s])
    for key in (1, -1, 2):
        xgot(key, yd[key], 1, False)
        for s in (1, -1):
            ref = quarter_of(yd[key], 2 * xd[2] + lead[s], 1)
            cp.arrived(("xr", key, s), ref, {"x": xd[-s]})
        for sub in (0, 1):
            split(yd[key], sub)
    for s in (1, -1):
        h, src = 1 - lead[s], xd[-s]
        if s > 0:
            cp.arrived(("xmr", s), meta.at[xd[2]], {"x": src})
    entries(meta, entry, z, y, c, x)
    for s in (1, -1):
        h, src = 1 - lead[s], xd[-s]
        cp.arrived(("xe", s, h), edge.at[src, pieces[h]], {"x": src})
        cp.arrived(("xer", s), edge.at[xd[2], pieces[1 - h]], {"x": src})
    cp.arrived(("core", (1, 4)), land.at[moved_at(zd[4], other)], {"core": other})
    split(*moved_at(zd[4], other))
    cp.drain()


def gather(lat, edges, ids):
    hbm = pl.BlockSpec(memory_space=pltpu.HBM)
    vmem = pl.BlockSpec(memory_space=pltpu.VMEM)
    return pl.pallas_call(
        gather_kernel,
        out_shape=(
            jax.ShapeDtypeStruct((ALL + 1, TILE, TILE), jnp.bfloat16),
            jax.ShapeDtypeStruct((ALL + 1, TILE, TILE), jnp.bfloat16),
            jax.ShapeDtypeStruct((NX, PLANES, NY, NC, NBR, TILE), jnp.int32),
            jax.ShapeDtypeStruct((NX, META, 1, TILE), jnp.int32),
        ),
        in_specs=[hbm] * 3,
        out_specs=(vmem,) * 4,
        scratch_shapes=[
            pltpu.VMEM((PARTS, 4, 4, TILE, TILE), jnp.float32),
            pltpu.VMEM((NX, META, IDS, 1, TILE), jnp.int32),
            pltpu.SemaphoreType.DMA((GATHER_SEMS,)),
            pltpu.SemaphoreType.DMA((GATHER_SEMS,)),
            pltpu.SemaphoreType.DMA((16,)),
        ],
        compiler_params=pltpu.CompilerParams(
            collective_id=0, has_side_effects=True, vmem_limit_bytes=GATHER_VMEM
        ),
        name="gather_rows",
    )(pltpu.with_memory_space_constraint(lat.reshape(4, 4, TILE, TILE), pltpu.HBM),
      pltpu.with_memory_space_constraint(edges, pltpu.HBM), ids)


def product(x, w, dims):
    left = jnp.concatenate(x, axis=1)
    none = jnp.zeros_like(w[0])
    if dims is NT:
        right = jnp.concatenate(
            [jnp.concatenate([w[0], w[0]], axis=1), jnp.concatenate([w[1], none], axis=1)], axis=0
        )
    else:
        right = jnp.concatenate(
            [jnp.concatenate([w[0], w[1]], axis=1), jnp.concatenate([w[0], none], axis=1)], axis=0
        )
    both = lax.dot_general(left, right, dims, preferred_element_type=jnp.float32)
    return both[:, :TILE] + both[:, TILE:]


def residue(left, right, edges, positive):
    scores = product(right, left, NT)
    bit = jnp.where(positive, lax.shift_left(jnp.ones_like(edges), edges & 31), 0)
    word = edges >> 5
    rows = lax.broadcasted_iota(jnp.int32, (NBR, TILE), 0)
    words, tests = [], []
    for w in range(4):
        have = jnp.where(word == w, bit, 0)
        for shift in (4, 2, 1):
            have = have | pltpu.roll(have, shift, 0)
        words += [have] * 4
        tests.append(lax.shift_left(jnp.ones_like(edges), rows + 8 * w))
    hit = (jnp.concatenate(words, axis=0) & jnp.concatenate(tests * 4, axis=0)) != 0
    value = 1.0 / (1.0 + jnp.exp(-scores)) - jnp.where(hit, 1.0, 0.0)
    top = value.astype(jnp.bfloat16)
    return top, (value - top.astype(jnp.float32)).astype(jnp.bfloat16)


def compute_kernel(entry, high, low, edge, grad, slots, held):
    z, y, c, x = position()

    def clear(part):
        grad[part] = jnp.zeros((4, 4, TILE, TILE), jnp.float32)

    def put(places, count):
        for k in range(0, len(places), 8):
            values = [entry[at] for at in places[k : k + 8]]
            for value in values:
                slots[count] = value
                count = count + (1 + (value >> 31))
        return count

    def first(zz, count):
        clear(zz)
        base = zz * (NY * NC) + y * NC
        return put([base + (q * META + yo) * TILE + cc
                    for q in range(NX) for yo in range(NY) for cc in range(NC)], count)

    def second(zz, count):
        clear(jnp.where(zz == z, NZ, zz))
        base = zz * (NC * TILE) + z * (NY * NC) + c
        return put([base + (q * META + NY + cc) * TILE + yo * NC
                    for q in range(NX) for yo in range(NY) for cc in range(NC)], count)

    nothing = TRASH + TRASH * 256
    for k in range(GROUP):
        slots[k] = nothing
    count = lax.fori_loop(z, NZ, first, GROUP)
    count = lax.fori_loop(0, z + 1, second, count)
    for k in range(2 * GROUP):
        slots[count + k] = nothing
    steps = (count - GROUP + GROUP - 1) // GROUP

    def parts(value):
        return value & 255, (value >> 8) & 255, (value >> 16) & 4095, value >> 28

    def block(at):
        return high[at], low[at]

    def add(at, value):
        p, s, j = at // 16, lax.rem(at // 4, 4), lax.rem(at, 4)
        grad[p, s, j] += value

    def work(step, carry):
        done = []
        for k in range(GROUP):
            li, ri, _, _ = parts(slots[step * GROUP + k])
            top, rest = held[k, 0], held[k, 1]
            left, right = block(li), block(ri)
            gr = product((top, rest), left, NN)
            gl = product((top.T, rest.T), right, NN)
            done.append((li, ri, gl, gr))
            li, ri, where, positive = parts(slots[(step + 1) * GROUP + k])
            top, rest = residue(block(li), block(ri), edge[where], positive > 0)
            held[k, 0] = top
            held[k, 1] = rest
        for li, ri, gl, gr in done:
            add(li, gl)
            add(ri, gr)
        return carry

    lax.fori_loop(0, steps + 1, work, 0)


def compute(entry, high, low, edges):
    smem = pl.BlockSpec(memory_space=pltpu.SMEM)
    vmem = pl.BlockSpec(memory_space=pltpu.VMEM)
    return pl.pallas_call(
        compute_kernel,
        out_shape=jax.ShapeDtypeStruct((PARTS + 1, 4, 4, TILE, TILE), jnp.float32),
        in_specs=[smem, vmem, vmem, vmem],
        out_specs=vmem,
        scratch_shapes=[
            pltpu.SMEM((NX * CAND + 3 * GROUP,), jnp.int32),
            pltpu.VMEM((GROUP, 2, TILE, TILE), jnp.bfloat16),
        ],
        compiler_params=pltpu.CompilerParams(vmem_limit_bytes=SLOT_VMEM),
        name="slot_gradients",
    )(entry.reshape(NX * META * TILE), high, low,
      edges.reshape(NX * CAND, NBR, TILE))


class Ring:
    def __init__(self, cp, name, axis, at, part, far, near, made):
        self.cp, self.name, self.axis, self.part = cp, name, axis, part
        self.far, self.near, self.made = far, near, made
        self.at = {d: step_of(at, d, 4) for d in (-1, 0, 1, 2)}

    def to(self, sign):
        return {self.axis: self.at[sign]}

    def begin(self):
        for k, s in enumerate((1, -1)):
            self.cp.start((self.name, "far", s), self.part(self.at[2], k), self.far.at[k], self.to(s))
        for k, s in enumerate((1, -1)):
            h = 1 - k
            self.cp.start((self.name, "near", s, h), self.part(self.at[s], h), self.near.at[k, h], self.to(s))

    def pass_on(self):
        for k, s in enumerate((1, -1)):
            self.cp.arrived((self.name, "far", s), self.far.at[k], self.to(-s))
            self.made[k] = self.part(self.at[s], k)[...] + self.far[k]
            self.cp.start((self.name, "near", s, k), self.made.at[k], self.near.at[k, k], self.to(s))

    def total(self, half):
        for k, s in enumerate((1, -1)):
            self.cp.arrived((self.name, "near", s, half), self.near.at[k, half], self.to(-s))
        return self.part(self.at[0], half)[...] + self.near[0, half] + self.near[1, half]


REDUCE_SEMS = 64


def reduce_kernel(grad, out, a_far, a_near, a_made, a_sum, b_far, b_near, b_made, b_sum,
                  c_far, c_near, c_made, d_far, d_near, d_made,
                  partner, z_in, z_out, send_sems, recv_sems):
    z, y, c, x = position()
    other = 1 - c
    zd = {d: step_of(z, d, NZ) for d in range(-4, 5)}
    cp = Copies(send_sems, recv_sems)

    barrier = pltpu.get_barrier_semaphore()
    peers = [{"y": step_of(y, 1, NY)}, {"y": step_of(y, -1, NY)}, {"x": step_of(x, 1, NX)},
             {"x": step_of(x, -1, NX)}, {"z": zd[1]}, {"z": zd[-1]}, {"core": other}]
    for peer in peers:
        pl.semaphore_signal(barrier, inc=1, device_id=peer, device_id_type=MESH)
    pl.semaphore_wait(barrier, len(peers))

    a = Ring(cp, "a", "y", y, lambda dest, h: grad.at[dest, pl.ds(2 * h, 2), pl.ds(0, 2)], a_far, a_near, a_made)
    b = Ring(cp, "b", "x", x, lambda dest, h: grad.at[pl.ds(2 * h, 2), dest, pl.ds(2, 2)], b_far, b_near, b_made)

    def moved_at(d, cc):
        return PARTS // 2 + zd[d] // 2, lax.rem(zd[d], 2) * NC + cc

    order = [4, 3, -3, 2, -2, 1, -1, 0]
    for d in order:
        cp.start(("p", d), grad.at[moved_at(d, other)], partner.at[zd[d]], {"core": other})
    a.begin()
    b.begin()

    slot = {}
    for s in (1, -1):
        for d in (4, 3, 2, 1):
            for sub in (0, 1):
                if d < 4 or sub == (0 if s > 0 else 1):
                    slot[s, d, sub] = len(slot)

    def mine(d, sub):
        p, s = moved_at(d, c)
        return grad[p, s, pl.ds(2 * sub, 2)] + partner[zd[d], pl.ds(2 * sub, 2)]

    def zsend(s, d, sub, received):
        at = slot[s, d, sub]
        value = mine(s * d if d < 4 else 4, sub)
        if received:
            value = value + z_in[slot[s, d + 1, sub]]
        z_out[at] = value
        cp.start(("z", s, d, sub), z_out.at[at], z_in.at[at], {"z": zd[s]})

    def zgot(s, d, sub):
        cp.arrived(("z", s, d, sub), z_in.at[slot[s, d, sub]], {"z": zd[-s]})

    def from_core(d):
        cp.arrived(("p", d), partner.at[zd[d]], {"core": other})

    lead = {1: 0, -1: 1}
    from_core(4)
    for s in (1, -1):
        zsend(s, 4, lead[s], False)
    for s in (1, -1):
        from_core(3 * s)
        zsend(s, 3, 1 - lead[s], False)
    from_core(2)
    from_core(-2)
    for s in (1, -1):
        zgot(s, 4, lead[s])
        zsend(s, 3, lead[s], True)
    a.pass_on()
    b.pass_on()
    for s in (1, -1):
        zgot(s, 3, 1 - lead[s])
        zsend(s, 2, 1 - lead[s], True)
    for s in (1, -1):
        zgot(s, 3, lead[s])
        zsend(s, 2, lead[s], True)
    from_core(1)
    from_core(-1)
    from_core(0)
    for s in (1, -1):
        zgot(s, 2, 1 - lead[s])
        zsend(s, 1, 1 - lead[s], True)
    for h in (1, 0):
        a_sum[pl.ds(2 * h, 2)] = a.total(h)
        b_sum[pl.ds(2 * h, 2)] = b.total(h)
    second_a = Ring(cp, "c", "x", x, lambda dest, h: a_sum.at[dest, pl.ds(h, 1)], c_far, c_near, c_made)
    second_b = Ring(cp, "d", "y", y, lambda dest, h: b_sum.at[dest, pl.ds(h, 1)], d_far, d_near, d_made)
    second_a.begin()
    second_b.begin()
    for s in (1, -1):
        zgot(s, 2, lead[s])
        zsend(s, 1, lead[s], True)
    second_a.pass_on()
    second_b.pass_on()
    for sub in (0, 1):
        zgot(1, 1, sub)
        zgot(-1, 1, sub)
        value = mine(0, sub) + z_in[slot[1, 1, sub]] + z_in[slot[-1, 1, sub]]
        ring = second_a if sub == 0 else second_b
        for h in (0, 1):
            out[2 * sub + h] = value[h] + ring.total(h)[0]
    cp.drain()


def reduce(grad):
    vmem = pl.BlockSpec(memory_space=pltpu.VMEM)
    tile = (TILE, TILE)
    f32 = jnp.float32

    def ring(blocks):
        return [pltpu.VMEM((2,) + blocks + tile, f32), pltpu.VMEM((2, 2) + blocks + tile, f32),
                pltpu.VMEM((2,) + blocks + tile, f32)]

    first, second = (2, 2), (1,)
    return pl.pallas_call(
        reduce_kernel,
        out_shape=jax.ShapeDtypeStruct((QUARTER,) + tile, f32),
        in_specs=[vmem],
        out_specs=vmem,
        scratch_shapes=ring(first) + [pltpu.VMEM((4, 2) + tile, f32)]
        + ring(first) + [pltpu.VMEM((4, 2) + tile, f32)]
        + ring(second) + ring(second)
        + [
            pltpu.VMEM((NZ, QUARTER) + tile, f32),
            pltpu.VMEM((14, 2) + tile, f32),
            pltpu.VMEM((14, 2) + tile, f32),
            pltpu.SemaphoreType.DMA((REDUCE_SEMS,)),
            pltpu.SemaphoreType.DMA((REDUCE_SEMS,)),
        ],
        compiler_params=pltpu.CompilerParams(
            collective_id=1, has_side_effects=True, vmem_limit_bytes=REDUCE_VMEM
        ),
        name="reduce_rows",
    )(grad)


def body(latent, left_block, right_block, slot_kind, edge_cols):
    lat = latent.reshape(BLOCKS, TILE, TILE)
    edges = edge_cols.reshape(NZ, NY, NC, 2, NBR, TILE)
    ids = jnp.stack([v[0, 0].T.reshape(2, 1, TILE // 2) for v in (left_block, right_block, slot_kind)], axis=1)
    ids = jnp.pad(ids, ((0, 0), (0, 0), (0, 0), (0, TILE // 2)))
    high, low, edge, entry = gather(lat, edges, ids)
    grad = compute(entry, high, low, edge)
    out = reduce(grad)
    return out.reshape(QUARTER * TILE, TILE)


def solution(mesh):
    fine = Mesh(mesh.devices.reshape(NZ, NY, NC, NX), ("z", "y", "core", "x"))
    rows = ("z", "y", "core")
    return jax.shard_map(
        body,
        mesh=fine,
        in_specs=(
            P(rows, None),
            P(rows, "x", None, None),
            P(rows, "x", None, None),
            P(rows, "x", None, None),
            P(rows, "x", None, None, None, None),
        ),
        out_specs=P(("z", "y", "core", "x"), None),
        check_vma=False,
    )
```

```python
import functools

import jax
import jax.numpy as jnp
from jax import lax
from jax.experimental import pallas as pl
from jax.experimental.pallas import tpu as pltpu
from jax.sharding import Mesh
from jax.sharding import PartitionSpec as P

NZ, NY, NC, NX = 8, 4, 2, 4
BLOCKS = 16
QUARTER = 4
TILE = 128
NBR = 8
OWN = NY * BLOCKS
MOVED = NZ * NC * QUARTER
ALL = OWN + MOVED
PLANES = NZ + 1
CAND = PLANES * NY * NC
META = NY + NZ * NC
PARTS = ALL // 16
TRASH = ALL
GROUP = 6
MESH = pl.DeviceIdType.MESH
GATHER_VMEM, SLOT_VMEM, REDUCE_VMEM = 32 << 20, 24 << 20, 28 << 20

NT = (((1,), (1,)), ((), ()))
NN = (((1,), (0,)), ((), ()))


def position():
    return tuple(lax.axis_index(name) for name in ("z", "y", "core", "x"))


def step_of(value, by, size):
    return lax.rem(value + (by + size), size)


class Copies:
    def __init__(self, send_sems, recv_sems):
        self.send_sems, self.recv_sems = send_sems, recv_sems
        self.index = {}
        self.sent = []

    def sems(self, name):
        at = self.index.setdefault(name, len(self.index))
        return self.send_sems.at[at], self.recv_sems.at[at]

    def make(self, name, src, dst, device):
        send, recv = self.sems(name)
        return pltpu.make_async_remote_copy(
            src_ref=src, dst_ref=dst, send_sem=send, recv_sem=recv,
            device_id=device, device_id_type=MESH,
        )

    def start(self, name, src, dst, device, when=None):
        copy = self.make(name, src, dst, device)
        self.sent.append((copy, when))
        if when is None:
            copy.start()
        else:
            pl.when(when)(copy.start)

    def arrived(self, name, landed, device, when=None):
        copy = self.make(name, landed, landed, device)
        if when is None:
            copy.wait_recv()
        else:
            pl.when(when)(copy.wait_recv)

    def drain(self):
        for copy, when in self.sent:
            if when is None:
                copy.wait_send()
            else:
                pl.when(when)(copy.wait_send)


GATHER_SEMS = 128
IDS = 3
ROWS = BLOCKS * TILE
SHARE = 192
HALF_SHARE = SHARE // 2
DIRECT = NX * SHARE
HALF_DIRECT = (ROWS - DIRECT) // 2
SPLIT_FROM = DIRECT // TILE
PEERS = NZ * NY * NC


def entries(meta, entry, z, y, c, x):
    step = NY * NC

    def one(q, carry):
        def write(rows, own_ids, moved_ids, kinds, yo, zc, plane, flip, live):
            cc = zc & 1
            own_at = yo * BLOCKS + own_ids
            moved_at = OWN + zc * QUARTER + moved_ids - x * QUARTER
            left, right = (moved_at, own_at) if flip else (own_at, moved_at)
            where = (q * PLANES + plane) * step + yo * NC + cc
            value = left + right * 256 + where * 65536 + jnp.where(kinds == 2, 1 << 28, 0)
            take = live & ((moved_ids >> 2) == x)
            entry[q, rows, :, pl.ds(0, PEERS)] = jnp.where(take, value, -1)

        shape = (NY, 1, PEERS)
        s = lax.broadcasted_iota(jnp.int32, shape, 2)
        yo = lax.broadcasted_iota(jnp.int32, shape, 0)
        rows = pl.ds(0, NY)
        lb, rb, kind = [meta[q, rows, v] for v in range(IDS)]
        live = s >= z * step + yo * NC + c
        write(rows, lb, rb, kind, yo, (s >> 3) * NC + (s & 1), s >> 3, False, live)

        shape = (NZ * NC, 1, PEERS)
        s = lax.broadcasted_iota(jnp.int32, shape, 2)
        zc = lax.broadcasted_iota(jnp.int32, shape, 0)
        rows = pl.ds(NY, NZ * NC)
        lb, rb, kind = [meta[q, rows, v] for v in range(IDS)]
        zz = zc >> 1
        live = zz * step + y * NC + (zc & 1) <= s
        write(rows, rb, lb, kind, (s >> 1) & 3, zc, jnp.where(zz == z, NZ, zz), True, live)
        return carry

    lax.fori_loop(0, NX, one, 0)


def gather_kernel(lat, edges, lefts, rights, kinds, high, low, edge, entry, land, meta, ids,
                  send_sems, recv_sems, local_sems, id_sems):
    z, y, c, x = position()
    other = 1 - c
    ys = [step_of(y, d, NY) for d in range(NY)]
    yd = {1: ys[1], -1: ys[3], 2: ys[2]}
    xd = {1: step_of(x, 1, NX), -1: step_of(x, -1, NX), 2: step_of(x, 2, NX)}
    zd = {d: step_of(z, d, NZ) for d in range(-4, NZ)}
    cp = Copies(send_sems, recv_sems)
    cs = [c, other]

    barrier = pltpu.get_barrier_semaphore()
    peers = [{"y": ys[d]} for d in (1, 2, 3)] + [{"x": xd[1]}, {"x": xd[-1]}]
    peers += [{"z": zd[dz], "core": cs[dc]} for dz in range(NZ) for dc in range(NC) if dz or dc]
    for peer in peers:
        pl.semaphore_signal(barrier, inc=1, device_id=peer, device_id_type=MESH)

    local = []

    def here(src, dst, when=None):
        copy = pltpu.make_async_copy(src, dst, local_sems.at[len(local)])
        local.append((copy, when))
        if when is None:
            copy.start()
        else:
            pl.when(when)(copy.start)

    def moved_at(zz, cc):
        return PARTS // 2 + zz // 2, (lax.rem(zz, 2) * NC + cc) * QUARTER

    def rows_of(part, start, count):
        return land.at[part, pl.ds(start, count)]

    def moved_rows(zz, cc):
        p, block = moved_at(zz, cc)
        return rows_of(p, block * TILE, QUARTER * TILE)

    def direct(half):
        return DIRECT + half * HALF_DIRECT

    raw = [pltpu.make_async_copy(ref, ids.at[:, v], id_sems.at[v])
           for v, ref in enumerate((lefts, rights, kinds))]
    for copy in raw:
        copy.start()
    for zp in range(NZ):
        here(edges.at[zp, y, :, 0], edge.at[x, zp, y], zp >= z)
    here(edges.at[z, :, c, 1], edge.at[x, NZ, :, c])
    edge_local = len(local)
    here(lat, land.at[y])
    here(lat.at[pl.ds(x * QUARTER * TILE, QUARTER * TILE)], moved_rows(z, c))

    for copy in raw:
        copy.wait()
    own_ids = [pltpu.make_async_copy(ids.at[0], meta.at[x, y], id_sems.at[0]),
               pltpu.make_async_copy(ids.at[1], meta.at[x, NY + z * NC + c], id_sems.at[1])]
    for copy in own_ids:
        copy.start()
    pl.semaphore_wait(barrier, len(peers))

    def moved_sub(zz, cc, sub):
        p, block = moved_at(zz, cc)
        return rows_of(p, (block + 2 * sub) * TILE, 2 * TILE)

    def zsend(sign, step, sub):
        origin = zd[-(step - 1)] if sign > 0 else zd[step - 1]
        dst = moved_sub(origin, c, sub)
        src = lat.at[pl.ds((x * QUARTER + 2 * sub) * TILE, 2 * TILE)] if step == 1 else dst
        cp.start(("z", sign, step, sub), src, dst, {"z": zd[sign]})

    def zgot(sign, step, sub):
        origin = zd[-step] if sign > 0 else zd[step]
        cp.arrived(("z", sign, step, sub), moved_sub(origin, c, sub), {"z": zd[-sign]})

    def to_core(key, origin, src):
        cp.start(("core", key), src, moved_rows(origin, c), {"core": other})

    def split(part, start, count=QUARTER):
        def one(j, carry):
            at = start + 2 * j
            value = land[part, pl.ds(pl.multiple_of(at * TILE, TILE), 2 * TILE)].reshape(2, TILE, TILE)
            top = value.astype(jnp.bfloat16)
            high[pl.ds(part * BLOCKS + at, 2)] = top
            low[pl.ds(part * BLOCKS + at, 2)] = (value - top.astype(jnp.float32)).astype(jnp.bfloat16)
            return carry

        lax.fori_loop(0, count // 2, one, 0)

    lead = {1: 0, -1: 1}

    for s in (1, -1):
        cp.start(("yx", s), lat.at[pl.ds(x * SHARE, SHARE)], rows_of(y, x * SHARE, SHARE), {"y": yd[s]})
    for d in (1, 2, 3):
        for zp in range(NZ):
            cp.start(("e0", d, zp), edges.at[zp, ys[d], :, 0], edge.at[x, zp, y], {"y": ys[d]}, zp >= z)
        cp.start(("m0", d), ids.at[0], meta.at[x, y], {"y": ys[d]})
    for dz in range(NZ):
        for dc in range(NC):
            if dz or dc:
                zs, cc = zd[dz], cs[dc]
                plane = NZ if dz == 0 else z
                cp.start(("e1", dz, dc), edges.at[zs, :, cc, 1], edge.at[x, plane, :, c],
                         {"z": zs, "core": cc}, zs >= z)
                cp.start(("m1", dz, dc), ids.at[1], meta.at[x, NY + z * NC + c],
                         {"z": zs, "core": cc})
    for s in (1, -1):
        zsend(s, 1, lead[s])
    for s in (1, -1):
        h = lead[s]
        cp.start(("yd", s, h), lat.at[pl.ds(direct(h), HALF_DIRECT)], rows_of(y, direct(h), HALF_DIRECT), {"y": yd[s]})
    for s in (1, -1):
        zsend(s, 1, 1 - lead[s])
    to_core(0, z, lat.at[pl.ds(x * QUARTER * TILE, QUARTER * TILE)])

    for copy, when in local[edge_local:]:
        copy.wait()
    split(y, 0, BLOCKS)
    split(*moved_at(z, c))
    def xpart(row, origin, s, half):
        h = half if s > 0 else 1 - half
        return rows_of(row, origin * SHARE + h * HALF_SHARE, HALF_SHARE)

    def xsend(key, row, half):
        for s in (1, -1):
            ref = xpart(row, x, s, half)
            cp.start(("xo", key, s, half), ref, ref, {"x": xd[s]})

    def xgot(key, row, half, relay):
        for s in (1, -1):
            origin = xd[-s]
            ref = xpart(row, origin, s, half)
            cp.arrived(("xo", key, s, half), ref, {"x": origin})
            if relay:
                cp.start(("xr", key, s), ref, ref, {"x": xd[s]})

    def zstep(step, k):
        for s in (1, -1):
            sub = lead[s] if k == 0 else 1 - lead[s]
            zgot(s, step, sub)
            if step < 3 or (step == 3 and k == 0):
                zsend(s, step + 1, sub)

    def zdone(step):
        for s in (1, -1):
            if step < 4 or s == 1:
                origin = zd[-s * step] if step < 4 else zd[4]
                to_core((s, step), origin, moved_rows(origin, c))

    for s in (1, -1):
        row = yd[-s]
        cp.arrived(("yx", s), rows_of(row, x * SHARE, SHARE), {"y": row})
        ref = xpart(row, x, s, 0)
        cp.start(("yxr", s), ref, ref, {"y": yd[s]})
    for s in (1, -1):
        h = 1 - lead[s]
        cp.start(("yd", s, h), lat.at[pl.ds(direct(h), HALF_DIRECT)], rows_of(y, direct(h), HALF_DIRECT), {"y": yd[s]})
    for half in (0, 1):
        for key in (1, -1):
            xsend(key, yd[key], half)
    zstep(1, 0)

    for copy in own_ids:
        copy.wait()
    for copy, when in local[:edge_local]:
        if when is None:
            copy.wait()
        else:
            pl.when(when)(copy.wait)
    for d in (1, 2, 3):
        src = ys[NY - d]
        for zp in range(NZ):
            cp.arrived(("e0", d, zp), edge.at[x, zp, src], {"y": src}, zp >= z)
        cp.arrived(("m0", d), meta.at[x, src], {"y": src})
    for dz in range(NZ):
        for dc in range(NC):
            if dz or dc:
                zr, cr = zd[(NZ - dz) % NZ], cs[dc]
                plane = NZ if dz == 0 else zr
                cp.arrived(("e1", dz, dc), edge.at[x, plane, :, cr], {"z": zr, "core": cr}, zr <= z)
                cp.arrived(("m1", dz, dc), meta.at[x, NY + zr * NC + cr], {"z": zr, "core": cr})
    pieces = {0: pl.ds(0, 5), 1: pl.ds(5, 4)}
    for s in (1, -1):
        cp.start(("xm", s), meta.at[x], meta.at[x], {"x": xd[s]})
    for k in (0, 1):
        for s in (1, -1):
            h = lead[s] if k == 0 else 1 - lead[s]
            cp.start(("xe", s, h), edge.at[x, pieces[h]], edge.at[x, pieces[h]], {"x": xd[s]})

    zstep(1, 1)
    zdone(1)
    for s in (1, -1):
        h, row = lead[s], yd[-s]
        ref = rows_of(row, direct(h), HALF_DIRECT)
        cp.arrived(("yd", s, h), ref, {"y": row})
        cp.start(("ydr", s), ref, ref, {"y": yd[s]})
    zstep(2, 0)
    for s in (1, -1):
        ref = xpart(yd[2], x, s, 0)
        cp.arrived(("yxr", s), ref, {"y": yd[-s]})
    for half in (0, 1):
        xsend(2, yd[2], half)
    for key in (1, -1):
        xgot(key, yd[key], 0, True)
    zstep(2, 1)
    zdone(2)
    for s in (1, -1):
        h, src = lead[s], xd[-s]
        cp.arrived(("xm", s), meta.at[src], {"x": src})
        if s > 0:
            cp.start(("xmr", s), meta.at[src], meta.at[src], {"x": xd[s]})
        cp.arrived(("xe", s, h), edge.at[src, pieces[h]], {"x": src})
        cp.start(("xer", s), edge.at[src, pieces[h]], edge.at[src, pieces[h]], {"x": xd[s]})
    xgot(2, yd[2], 0, True)
    zstep(3, 0)
    zstep(3, 1)
    zdone(3)
    cp.arrived(("core", 0), moved_rows(z, other), {"core": other})
    split(*moved_at(z, other))
    for step in (1, 2):
        for s in (1, -1):
            origin = zd[-s * step]
            cp.arrived(("core", (s, step)), moved_rows(origin, other), {"core": other})
            split(*moved_at(origin, other))
            split(*moved_at(origin, c))
    for s in (1, -1):
        h, row = 1 - lead[s], yd[-s]
        cp.arrived(("yd", s, h), rows_of(row, direct(h), HALF_DIRECT), {"y": row})
        split(row, SPLIT_FROM, BLOCKS - SPLIT_FROM)
    zstep(4, 0)
    zdone(4)
    for s in (1, -1):
        origin = zd[-s * 3]
        cp.arrived(("core", (s, 3)), moved_rows(origin, other), {"core": other})
        split(*moved_at(origin, other))
        split(*moved_at(origin, c))
    split(*moved_at(zd[4], c))
    for s in (1, -1):
        cp.arrived(("ydr", s), rows_of(yd[2], direct(lead[s]), HALF_DIRECT), {"y": yd[-s]})
    split(yd[2], SPLIT_FROM, BLOCKS - SPLIT_FROM)
    for key in (1, -1, 2):
        xgot(key, yd[key], 1, False)
        for s in (1, -1):
            cp.arrived(("xr", key, s), xpart(yd[key], xd[2], s, 0), {"x": xd[-s]})
        split(yd[key], 0, SPLIT_FROM)
    for s in (1, -1):
        h, src = 1 - lead[s], xd[-s]
        if s > 0:
            cp.arrived(("xmr", s), meta.at[xd[2]], {"x": src})
    entries(meta, entry, z, y, c, x)
    for s in (1, -1):
        h, src = 1 - lead[s], xd[-s]
        cp.arrived(("xe", s, h), edge.at[src, pieces[h]], {"x": src})
        cp.arrived(("xer", s), edge.at[xd[2], pieces[1 - h]], {"x": src})
    cp.arrived(("core", (1, 4)), moved_rows(zd[4], other), {"core": other})
    split(*moved_at(zd[4], other))
    cp.drain()


def gather(lat, edges, lefts, rights, kinds):
    hbm = pl.BlockSpec(memory_space=pltpu.HBM)
    vmem = pl.BlockSpec(memory_space=pltpu.VMEM)
    return pl.pallas_call(
        gather_kernel,
        out_shape=(
            jax.ShapeDtypeStruct((ALL + 1, TILE, TILE), jnp.bfloat16),
            jax.ShapeDtypeStruct((ALL + 1, TILE, TILE), jnp.bfloat16),
            jax.ShapeDtypeStruct((NX, PLANES, NY, NC, NBR, TILE), jnp.int32),
            jax.ShapeDtypeStruct((NX, META, 1, TILE), jnp.int32),
        ),
        in_specs=[hbm] * 5,
        out_specs=(vmem,) * 4,
        scratch_shapes=[
            pltpu.VMEM((PARTS, ROWS, TILE), jnp.float32),
            pltpu.VMEM((NX, META, IDS, 1, PEERS), jnp.int32),
            pltpu.VMEM((NC, IDS, 1, PEERS), jnp.int32),
            pltpu.SemaphoreType.DMA((GATHER_SEMS,)),
            pltpu.SemaphoreType.DMA((GATHER_SEMS,)),
            pltpu.SemaphoreType.DMA((16,)),
            pltpu.SemaphoreType.DMA((IDS,)),
        ],
        compiler_params=pltpu.CompilerParams(
            collective_id=0, has_side_effects=True, vmem_limit_bytes=GATHER_VMEM
        ),
        name="gather_rows",
    )(*[pltpu.with_memory_space_constraint(v, pltpu.HBM) for v in (lat, edges, lefts, rights, kinds)])


def product(x, w, dims):
    left = jnp.concatenate(x, axis=1)
    none = jnp.zeros_like(w[0])
    if dims is NT:
        right = jnp.concatenate(
            [jnp.concatenate([w[0], w[0]], axis=1), jnp.concatenate([w[1], none], axis=1)], axis=0
        )
    else:
        right = jnp.concatenate(
            [jnp.concatenate([w[0], w[1]], axis=1), jnp.concatenate([w[0], none], axis=1)], axis=0
        )
    both = lax.dot_general(left, right, dims, preferred_element_type=jnp.float32)
    return both[:, :TILE] + both[:, TILE:]


def residue(left, right, edges, positive):
    scores = product(right, left, NT)
    bit = jnp.where(positive, lax.shift_left(jnp.ones_like(edges), edges & 31), 0)
    word = edges >> 5
    rows = lax.broadcasted_iota(jnp.int32, (NBR, TILE), 0)
    words, tests = [], []
    for w in range(4):
        have = jnp.where(word == w, bit, 0)
        for shift in (4, 2, 1):
            have = have | pltpu.roll(have, shift, 0)
        words += [have] * 4
        tests.append(lax.shift_left(jnp.ones_like(edges), rows + 8 * w))
    hit = (jnp.concatenate(words, axis=0) & jnp.concatenate(tests * 4, axis=0)) != 0
    value = 1.0 / (1.0 + jnp.exp(-scores)) - jnp.where(hit, 1.0, 0.0)
    top = value.astype(jnp.bfloat16)
    return top, (value - top.astype(jnp.float32)).astype(jnp.bfloat16)


def compute_kernel(entry, high, low, edge, grad, slots, held):
    z, y, c, x = position()

    def clear(part):
        grad[part] = jnp.zeros((4, 4, TILE, TILE), jnp.float32)

    def put(places, count):
        for k in range(0, len(places), 8):
            values = [entry[at] for at in places[k : k + 8]]
            for value in values:
                slots[count] = value
                count = count + (1 + (value >> 31))
        return count

    def first(zz, count):
        clear(zz)
        base = zz * (NY * NC) + y * NC
        return put([base + (q * META + yo) * TILE + cc
                    for q in range(NX) for yo in range(NY) for cc in range(NC)], count)

    def second(zz, count):
        clear(jnp.where(zz == z, NZ, zz))
        base = zz * (NC * TILE) + z * (NY * NC) + c
        return put([base + (q * META + NY + cc) * TILE + yo * NC
                    for q in range(NX) for yo in range(NY) for cc in range(NC)], count)

    nothing = TRASH + TRASH * 256
    for k in range(GROUP):
        slots[k] = nothing
    count = lax.fori_loop(z, NZ, first, GROUP)
    count = lax.fori_loop(0, z + 1, second, count)
    for k in range(2 * GROUP):
        slots[count + k] = nothing
    steps = (count - GROUP + GROUP - 1) // GROUP

    def parts(value):
        return value & 255, (value >> 8) & 255, (value >> 16) & 4095, value >> 28

    def block(at):
        return high[at], low[at]

    def add(at, value):
        p, s, j = at // 16, lax.rem(at // 4, 4), lax.rem(at, 4)
        grad[p, s, j] += value

    def work(step, carry):
        done = []
        for k in range(GROUP):
            li, ri, _, _ = parts(slots[step * GROUP + k])
            top, rest = held[k, 0], held[k, 1]
            left, right = block(li), block(ri)
            gr = product((top, rest), left, NN)
            gl = product((top.T, rest.T), right, NN)
            done.append((li, ri, gl, gr))
            li, ri, where, positive = parts(slots[(step + 1) * GROUP + k])
            top, rest = residue(block(li), block(ri), edge[where], positive > 0)
            held[k, 0] = top
            held[k, 1] = rest
        for li, ri, gl, gr in done:
            add(li, gl)
            add(ri, gr)
        return carry

    lax.fori_loop(0, steps + 1, work, 0)


def compute(entry, high, low, edges):
    smem = pl.BlockSpec(memory_space=pltpu.SMEM)
    vmem = pl.BlockSpec(memory_space=pltpu.VMEM)
    return pl.pallas_call(
        compute_kernel,
        out_shape=jax.ShapeDtypeStruct((PARTS + 1, 4, 4, TILE, TILE), jnp.float32),
        in_specs=[smem, vmem, vmem, vmem],
        out_specs=vmem,
        scratch_shapes=[
            pltpu.SMEM((NX * CAND + 3 * GROUP,), jnp.int32),
            pltpu.VMEM((GROUP, 2, TILE, TILE), jnp.bfloat16),
        ],
        compiler_params=pltpu.CompilerParams(vmem_limit_bytes=SLOT_VMEM),
        name="slot_gradients",
    )(entry.reshape(NX * META * TILE), high, low,
      edges.reshape(NX * CAND, NBR, TILE))


class Ring:
    def __init__(self, cp, name, axis, at, part, far, near, made):
        self.cp, self.name, self.axis, self.part = cp, name, axis, part
        self.far, self.near, self.made = far, near, made
        self.at = {d: step_of(at, d, 4) for d in (-1, 0, 1, 2)}

    def to(self, sign):
        return {self.axis: self.at[sign]}

    def begin(self):
        for k, s in enumerate((1, -1)):
            self.cp.start((self.name, "far", s), self.part(self.at[2], k), self.far.at[k], self.to(s))
        for k, s in enumerate((1, -1)):
            h = 1 - k
            self.cp.start((self.name, "near", s, h), self.part(self.at[s], h), self.near.at[k, h], self.to(s))

    def pass_on(self):
        for k, s in enumerate((1, -1)):
            self.cp.arrived((self.name, "far", s), self.far.at[k], self.to(-s))
            self.made[k] = self.part(self.at[s], k)[...] + self.far[k]
            self.cp.start((self.name, "near", s, k), self.made.at[k], self.near.at[k, k], self.to(s))

    def total(self, half):
        for k, s in enumerate((1, -1)):
            self.cp.arrived((self.name, "near", s, half), self.near.at[k, half], self.to(-s))
        return self.part(self.at[0], half)[...] + self.near[0, half] + self.near[1, half]


REDUCE_SEMS = 64


def reduce_kernel(grad, out, a_far, a_near, a_made, a_sum, b_far, b_near, b_made, b_sum,
                  c_far, c_near, c_made, d_far, d_near, d_made,
                  partner, z_in, z_out, send_sems, recv_sems):
    z, y, c, x = position()
    other = 1 - c
    zd = {d: step_of(z, d, NZ) for d in range(-4, 5)}
    cp = Copies(send_sems, recv_sems)

    barrier = pltpu.get_barrier_semaphore()
    peers = [{"y": step_of(y, 1, NY)}, {"y": step_of(y, -1, NY)}, {"x": step_of(x, 1, NX)},
             {"x": step_of(x, -1, NX)}, {"z": zd[1]}, {"z": zd[-1]}, {"core": other}]
    for peer in peers:
        pl.semaphore_signal(barrier, inc=1, device_id=peer, device_id_type=MESH)
    pl.semaphore_wait(barrier, len(peers))

    a = Ring(cp, "a", "y", y, lambda dest, h: grad.at[dest, pl.ds(2 * h, 2), pl.ds(0, 2)], a_far, a_near, a_made)
    b = Ring(cp, "b", "x", x, lambda dest, h: grad.at[pl.ds(2 * h, 2), dest, pl.ds(2, 2)], b_far, b_near, b_made)

    def moved_at(d, cc):
        return PARTS // 2 + zd[d] // 2, lax.rem(zd[d], 2) * NC + cc

    order = [4, 3, -3, 2, -2, 1, -1, 0]
    for d in order:
        cp.start(("p", d), grad.at[moved_at(d, other)], partner.at[zd[d]], {"core": other})
    a.begin()
    b.begin()

    slot = {}
    for s in (1, -1):
        for d in (4, 3, 2, 1):
            for sub in (0, 1):
                if d < 4 or sub == (0 if s > 0 else 1):
                    slot[s, d, sub] = len(slot)

    def mine(d, sub):
        p, s = moved_at(d, c)
        return grad[p, s, pl.ds(2 * sub, 2)] + partner[zd[d], pl.ds(2 * sub, 2)]

    def zsend(s, d, sub, received):
        at = slot[s, d, sub]
        value = mine(s * d if d < 4 else 4, sub)
        if received:
            value = value + z_in[slot[s, d + 1, sub]]
        z_out[at] = value
        cp.start(("z", s, d, sub), z_out.at[at], z_in.at[at], {"z": zd[s]})

    def zgot(s, d, sub):
        cp.arrived(("z", s, d, sub), z_in.at[slot[s, d, sub]], {"z": zd[-s]})

    def from_core(d):
        cp.arrived(("p", d), partner.at[zd[d]], {"core": other})

    lead = {1: 0, -1: 1}
    from_core(4)
    for s in (1, -1):
        zsend(s, 4, lead[s], False)
    for s in (1, -1):
        from_core(3 * s)
        zsend(s, 3, 1 - lead[s], False)
    from_core(2)
    from_core(-2)
    for s in (1, -1):
        zgot(s, 4, lead[s])
        zsend(s, 3, lead[s], True)
    a.pass_on()
    b.pass_on()
    for s in (1, -1):
        zgot(s, 3, 1 - lead[s])
        zsend(s, 2, 1 - lead[s], True)
    for s in (1, -1):
        zgot(s, 3, lead[s])
        zsend(s, 2, lead[s], True)
    from_core(1)
    from_core(-1)
    from_core(0)
    for s in (1, -1):
        zgot(s, 2, 1 - lead[s])
        zsend(s, 1, 1 - lead[s], True)
    for h in (1, 0):
        a_sum[pl.ds(2 * h, 2)] = a.total(h)
        b_sum[pl.ds(2 * h, 2)] = b.total(h)
    second_a = Ring(cp, "c", "x", x, lambda dest, h: a_sum.at[dest, pl.ds(h, 1)], c_far, c_near, c_made)
    second_b = Ring(cp, "d", "y", y, lambda dest, h: b_sum.at[dest, pl.ds(h, 1)], d_far, d_near, d_made)
    second_a.begin()
    second_b.begin()
    for s in (1, -1):
        zgot(s, 2, lead[s])
        zsend(s, 1, lead[s], True)
    second_a.pass_on()
    second_b.pass_on()
    for sub in (0, 1):
        zgot(1, 1, sub)
        zgot(-1, 1, sub)
        value = mine(0, sub) + z_in[slot[1, 1, sub]] + z_in[slot[-1, 1, sub]]
        ring = second_a if sub == 0 else second_b
        for h in (0, 1):
            out[2 * sub + h] = value[h] + ring.total(h)[0]
    cp.drain()


def reduce(grad):
    vmem = pl.BlockSpec(memory_space=pltpu.VMEM)
    tile = (TILE, TILE)
    f32 = jnp.float32

    def ring(blocks):
        return [pltpu.VMEM((2,) + blocks + tile, f32), pltpu.VMEM((2, 2) + blocks + tile, f32),
                pltpu.VMEM((2,) + blocks + tile, f32)]

    first, second = (2, 2), (1,)
    return pl.pallas_call(
        reduce_kernel,
        out_shape=jax.ShapeDtypeStruct((QUARTER,) + tile, f32),
        in_specs=[vmem],
        out_specs=vmem,
        scratch_shapes=ring(first) + [pltpu.VMEM((4, 2) + tile, f32)]
        + ring(first) + [pltpu.VMEM((4, 2) + tile, f32)]
        + ring(second) + ring(second)
        + [
            pltpu.VMEM((NZ, QUARTER) + tile, f32),
            pltpu.VMEM((14, 2) + tile, f32),
            pltpu.VMEM((14, 2) + tile, f32),
            pltpu.SemaphoreType.DMA((REDUCE_SEMS,)),
            pltpu.SemaphoreType.DMA((REDUCE_SEMS,)),
        ],
        compiler_params=pltpu.CompilerParams(
            collective_id=1, has_side_effects=True, vmem_limit_bytes=REDUCE_VMEM
        ),
        name="reduce_rows",
    )(grad)


def body(latent, left_block, right_block, slot_kind, edge_cols):
    edges = edge_cols.reshape(NZ, NY, NC, 2, NBR, TILE)
    ids = [v[0, 0].T.reshape(2, 1, PEERS) for v in (left_block, right_block, slot_kind)]
    high, low, edge, entry = gather(latent, edges, *ids)
    grad = compute(entry, high, low, edge)
    out = reduce(grad)
    return out.reshape(QUARTER * TILE, TILE)


def solution(mesh):
    fine = Mesh(mesh.devices.reshape(NZ, NY, NC, NX), ("z", "y", "core", "x"))
    rows = ("z", "y", "core")
    return jax.shard_map(
        body,
        mesh=fine,
        in_specs=(
            P(rows, None),
            P(rows, "x", None, None),
            P(rows, "x", None, None),
            P(rows, "x", None, None),
            P(rows, "x", None, None, None, None),
        ),
        out_specs=P(("z", "y", "core", "x"), None),
        check_vma=False,
    )
```

```python
import functools

import jax
import jax.numpy as jnp
from jax import lax
from jax.experimental import pallas as pl
from jax.experimental.pallas import tpu as pltpu
from jax.sharding import Mesh
from jax.sharding import PartitionSpec as P

NZ, NY, NC, NX = 8, 4, 2, 4
BLOCKS = 16
QUARTER = 4
TILE = 128
NBR = 8
OWN = NY * BLOCKS
MOVED = NZ * NC * QUARTER
ALL = OWN + MOVED
PLANES = NZ + 1
CAND = PLANES * NY * NC
META = NY + NZ * NC
PARTS = ALL // 16
TRASH = ALL
GROUP = 12
MESH = pl.DeviceIdType.MESH
GATHER_VMEM, SLOT_VMEM, REDUCE_VMEM = 32 << 20, 24 << 20, 28 << 20

NT = (((1,), (1,)), ((), ()))
NN = (((1,), (0,)), ((), ()))


def position():
    return tuple(lax.axis_index(name) for name in ("z", "y", "core", "x"))


def step_of(value, by, size):
    return lax.rem(value + (by + size), size)


class Copies:
    def __init__(self, send_sems, recv_sems):
        self.send_sems, self.recv_sems = send_sems, recv_sems
        self.index = {}
        self.sent = []

    def sems(self, name):
        at = self.index.setdefault(name, len(self.index))
        return self.send_sems.at[at], self.recv_sems.at[at]

    def make(self, name, src, dst, device):
        send, recv = self.sems(name)
        return pltpu.make_async_remote_copy(
            src_ref=src, dst_ref=dst, send_sem=send, recv_sem=recv,
            device_id=device, device_id_type=MESH,
        )

    def start(self, name, src, dst, device, when=None):
        copy = self.make(name, src, dst, device)
        self.sent.append((copy, when))
        if when is None:
            copy.start()
        else:
            pl.when(when)(copy.start)

    def arrived(self, name, landed, device, when=None):
        copy = self.make(name, landed, landed, device)
        if when is None:
            copy.wait_recv()
        else:
            pl.when(when)(copy.wait_recv)

    def drain(self):
        for copy, when in self.sent:
            if when is None:
                copy.wait_send()
            else:
                pl.when(when)(copy.wait_send)


GATHER_SEMS = 128
IDS = 3
ROWS = BLOCKS * TILE
SHARE = 192
HALF_SHARE = SHARE // 2
DIRECT = NX * SHARE
HALF_DIRECT = (ROWS - DIRECT) // 2
SPLIT_FROM = DIRECT // TILE
PEERS = NZ * NY * NC


def entries(meta, entry, z, y, c, x):
    step = NY * NC

    def one(q, carry):
        def write(rows, own_ids, moved_ids, kinds, yo, zc, plane, flip, live):
            cc = zc & 1
            own_at = yo * BLOCKS + own_ids
            moved_at = OWN + zc * QUARTER + moved_ids - x * QUARTER
            left, right = (moved_at, own_at) if flip else (own_at, moved_at)
            where = (q * PLANES + plane) * step + yo * NC + cc
            value = left + right * 256 + where * 65536 + jnp.where(kinds == 2, 1 << 28, 0)
            take = live & ((moved_ids >> 2) == x)
            entry[q, rows, :, pl.ds(0, PEERS)] = jnp.where(take, value, -1)

        shape = (NY, 1, PEERS)
        s = lax.broadcasted_iota(jnp.int32, shape, 2)
        yo = lax.broadcasted_iota(jnp.int32, shape, 0)
        rows = pl.ds(0, NY)
        lb, rb, kind = [meta[q, rows, v] for v in range(IDS)]
        live = s >= z * step + yo * NC + c
        write(rows, lb, rb, kind, yo, (s >> 3) * NC + (s & 1), s >> 3, False, live)

        shape = (NZ * NC, 1, PEERS)
        s = lax.broadcasted_iota(jnp.int32, shape, 2)
        zc = lax.broadcasted_iota(jnp.int32, shape, 0)
        rows = pl.ds(NY, NZ * NC)
        lb, rb, kind = [meta[q, rows, v] for v in range(IDS)]
        zz = zc >> 1
        live = zz * step + y * NC + (zc & 1) <= s
        write(rows, rb, lb, kind, (s >> 1) & 3, zc, jnp.where(zz == z, NZ, zz), True, live)
        return carry

    lax.fori_loop(0, NX, one, 0)


def gather_kernel(lat, edges, lefts, rights, kinds, high, low, edge, entry, land, meta, ids,
                  send_sems, recv_sems, local_sems, id_sems):
    z, y, c, x = position()
    other = 1 - c
    ys = [step_of(y, d, NY) for d in range(NY)]
    yd = {1: ys[1], -1: ys[3], 2: ys[2]}
    xd = {1: step_of(x, 1, NX), -1: step_of(x, -1, NX), 2: step_of(x, 2, NX)}
    zd = {d: step_of(z, d, NZ) for d in range(-4, NZ)}
    cp = Copies(send_sems, recv_sems)
    cs = [c, other]

    barrier = pltpu.get_barrier_semaphore()
    peers = [{"y": ys[d]} for d in (1, 2, 3)] + [{"x": xd[1]}, {"x": xd[-1]}]
    peers += [{"z": zd[dz], "core": cs[dc]} for dz in range(NZ) for dc in range(NC) if dz or dc]
    for peer in peers:
        pl.semaphore_signal(barrier, inc=1, device_id=peer, device_id_type=MESH)

    local = []

    def here(src, dst, when=None):
        copy = pltpu.make_async_copy(src, dst, local_sems.at[len(local)])
        local.append((copy, when))
        if when is None:
            copy.start()
        else:
            pl.when(when)(copy.start)

    def moved_at(zz, cc):
        return PARTS // 2 + zz // 2, (lax.rem(zz, 2) * NC + cc) * QUARTER

    def rows_of(part, start, count):
        return land.at[part, pl.ds(start, count)]

    def moved_rows(zz, cc):
        p, block = moved_at(zz, cc)
        return rows_of(p, block * TILE, QUARTER * TILE)

    def direct(half):
        return DIRECT + half * HALF_DIRECT

    raw = [pltpu.make_async_copy(ref, ids.at[:, v], id_sems.at[v])
           for v, ref in enumerate((lefts, rights, kinds))]
    for copy in raw:
        copy.start()
    for zp in range(NZ):
        here(edges.at[zp, y, :, 0], edge.at[x, zp, y], zp >= z)
    here(edges.at[z, :, c, 1], edge.at[x, NZ, :, c])
    edge_local = len(local)
    here(lat, land.at[y])
    here(lat.at[pl.ds(x * QUARTER * TILE, QUARTER * TILE)], moved_rows(z, c))

    for copy in raw:
        copy.wait()
    own_ids = [pltpu.make_async_copy(ids.at[0], meta.at[x, y], id_sems.at[0]),
               pltpu.make_async_copy(ids.at[1], meta.at[x, NY + z * NC + c], id_sems.at[1])]
    for copy in own_ids:
        copy.start()
    pl.semaphore_wait(barrier, len(peers))

    def moved_sub(zz, cc, sub):
        p, block = moved_at(zz, cc)
        return rows_of(p, (block + 2 * sub) * TILE, 2 * TILE)

    def zsend(sign, step, sub):
        origin = zd[-(step - 1)] if sign > 0 else zd[step - 1]
        dst = moved_sub(origin, c, sub)
        src = lat.at[pl.ds((x * QUARTER + 2 * sub) * TILE, 2 * TILE)] if step == 1 else dst
        cp.start(("z", sign, step, sub), src, dst, {"z": zd[sign]})

    def zgot(sign, step, sub):
        origin = zd[-step] if sign > 0 else zd[step]
        cp.arrived(("z", sign, step, sub), moved_sub(origin, c, sub), {"z": zd[-sign]})

    def to_core(key, origin, src):
        cp.start(("core", key), src, moved_rows(origin, c), {"core": other})

    def split(part, start, count=QUARTER):
        def one(j, carry):
            at = start + 2 * j
            value = land[part, pl.ds(pl.multiple_of(at * TILE, TILE), 2 * TILE)].reshape(2, TILE, TILE)
            top = value.astype(jnp.bfloat16)
            high[pl.ds(part * BLOCKS + at, 2)] = top
            low[pl.ds(part * BLOCKS + at, 2)] = (value - top.astype(jnp.float32)).astype(jnp.bfloat16)
            return carry

        lax.fori_loop(0, count // 2, one, 0)

    lead = {1: 0, -1: 1}

    for s in (1, -1):
        cp.start(("yx", s), lat.at[pl.ds(x * SHARE, SHARE)], rows_of(y, x * SHARE, SHARE), {"y": yd[s]})
    for d in (1, 2, 3):
        for zp in range(NZ):
            cp.start(("e0", d, zp), edges.at[zp, ys[d], :, 0], edge.at[x, zp, y], {"y": ys[d]}, zp >= z)
        cp.start(("m0", d), ids.at[0], meta.at[x, y], {"y": ys[d]})
    for dz in range(NZ):
        for dc in range(NC):
            if dz or dc:
                zs, cc = zd[dz], cs[dc]
                plane = NZ if dz == 0 else z
                cp.start(("e1", dz, dc), edges.at[zs, :, cc, 1], edge.at[x, plane, :, c],
                         {"z": zs, "core": cc}, zs >= z)
                cp.start(("m1", dz, dc), ids.at[1], meta.at[x, NY + z * NC + c],
                         {"z": zs, "core": cc})
    for s in (1, -1):
        zsend(s, 1, lead[s])
    for s in (1, -1):
        h = lead[s]
        cp.start(("yd", s, h), lat.at[pl.ds(direct(h), HALF_DIRECT)], rows_of(y, direct(h), HALF_DIRECT), {"y": yd[s]})
    for s in (1, -1):
        zsend(s, 1, 1 - lead[s])
    to_core(0, z, lat.at[pl.ds(x * QUARTER * TILE, QUARTER * TILE)])

    for copy, when in local[edge_local:]:
        copy.wait()
    split(y, 0, BLOCKS)
    split(*moved_at(z, c))
    def xpart(row, origin, s, half):
        h = half if s > 0 else 1 - half
        return rows_of(row, origin * SHARE + h * HALF_SHARE, HALF_SHARE)

    def xsend(key, row, half):
        for s in (1, -1):
            ref = xpart(row, x, s, half)
            cp.start(("xo", key, s, half), ref, ref, {"x": xd[s]})

    def xgot(key, row, half, relay):
        for s in (1, -1):
            origin = xd[-s]
            ref = xpart(row, origin, s, half)
            cp.arrived(("xo", key, s, half), ref, {"x": origin})
            if relay:
                cp.start(("xr", key, s), ref, ref, {"x": xd[s]})

    def zstep(step, k):
        for s in (1, -1):
            sub = lead[s] if k == 0 else 1 - lead[s]
            zgot(s, step, sub)
            if step < 3 or (step == 3 and k == 0):
                zsend(s, step + 1, sub)

    def zdone(step):
        for s in (1, -1):
            if step < 4 or s == 1:
                origin = zd[-s * step] if step < 4 else zd[4]
                to_core((s, step), origin, moved_rows(origin, c))

    for s in (1, -1):
        row = yd[-s]
        cp.arrived(("yx", s), rows_of(row, x * SHARE, SHARE), {"y": row})
        ref = xpart(row, x, s, 0)
        cp.start(("yxr", s), ref, ref, {"y": yd[s]})
    for s in (1, -1):
        h = 1 - lead[s]
        cp.start(("yd", s, h), lat.at[pl.ds(direct(h), HALF_DIRECT)], rows_of(y, direct(h), HALF_DIRECT), {"y": yd[s]})
    for half in (0, 1):
        for key in (1, -1):
            xsend(key, yd[key], half)
    zstep(1, 0)

    for copy in own_ids:
        copy.wait()
    for copy, when in local[:edge_local]:
        if when is None:
            copy.wait()
        else:
            pl.when(when)(copy.wait)
    for d in (1, 2, 3):
        src = ys[NY - d]
        for zp in range(NZ):
            cp.arrived(("e0", d, zp), edge.at[x, zp, src], {"y": src}, zp >= z)
        cp.arrived(("m0", d), meta.at[x, src], {"y": src})
    for dz in range(NZ):
        for dc in range(NC):
            if dz or dc:
                zr, cr = zd[(NZ - dz) % NZ], cs[dc]
                plane = NZ if dz == 0 else zr
                cp.arrived(("e1", dz, dc), edge.at[x, plane, :, cr], {"z": zr, "core": cr}, zr <= z)
                cp.arrived(("m1", dz, dc), meta.at[x, NY + zr * NC + cr], {"z": zr, "core": cr})
    pieces = {0: pl.ds(0, 5), 1: pl.ds(5, 4)}
    for s in (1, -1):
        cp.start(("xm", s), meta.at[x], meta.at[x], {"x": xd[s]})
    for k in (0, 1):
        for s in (1, -1):
            h = lead[s] if k == 0 else 1 - lead[s]
            cp.start(("xe", s, h), edge.at[x, pieces[h]], edge.at[x, pieces[h]], {"x": xd[s]})

    zstep(1, 1)
    zdone(1)
    for s in (1, -1):
        h, row = lead[s], yd[-s]
        ref = rows_of(row, direct(h), HALF_DIRECT)
        cp.arrived(("yd", s, h), ref, {"y": row})
        cp.start(("ydr", s), ref, ref, {"y": yd[s]})
    zstep(2, 0)
    for s in (1, -1):
        ref = xpart(yd[2], x, s, 0)
        cp.arrived(("yxr", s), ref, {"y": yd[-s]})
    for half in (0, 1):
        xsend(2, yd[2], half)
    for key in (1, -1):
        xgot(key, yd[key], 0, True)
    zstep(2, 1)
    zdone(2)
    for s in (1, -1):
        h, src = lead[s], xd[-s]
        cp.arrived(("xm", s), meta.at[src], {"x": src})
        if s > 0:
            cp.start(("xmr", s), meta.at[src], meta.at[src], {"x": xd[s]})
        cp.arrived(("xe", s, h), edge.at[src, pieces[h]], {"x": src})
        cp.start(("xer", s), edge.at[src, pieces[h]], edge.at[src, pieces[h]], {"x": xd[s]})
    xgot(2, yd[2], 0, True)
    zstep(3, 0)
    zstep(3, 1)
    zdone(3)
    cp.arrived(("core", 0), moved_rows(z, other), {"core": other})
    split(*moved_at(z, other))
    for step in (1, 2):
        for s in (1, -1):
            origin = zd[-s * step]
            cp.arrived(("core", (s, step)), moved_rows(origin, other), {"core": other})
            split(*moved_at(origin, other))
            split(*moved_at(origin, c))
    for s in (1, -1):
        h, row = 1 - lead[s], yd[-s]
        cp.arrived(("yd", s, h), rows_of(row, direct(h), HALF_DIRECT), {"y": row})
        split(row, SPLIT_FROM, BLOCKS - SPLIT_FROM)
    zstep(4, 0)
    zdone(4)
    for s in (1, -1):
        origin = zd[-s * 3]
        cp.arrived(("core", (s, 3)), moved_rows(origin, other), {"core": other})
        split(*moved_at(origin, other))
        split(*moved_at(origin, c))
    split(*moved_at(zd[4], c))
    for s in (1, -1):
        cp.arrived(("ydr", s), rows_of(yd[2], direct(lead[s]), HALF_DIRECT), {"y": yd[-s]})
    split(yd[2], SPLIT_FROM, BLOCKS - SPLIT_FROM)
    for key in (1, -1, 2):
        xgot(key, yd[key], 1, False)
        for s in (1, -1):
            cp.arrived(("xr", key, s), xpart(yd[key], xd[2], s, 0), {"x": xd[-s]})
        split(yd[key], 0, SPLIT_FROM)
    for s in (1, -1):
        h, src = 1 - lead[s], xd[-s]
        if s > 0:
            cp.arrived(("xmr", s), meta.at[xd[2]], {"x": src})
    entries(meta, entry, z, y, c, x)
    for s in (1, -1):
        h, src = 1 - lead[s], xd[-s]
        cp.arrived(("xe", s, h), edge.at[src, pieces[h]], {"x": src})
        cp.arrived(("xer", s), edge.at[xd[2], pieces[1 - h]], {"x": src})
    cp.arrived(("core", (1, 4)), moved_rows(zd[4], other), {"core": other})
    split(*moved_at(zd[4], other))
    cp.drain()


def gather(lat, edges, lefts, rights, kinds):
    hbm = pl.BlockSpec(memory_space=pltpu.HBM)
    vmem = pl.BlockSpec(memory_space=pltpu.VMEM)
    return pl.pallas_call(
        gather_kernel,
        out_shape=(
            jax.ShapeDtypeStruct((ALL + 1, TILE, TILE), jnp.bfloat16),
            jax.ShapeDtypeStruct((ALL + 1, TILE, TILE), jnp.bfloat16),
            jax.ShapeDtypeStruct((NX, PLANES, NY, NC, NBR, TILE), jnp.int32),
            jax.ShapeDtypeStruct((NX, META, 1, TILE), jnp.int32),
        ),
        in_specs=[hbm] * 5,
        out_specs=(vmem,) * 4,
        scratch_shapes=[
            pltpu.VMEM((PARTS, ROWS, TILE), jnp.float32),
            pltpu.VMEM((NX, META, IDS, 1, PEERS), jnp.int32),
            pltpu.VMEM((NC, IDS, 1, PEERS), jnp.int32),
            pltpu.SemaphoreType.DMA((GATHER_SEMS,)),
            pltpu.SemaphoreType.DMA((GATHER_SEMS,)),
            pltpu.SemaphoreType.DMA((16,)),
            pltpu.SemaphoreType.DMA((IDS,)),
        ],
        compiler_params=pltpu.CompilerParams(
            collective_id=0, has_side_effects=True, vmem_limit_bytes=GATHER_VMEM
        ),
        name="gather_rows",
    )(*[pltpu.with_memory_space_constraint(v, pltpu.HBM) for v in (lat, edges, lefts, rights, kinds)])


def product(x, w, dims):
    left = jnp.concatenate(x, axis=1)
    none = jnp.zeros_like(w[0])
    if dims is NT:
        right = jnp.concatenate(
            [jnp.concatenate([w[0], w[0]], axis=1), jnp.concatenate([w[1], none], axis=1)], axis=0
        )
    else:
        right = jnp.concatenate(
            [jnp.concatenate([w[0], w[1]], axis=1), jnp.concatenate([w[0], none], axis=1)], axis=0
        )
    both = lax.dot_general(left, right, dims, preferred_element_type=jnp.float32)
    return both[:, :TILE] + both[:, TILE:]


def residue(left, right, edges, positive):
    scores = product(right, left, NT)
    bit = jnp.where(positive, lax.shift_left(jnp.ones_like(edges), edges & 31), 0)
    word = edges >> 5
    rows = lax.broadcasted_iota(jnp.int32, (NBR, TILE), 0)
    words, tests = [], []
    for w in range(4):
        have = jnp.where(word == w, bit, 0)
        for shift in (4, 2, 1):
            have = have | pltpu.roll(have, shift, 0)
        words += [have] * 4
        tests.append(lax.shift_left(jnp.ones_like(edges), rows + 8 * w))
    hit = (jnp.concatenate(words, axis=0) & jnp.concatenate(tests * 4, axis=0)) != 0
    value = 1.0 / (1.0 + jnp.exp(-scores)) - jnp.where(hit, 1.0, 0.0)
    top = value.astype(jnp.bfloat16)
    return top, (value - top.astype(jnp.float32)).astype(jnp.bfloat16)


def compute_kernel(entry, high, low, edge, grad, slots, held):
    z, y, c, x = position()

    def clear(part):
        grad[part] = jnp.zeros((4, 4, TILE, TILE), jnp.float32)

    def put(places, count):
        for k in range(0, len(places), 8):
            values = [entry[at] for at in places[k : k + 8]]
            for value in values:
                slots[count] = value
                count = count + (1 + (value >> 31))
        return count

    def first(zz, count):
        clear(zz)
        base = zz * (NY * NC) + y * NC
        return put([base + (q * META + yo) * TILE + cc
                    for q in range(NX) for yo in range(NY) for cc in range(NC)], count)

    def second(zz, count):
        clear(jnp.where(zz == z, NZ, zz))
        base = zz * (NC * TILE) + z * (NY * NC) + c
        return put([base + (q * META + NY + cc) * TILE + yo * NC
                    for q in range(NX) for yo in range(NY) for cc in range(NC)], count)

    nothing = TRASH + TRASH * 256
    count = lax.fori_loop(z, NZ, first, 0)
    count = lax.fori_loop(0, z + 1, second, count)
    for k in range(GROUP):
        slots[count + k] = nothing
    steps = jnp.maximum((count + GROUP - 1) // GROUP, 1)

    def parts(value):
        return value & 255, (value >> 8) & 255, (value >> 16) & 4095, value >> 28

    def block(at):
        return high[at], low[at]

    def add(at, value):
        p, s, j = at // 16, lax.rem(at // 4, 4), lax.rem(at, 4)
        grad[p, s, j] += value

    def residues(step, k):
        li, ri, where, positive = parts(slots[step * GROUP + k])
        held[k, 0], held[k, 1] = residue(block(li), block(ri), edge[where], positive > 0)

    def gradients(step, k, kept):
        li, ri, _, _ = parts(slots[step * GROUP + k])
        left, right = block(li), block(ri)
        gr = product(kept, left, NN)
        gl = product((kept[0].T, kept[1].T), right, NN)
        return li, ri, gl, gr

    def flush(done):
        for li, ri, gl, gr in done:
            add(li, gl)
            add(ri, gr)

    def work(step, carry):
        done = []
        for k in range(GROUP):
            kept = held[k, 0], held[k, 1]
            residues(step, k)
            done.append(gradients(step - 1, k, kept))
        flush(done)
        return carry

    for k in range(GROUP):
        residues(0, k)
    lax.fori_loop(1, steps, work, 0)
    flush([gradients(steps - 1, k, (held[k, 0], held[k, 1])) for k in range(GROUP)])


def compute(entry, high, low, edges):
    smem = pl.BlockSpec(memory_space=pltpu.SMEM)
    vmem = pl.BlockSpec(memory_space=pltpu.VMEM)
    return pl.pallas_call(
        compute_kernel,
        out_shape=jax.ShapeDtypeStruct((PARTS + 1, 4, 4, TILE, TILE), jnp.float32),
        in_specs=[smem, vmem, vmem, vmem],
        out_specs=vmem,
        scratch_shapes=[
            pltpu.SMEM((NX * CAND + 3 * GROUP,), jnp.int32),
            pltpu.VMEM((GROUP, 2, TILE, TILE), jnp.bfloat16),
        ],
        compiler_params=pltpu.CompilerParams(vmem_limit_bytes=SLOT_VMEM),
        name="slot_gradients",
    )(entry.reshape(NX * META * TILE), high, low,
      edges.reshape(NX * CAND, NBR, TILE))


class Ring:
    def __init__(self, cp, name, axis, at, part, far, near, made):
        self.cp, self.name, self.axis, self.part = cp, name, axis, part
        self.far, self.near, self.made = far, near, made
        self.at = {d: step_of(at, d, 4) for d in (-1, 0, 1, 2)}

    def to(self, sign):
        return {self.axis: self.at[sign]}

    def begin(self):
        for k, s in enumerate((1, -1)):
            self.cp.start((self.name, "far", s), self.part(self.at[2], k), self.far.at[k], self.to(s))
        for k, s in enumerate((1, -1)):
            h = 1 - k
            self.cp.start((self.name, "near", s, h), self.part(self.at[s], h), self.near.at[k, h], self.to(s))

    def pass_on(self):
        for k, s in enumerate((1, -1)):
            self.cp.arrived((self.name, "far", s), self.far.at[k], self.to(-s))
            self.made[k] = self.part(self.at[s], k)[...] + self.far[k]
            self.cp.start((self.name, "near", s, k), self.made.at[k], self.near.at[k, k], self.to(s))

    def total(self, half):
        for k, s in enumerate((1, -1)):
            self.cp.arrived((self.name, "near", s, half), self.near.at[k, half], self.to(-s))
        return self.part(self.at[0], half)[...] + self.near[0, half] + self.near[1, half]


REDUCE_SEMS = 64


def reduce_kernel(grad, out, a_far, a_near, a_made, a_sum, b_far, b_near, b_made, b_sum,
                  c_far, c_near, c_made, d_far, d_near, d_made,
                  partner, z_in, z_out, send_sems, recv_sems):
    z, y, c, x = position()
    other = 1 - c
    zd = {d: step_of(z, d, NZ) for d in range(-4, 5)}
    cp = Copies(send_sems, recv_sems)

    barrier = pltpu.get_barrier_semaphore()
    peers = [{"y": step_of(y, 1, NY)}, {"y": step_of(y, -1, NY)}, {"x": step_of(x, 1, NX)},
             {"x": step_of(x, -1, NX)}, {"z": zd[1]}, {"z": zd[-1]}, {"core": other}]
    for peer in peers:
        pl.semaphore_signal(barrier, inc=1, device_id=peer, device_id_type=MESH)
    pl.semaphore_wait(barrier, len(peers))

    a = Ring(cp, "a", "y", y, lambda dest, h: grad.at[dest, pl.ds(2 * h, 2), pl.ds(0, 2)], a_far, a_near, a_made)
    b = Ring(cp, "b", "x", x, lambda dest, h: grad.at[pl.ds(2 * h, 2), dest, pl.ds(2, 2)], b_far, b_near, b_made)

    def moved_at(d, cc):
        return PARTS // 2 + zd[d] // 2, lax.rem(zd[d], 2) * NC + cc

    order = [4, 3, -3, 2, -2, 1, -1, 0]
    for d in order:
        cp.start(("p", d), grad.at[moved_at(d, other)], partner.at[zd[d]], {"core": other})
    a.begin()
    b.begin()

    slot = {}
    for s in (1, -1):
        for d in (4, 3, 2, 1):
            for sub in (0, 1):
                if d < 4 or sub == (0 if s > 0 else 1):
                    slot[s, d, sub] = len(slot)

    def mine(d, sub):
        p, s = moved_at(d, c)
        return grad[p, s, pl.ds(2 * sub, 2)] + partner[zd[d], pl.ds(2 * sub, 2)]

    def zsend(s, d, sub, received):
        at = slot[s, d, sub]
        value = mine(s * d if d < 4 else 4, sub)
        if received:
            value = value + z_in[slot[s, d + 1, sub]]
        z_out[at] = value
        cp.start(("z", s, d, sub), z_out.at[at], z_in.at[at], {"z": zd[s]})

    def zgot(s, d, sub):
        cp.arrived(("z", s, d, sub), z_in.at[slot[s, d, sub]], {"z": zd[-s]})

    def from_core(d):
        cp.arrived(("p", d), partner.at[zd[d]], {"core": other})

    lead = {1: 0, -1: 1}
    from_core(4)
    for s in (1, -1):
        zsend(s, 4, lead[s], False)
    for s in (1, -1):
        from_core(3 * s)
        zsend(s, 3, 1 - lead[s], False)
    from_core(2)
    from_core(-2)
    for s in (1, -1):
        zgot(s, 4, lead[s])
        zsend(s, 3, lead[s], True)
    a.pass_on()
    b.pass_on()
    for s in (1, -1):
        zgot(s, 3, 1 - lead[s])
        zsend(s, 2, 1 - lead[s], True)
    for s in (1, -1):
        zgot(s, 3, lead[s])
        zsend(s, 2, lead[s], True)
    from_core(1)
    from_core(-1)
    from_core(0)
    for s in (1, -1):
        zgot(s, 2, 1 - lead[s])
        zsend(s, 1, 1 - lead[s], True)
    for h in (1, 0):
        a_sum[pl.ds(2 * h, 2)] = a.total(h)
        b_sum[pl.ds(2 * h, 2)] = b.total(h)
    second_a = Ring(cp, "c", "x", x, lambda dest, h: a_sum.at[dest, pl.ds(h, 1)], c_far, c_near, c_made)
    second_b = Ring(cp, "d", "y", y, lambda dest, h: b_sum.at[dest, pl.ds(h, 1)], d_far, d_near, d_made)
    second_a.begin()
    second_b.begin()
    for s in (1, -1):
        zgot(s, 2, lead[s])
        zsend(s, 1, lead[s], True)
    second_a.pass_on()
    second_b.pass_on()
    for sub in (0, 1):
        zgot(1, 1, sub)
        zgot(-1, 1, sub)
        value = mine(0, sub) + z_in[slot[1, 1, sub]] + z_in[slot[-1, 1, sub]]
        ring = second_a if sub == 0 else second_b
        for h in (0, 1):
            out[2 * sub + h] = value[h] + ring.total(h)[0]
    cp.drain()


def reduce(grad):
    vmem = pl.BlockSpec(memory_space=pltpu.VMEM)
    tile = (TILE, TILE)
    f32 = jnp.float32

    def ring(blocks):
        return [pltpu.VMEM((2,) + blocks + tile, f32), pltpu.VMEM((2, 2) + blocks + tile, f32),
                pltpu.VMEM((2,) + blocks + tile, f32)]

    first, second = (2, 2), (1,)
    return pl.pallas_call(
        reduce_kernel,
        out_shape=jax.ShapeDtypeStruct((QUARTER,) + tile, f32),
        in_specs=[vmem],
        out_specs=vmem,
        scratch_shapes=ring(first) + [pltpu.VMEM((4, 2) + tile, f32)]
        + ring(first) + [pltpu.VMEM((4, 2) + tile, f32)]
        + ring(second) + ring(second)
        + [
            pltpu.VMEM((NZ, QUARTER) + tile, f32),
            pltpu.VMEM((14, 2) + tile, f32),
            pltpu.VMEM((14, 2) + tile, f32),
            pltpu.SemaphoreType.DMA((REDUCE_SEMS,)),
            pltpu.SemaphoreType.DMA((REDUCE_SEMS,)),
        ],
        compiler_params=pltpu.CompilerParams(
            collective_id=1, has_side_effects=True, vmem_limit_bytes=REDUCE_VMEM
        ),
        name="reduce_rows",
    )(grad)


def body(latent, left_block, right_block, slot_kind, edge_cols):
    edges = edge_cols.reshape(NZ, NY, NC, 2, NBR, TILE)
    ids = [v[0, 0].T.reshape(2, 1, PEERS) for v in (left_block, right_block, slot_kind)]
    high, low, edge, entry = gather(latent, edges, *ids)
    grad = compute(entry, high, low, edge)
    out = reduce(grad)
    return out.reshape(QUARTER * TILE, TILE)


def solution(mesh):
    fine = Mesh(mesh.devices.reshape(NZ, NY, NC, NX), ("z", "y", "core", "x"))
    rows = ("z", "y", "core")
    return jax.shard_map(
        body,
        mesh=fine,
        in_specs=(
            P(rows, None),
            P(rows, "x", None, None),
            P(rows, "x", None, None),
            P(rows, "x", None, None),
            P(rows, "x", None, None, None, None),
        ),
        out_specs=P(("z", "y", "core", "x"), None),
        check_vma=False,
    )
```

```python
import functools

import jax
import jax.numpy as jnp
from jax import lax
from jax.experimental import pallas as pl
from jax.experimental.pallas import tpu as pltpu
from jax.sharding import Mesh
from jax.sharding import PartitionSpec as P

NZ, NY, NC, NX = 8, 4, 2, 4
BLOCKS = 16
QUARTER = 4
TILE = 128
NBR = 8
OWN = NY * BLOCKS
MOVED = NZ * NC * QUARTER
ALL = OWN + MOVED
PLANES = NZ + 1
CAND = PLANES * NY * NC
META = NY + NZ * NC
PARTS = ALL // 16
TRASH = ALL
GROUP = 12
MESH = pl.DeviceIdType.MESH
GATHER_VMEM, SLOT_VMEM, REDUCE_VMEM = 32 << 20, 24 << 20, 28 << 20

NT = (((1,), (1,)), ((), ()))
NN = (((1,), (0,)), ((), ()))


def position():
    return tuple(lax.axis_index(name) for name in ("z", "y", "core", "x"))


def step_of(value, by, size):
    return lax.rem(value + (by + size), size)


class Copies:
    def __init__(self, send_sems, recv_sems):
        self.send_sems, self.recv_sems = send_sems, recv_sems
        self.index = {}
        self.sent = []

    def sems(self, name):
        at = self.index.setdefault(name, len(self.index))
        return self.send_sems.at[at], self.recv_sems.at[at]

    def make(self, name, src, dst, device):
        send, recv = self.sems(name)
        return pltpu.make_async_remote_copy(
            src_ref=src, dst_ref=dst, send_sem=send, recv_sem=recv,
            device_id=device, device_id_type=MESH,
        )

    def start(self, name, src, dst, device, when=None):
        copy = self.make(name, src, dst, device)
        self.sent.append((copy, when))
        if when is None:
            copy.start()
        else:
            pl.when(when)(copy.start)

    def arrived(self, name, landed, device, when=None):
        copy = self.make(name, landed, landed, device)
        if when is None:
            copy.wait_recv()
        else:
            pl.when(when)(copy.wait_recv)

    def drain(self):
        for copy, when in self.sent:
            if when is None:
                copy.wait_send()
            else:
                pl.when(when)(copy.wait_send)


GATHER_SEMS = 128
IDS = 3
ROWS = BLOCKS * TILE
SHARE = 192
HALF_SHARE = SHARE // 2
DIRECT = NX * SHARE
HALF_DIRECT = (ROWS - DIRECT) // 2
SPLIT_FROM = DIRECT // TILE
PEERS = NZ * NY * NC


def entries(meta, entry, z, y, c, x):
    step = NY * NC

    def one(q, carry):
        def write(rows, own_ids, moved_ids, kinds, yo, zc, plane, flip, live):
            cc = zc & 1
            own_at = yo * BLOCKS + own_ids
            moved_at = OWN + zc * QUARTER + moved_ids - x * QUARTER
            left, right = (moved_at, own_at) if flip else (own_at, moved_at)
            where = (q * PLANES + plane) * step + yo * NC + cc
            value = left + right * 256 + where * 65536 + jnp.where(kinds == 2, 1 << 28, 0)
            take = live & ((moved_ids >> 2) == x)
            entry[q, rows, :, pl.ds(0, PEERS)] = jnp.where(take, value + (1 << 30), 0)

        shape = (NY, 1, PEERS)
        s = lax.broadcasted_iota(jnp.int32, shape, 2)
        yo = lax.broadcasted_iota(jnp.int32, shape, 0)
        rows = pl.ds(0, NY)
        lb, rb, kind = [meta[q, rows, v] for v in range(IDS)]
        live = s >= z * step + yo * NC + c
        write(rows, lb, rb, kind, yo, (s >> 3) * NC + (s & 1), s >> 3, False, live)

        shape = (NZ * NC, 1, PEERS)
        s = lax.broadcasted_iota(jnp.int32, shape, 2)
        zc = lax.broadcasted_iota(jnp.int32, shape, 0)
        rows = pl.ds(NY, NZ * NC)
        lb, rb, kind = [meta[q, rows, v] for v in range(IDS)]
        zz = zc >> 1
        live = zz * step + y * NC + (zc & 1) <= s
        write(rows, rb, lb, kind, (s >> 1) & 3, zc, jnp.where(zz == z, NZ, zz), True, live)
        return carry

    lax.fori_loop(0, NX, one, 0)


def gather_kernel(lat, edges, lefts, rights, kinds, high, low, edge, entry, land, meta, ids,
                  send_sems, recv_sems, local_sems, id_sems):
    z, y, c, x = position()
    other = 1 - c
    ys = [step_of(y, d, NY) for d in range(NY)]
    yd = {1: ys[1], -1: ys[3], 2: ys[2]}
    xd = {1: step_of(x, 1, NX), -1: step_of(x, -1, NX), 2: step_of(x, 2, NX)}
    zd = {d: step_of(z, d, NZ) for d in range(-4, NZ)}
    cp = Copies(send_sems, recv_sems)
    cs = [c, other]

    barrier = pltpu.get_barrier_semaphore()
    peers = [{"y": ys[d]} for d in (1, 2, 3)] + [{"x": xd[1]}, {"x": xd[-1]}]
    peers += [{"z": zd[dz], "core": cs[dc]} for dz in range(NZ) for dc in range(NC) if dz or dc]
    for peer in peers:
        pl.semaphore_signal(barrier, inc=1, device_id=peer, device_id_type=MESH)

    local = []

    def here(src, dst, when=None):
        copy = pltpu.make_async_copy(src, dst, local_sems.at[len(local)])
        local.append((copy, when))
        if when is None:
            copy.start()
        else:
            pl.when(when)(copy.start)

    def moved_at(zz, cc):
        return PARTS // 2 + zz // 2, (lax.rem(zz, 2) * NC + cc) * QUARTER

    def rows_of(part, start, count):
        return land.at[part, pl.ds(start, count)]

    def moved_rows(zz, cc):
        p, block = moved_at(zz, cc)
        return rows_of(p, block * TILE, QUARTER * TILE)

    def direct(half):
        return DIRECT + half * HALF_DIRECT

    raw = [pltpu.make_async_copy(ref, ids.at[:, v], id_sems.at[v])
           for v, ref in enumerate((lefts, rights, kinds))]
    for copy in raw:
        copy.start()
    for zp in range(NZ):
        here(edges.at[zp, y, :, 0], edge.at[x, zp, y], zp >= z)
    here(edges.at[z, :, c, 1], edge.at[x, NZ, :, c])
    edge_local = len(local)
    here(lat, land.at[y])
    here(lat.at[pl.ds(x * QUARTER * TILE, QUARTER * TILE)], moved_rows(z, c))

    for copy in raw:
        copy.wait()
    own_ids = [pltpu.make_async_copy(ids.at[0], meta.at[x, y], id_sems.at[0]),
               pltpu.make_async_copy(ids.at[1], meta.at[x, NY + z * NC + c], id_sems.at[1])]
    for copy in own_ids:
        copy.start()
    pl.semaphore_wait(barrier, len(peers))

    def moved_sub(zz, cc, sub):
        p, block = moved_at(zz, cc)
        return rows_of(p, (block + 2 * sub) * TILE, 2 * TILE)

    def zsend(sign, step, sub):
        origin = zd[-(step - 1)] if sign > 0 else zd[step - 1]
        dst = moved_sub(origin, c, sub)
        src = lat.at[pl.ds((x * QUARTER + 2 * sub) * TILE, 2 * TILE)] if step == 1 else dst
        cp.start(("z", sign, step, sub), src, dst, {"z": zd[sign]})

    def zgot(sign, step, sub):
        origin = zd[-step] if sign > 0 else zd[step]
        cp.arrived(("z", sign, step, sub), moved_sub(origin, c, sub), {"z": zd[-sign]})

    def to_core(key, origin, src):
        cp.start(("core", key), src, moved_rows(origin, c), {"core": other})

    def split(part, start, count=QUARTER):
        def one(j, carry):
            at = start + 2 * j
            value = land[part, pl.ds(pl.multiple_of(at * TILE, TILE), 2 * TILE)].reshape(2, TILE, TILE)
            top = value.astype(jnp.bfloat16)
            high[pl.ds(part * BLOCKS + at, 2)] = top
            low[pl.ds(part * BLOCKS + at, 2)] = (value - top.astype(jnp.float32)).astype(jnp.bfloat16)
            return carry

        lax.fori_loop(0, count // 2, one, 0)

    lead = {1: 0, -1: 1}

    for s in (1, -1):
        cp.start(("yx", s), lat.at[pl.ds(x * SHARE, SHARE)], rows_of(y, x * SHARE, SHARE), {"y": yd[s]})
    for d in (1, 2, 3):
        for zp in range(NZ):
            cp.start(("e0", d, zp), edges.at[zp, ys[d], :, 0], edge.at[x, zp, y], {"y": ys[d]}, zp >= z)
        cp.start(("m0", d), ids.at[0], meta.at[x, y], {"y": ys[d]})
    for dz in range(NZ):
        for dc in range(NC):
            if dz or dc:
                zs, cc = zd[dz], cs[dc]
                plane = NZ if dz == 0 else z
                cp.start(("e1", dz, dc), edges.at[zs, :, cc, 1], edge.at[x, plane, :, c],
                         {"z": zs, "core": cc}, zs >= z)
                cp.start(("m1", dz, dc), ids.at[1], meta.at[x, NY + z * NC + c],
                         {"z": zs, "core": cc})
    for s in (1, -1):
        zsend(s, 1, lead[s])
    for s in (1, -1):
        h = lead[s]
        cp.start(("yd", s, h), lat.at[pl.ds(direct(h), HALF_DIRECT)], rows_of(y, direct(h), HALF_DIRECT), {"y": yd[s]})
    for s in (1, -1):
        zsend(s, 1, 1 - lead[s])
    to_core(0, z, lat.at[pl.ds(x * QUARTER * TILE, QUARTER * TILE)])

    for copy, when in local[edge_local:]:
        copy.wait()
    split(y, 0, BLOCKS)
    split(*moved_at(z, c))
    def xpart(row, origin, s, half):
        h = half if s > 0 else 1 - half
        return rows_of(row, origin * SHARE + h * HALF_SHARE, HALF_SHARE)

    def xsend(key, row, half):
        for s in (1, -1):
            ref = xpart(row, x, s, half)
            cp.start(("xo", key, s, half), ref, ref, {"x": xd[s]})

    def xgot(key, row, half, relay):
        for s in (1, -1):
            origin = xd[-s]
            ref = xpart(row, origin, s, half)
            cp.arrived(("xo", key, s, half), ref, {"x": origin})
            if relay:
                cp.start(("xr", key, s), ref, ref, {"x": xd[s]})

    def zstep(step, k):
        for s in (1, -1):
            sub = lead[s] if k == 0 else 1 - lead[s]
            zgot(s, step, sub)
            if step < 3 or (step == 3 and k == 0):
                zsend(s, step + 1, sub)

    def zdone(step):
        for s in (1, -1):
            if step < 4 or s == 1:
                origin = zd[-s * step] if step < 4 else zd[4]
                to_core((s, step), origin, moved_rows(origin, c))

    for s in (1, -1):
        row = yd[-s]
        cp.arrived(("yx", s), rows_of(row, x * SHARE, SHARE), {"y": row})
        ref = xpart(row, x, s, 0)
        cp.start(("yxr", s), ref, ref, {"y": yd[s]})
    for s in (1, -1):
        h = 1 - lead[s]
        cp.start(("yd", s, h), lat.at[pl.ds(direct(h), HALF_DIRECT)], rows_of(y, direct(h), HALF_DIRECT), {"y": yd[s]})
    for half in (0, 1):
        for key in (1, -1):
            xsend(key, yd[key], half)
    zstep(1, 0)

    for copy in own_ids:
        copy.wait()
    for copy, when in local[:edge_local]:
        if when is None:
            copy.wait()
        else:
            pl.when(when)(copy.wait)
    for d in (1, 2, 3):
        src = ys[NY - d]
        for zp in range(NZ):
            cp.arrived(("e0", d, zp), edge.at[x, zp, src], {"y": src}, zp >= z)
        cp.arrived(("m0", d), meta.at[x, src], {"y": src})
    for dz in range(NZ):
        for dc in range(NC):
            if dz or dc:
                zr, cr = zd[(NZ - dz) % NZ], cs[dc]
                plane = NZ if dz == 0 else zr
                cp.arrived(("e1", dz, dc), edge.at[x, plane, :, cr], {"z": zr, "core": cr}, zr <= z)
                cp.arrived(("m1", dz, dc), meta.at[x, NY + zr * NC + cr], {"z": zr, "core": cr})
    pieces = {0: pl.ds(0, 5), 1: pl.ds(5, 4)}
    for s in (1, -1):
        cp.start(("xm", s), meta.at[x], meta.at[x], {"x": xd[s]})
    for k in (0, 1):
        for s in (1, -1):
            h = lead[s] if k == 0 else 1 - lead[s]
            cp.start(("xe", s, h), edge.at[x, pieces[h]], edge.at[x, pieces[h]], {"x": xd[s]})

    zstep(1, 1)
    zdone(1)
    for s in (1, -1):
        h, row = lead[s], yd[-s]
        ref = rows_of(row, direct(h), HALF_DIRECT)
        cp.arrived(("yd", s, h), ref, {"y": row})
        cp.start(("ydr", s), ref, ref, {"y": yd[s]})
    zstep(2, 0)
    for s in (1, -1):
        ref = xpart(yd[2], x, s, 0)
        cp.arrived(("yxr", s), ref, {"y": yd[-s]})
    for half in (0, 1):
        xsend(2, yd[2], half)
    for key in (1, -1):
        xgot(key, yd[key], 0, True)
    zstep(2, 1)
    zdone(2)
    for s in (1, -1):
        h, src = lead[s], xd[-s]
        cp.arrived(("xm", s), meta.at[src], {"x": src})
        if s > 0:
            cp.start(("xmr", s), meta.at[src], meta.at[src], {"x": xd[s]})
        cp.arrived(("xe", s, h), edge.at[src, pieces[h]], {"x": src})
        cp.start(("xer", s), edge.at[src, pieces[h]], edge.at[src, pieces[h]], {"x": xd[s]})
    xgot(2, yd[2], 0, True)
    zstep(3, 0)
    zstep(3, 1)
    zdone(3)
    cp.arrived(("core", 0), moved_rows(z, other), {"core": other})
    split(*moved_at(z, other))
    for step in (1, 2):
        for s in (1, -1):
            origin = zd[-s * step]
            cp.arrived(("core", (s, step)), moved_rows(origin, other), {"core": other})
            split(*moved_at(origin, other))
            split(*moved_at(origin, c))
    for s in (1, -1):
        h, row = 1 - lead[s], yd[-s]
        cp.arrived(("yd", s, h), rows_of(row, direct(h), HALF_DIRECT), {"y": row})
        split(row, SPLIT_FROM, BLOCKS - SPLIT_FROM)
    zstep(4, 0)
    zdone(4)
    for s in (1, -1):
        origin = zd[-s * 3]
        cp.arrived(("core", (s, 3)), moved_rows(origin, other), {"core": other})
        split(*moved_at(origin, other))
        split(*moved_at(origin, c))
    split(*moved_at(zd[4], c))
    for s in (1, -1):
        cp.arrived(("ydr", s), rows_of(yd[2], direct(lead[s]), HALF_DIRECT), {"y": yd[-s]})
    split(yd[2], SPLIT_FROM, BLOCKS - SPLIT_FROM)
    for key in (1, -1, 2):
        xgot(key, yd[key], 1, False)
        for s in (1, -1):
            cp.arrived(("xr", key, s), xpart(yd[key], xd[2], s, 0), {"x": xd[-s]})
        split(yd[key], 0, SPLIT_FROM)
    for s in (1, -1):
        h, src = 1 - lead[s], xd[-s]
        if s > 0:
            cp.arrived(("xmr", s), meta.at[xd[2]], {"x": src})
    entries(meta, entry, z, y, c, x)
    for s in (1, -1):
        h, src = 1 - lead[s], xd[-s]
        cp.arrived(("xe", s, h), edge.at[src, pieces[h]], {"x": src})
        cp.arrived(("xer", s), edge.at[xd[2], pieces[1 - h]], {"x": src})
    cp.arrived(("core", (1, 4)), moved_rows(zd[4], other), {"core": other})
    split(*moved_at(zd[4], other))
    cp.drain()


def gather(lat, edges, lefts, rights, kinds):
    hbm = pl.BlockSpec(memory_space=pltpu.HBM)
    vmem = pl.BlockSpec(memory_space=pltpu.VMEM)
    return pl.pallas_call(
        gather_kernel,
        out_shape=(
            jax.ShapeDtypeStruct((ALL + 1, TILE, TILE), jnp.bfloat16),
            jax.ShapeDtypeStruct((ALL + 1, TILE, TILE), jnp.bfloat16),
            jax.ShapeDtypeStruct((NX, PLANES, NY, NC, NBR, TILE), jnp.int32),
            jax.ShapeDtypeStruct((NX, META, 1, TILE), jnp.int32),
        ),
        in_specs=[hbm] * 5,
        out_specs=(vmem,) * 4,
        scratch_shapes=[
            pltpu.VMEM((PARTS, ROWS, TILE), jnp.float32),
            pltpu.VMEM((NX, META, IDS, 1, PEERS), jnp.int32),
            pltpu.VMEM((NC, IDS, 1, PEERS), jnp.int32),
            pltpu.SemaphoreType.DMA((GATHER_SEMS,)),
            pltpu.SemaphoreType.DMA((GATHER_SEMS,)),
            pltpu.SemaphoreType.DMA((16,)),
            pltpu.SemaphoreType.DMA((IDS,)),
        ],
        compiler_params=pltpu.CompilerParams(
            collective_id=0, has_side_effects=True, vmem_limit_bytes=GATHER_VMEM
        ),
        name="gather_rows",
    )(*[pltpu.with_memory_space_constraint(v, pltpu.HBM) for v in (lat, edges, lefts, rights, kinds)])


def product(x, w, dims):
    left = jnp.concatenate(x, axis=1)
    none = jnp.zeros_like(w[0])
    if dims is NT:
        right = jnp.concatenate(
            [jnp.concatenate([w[0], w[0]], axis=1), jnp.concatenate([w[1], none], axis=1)], axis=0
        )
    else:
        right = jnp.concatenate(
            [jnp.concatenate([w[0], w[1]], axis=1), jnp.concatenate([w[0], none], axis=1)], axis=0
        )
    both = lax.dot_general(left, right, dims, preferred_element_type=jnp.float32)
    return both[:, :TILE] + both[:, TILE:]


def residue(left, right, edges, positive):
    scores = product(right, left, NT)
    bit = jnp.where(positive, lax.shift_left(jnp.ones_like(edges), edges & 31), 0)
    word = edges >> 5
    rows = lax.broadcasted_iota(jnp.int32, (NBR, TILE), 0)
    words, tests = [], []
    for w in range(4):
        have = jnp.where(word == w, bit, 0)
        for shift in (4, 2, 1):
            have = have | pltpu.roll(have, shift, 0)
        words += [have] * 4
        tests.append(lax.shift_left(jnp.ones_like(edges), rows + 8 * w))
    hit = (jnp.concatenate(words, axis=0) & jnp.concatenate(tests * 4, axis=0)) != 0
    value = 1.0 / (1.0 + jnp.exp(-scores)) - jnp.where(hit, 1.0, 0.0)
    top = value.astype(jnp.bfloat16)
    return top, (value - top.astype(jnp.float32)).astype(jnp.bfloat16)


def compute_kernel(entry, high, low, edge, grad, slots, held):
    z, y, c, x = position()

    def put(part, places, count):
        size = 8
        values = [entry[at] for at in places[:size]]
        for k in range(0, len(places), size):
            following = [entry[at] for at in places[k + size : k + 2 * size]]
            grad[part, k // size] = jnp.zeros((4, TILE, TILE), jnp.float32)
            for value in values:
                slots[count] = value
                count = count + (value >> 30)
            values = following
        return count

    def first(zz, count):
        base = zz * (NY * NC) + y * NC
        return put(zz, [base + (q * META + yo) * TILE + cc
                    for q in range(NX) for yo in range(NY) for cc in range(NC)], count)

    def second(zz, count):
        base = zz * (NC * TILE) + z * (NY * NC) + c
        return put(jnp.where(zz == z, NZ, zz), [base + (q * META + NY + cc) * TILE + yo * NC
                    for q in range(NX) for yo in range(NY) for cc in range(NC)], count)

    nothing = TRASH + TRASH * 256
    count = lax.fori_loop(z, NZ, first, 0)
    count = lax.fori_loop(0, z + 1, second, count)
    for k in range(GROUP):
        slots[count + k] = nothing
    steps = jnp.maximum((count + GROUP - 1) // GROUP, 1)

    def parts(value):
        return value & 255, (value >> 8) & 255, (value >> 16) & 4095, (value >> 28) & 1

    def block(at):
        return high[at], low[at]

    def add(at, value):
        p, s, j = at // 16, lax.rem(at // 4, 4), lax.rem(at, 4)
        grad[p, s, j] += value

    def residues(step, k):
        li, ri, where, positive = parts(slots[step * GROUP + k])
        held[k, 0], held[k, 1] = residue(block(li), block(ri), edge[where], positive > 0)

    def gradients(step, k, kept):
        li, ri, _, _ = parts(slots[step * GROUP + k])
        left, right = block(li), block(ri)
        gr = product(kept, left, NN)
        gl = product((kept[0].T, kept[1].T), right, NN)
        return li, ri, gl, gr

    def flush(done):
        for li, ri, gl, gr in done:
            add(li, gl)
            add(ri, gr)

    def work(step, carry):
        done = []
        for k in range(GROUP):
            kept = held[k, 0], held[k, 1]
            residues(step, k)
            done.append(gradients(step - 1, k, kept))
        flush(done)
        return carry

    for k in range(GROUP):
        residues(0, k)
    lax.fori_loop(1, steps, work, 0)
    flush([gradients(steps - 1, k, (held[k, 0], held[k, 1])) for k in range(GROUP)])


def compute(entry, high, low, edges):
    smem = pl.BlockSpec(memory_space=pltpu.SMEM)
    vmem = pl.BlockSpec(memory_space=pltpu.VMEM)
    return pl.pallas_call(
        compute_kernel,
        out_shape=jax.ShapeDtypeStruct((PARTS + 1, 4, 4, TILE, TILE), jnp.float32),
        in_specs=[smem, vmem, vmem, vmem],
        out_specs=vmem,
        scratch_shapes=[
            pltpu.SMEM((NX * CAND + 3 * GROUP,), jnp.int32),
            pltpu.VMEM((GROUP, 2, TILE, TILE), jnp.bfloat16),
        ],
        compiler_params=pltpu.CompilerParams(vmem_limit_bytes=SLOT_VMEM),
        name="slot_gradients",
    )(entry.reshape(NX * META * TILE), high, low,
      edges.reshape(NX * CAND, NBR, TILE))


class Ring:
    def __init__(self, cp, name, axis, at, part, far, near, made):
        self.cp, self.name, self.axis, self.part = cp, name, axis, part
        self.far, self.near, self.made = far, near, made
        self.at = {d: step_of(at, d, 4) for d in (-1, 0, 1, 2)}

    def to(self, sign):
        return {self.axis: self.at[sign]}

    def begin(self):
        for k, s in enumerate((1, -1)):
            self.cp.start((self.name, "far", s), self.part(self.at[2], k), self.far.at[k], self.to(s))
        for k, s in enumerate((1, -1)):
            h = 1 - k
            self.cp.start((self.name, "near", s, h), self.part(self.at[s], h), self.near.at[k, h], self.to(s))

    def pass_on(self):
        for k, s in enumerate((1, -1)):
            self.cp.arrived((self.name, "far", s), self.far.at[k], self.to(-s))
            self.made[k] = self.part(self.at[s], k)[...] + self.far[k]
            self.cp.start((self.name, "near", s, k), self.made.at[k], self.near.at[k, k], self.to(s))

    def total(self, half):
        for k, s in enumerate((1, -1)):
            self.cp.arrived((self.name, "near", s, half), self.near.at[k, half], self.to(-s))
        return self.part(self.at[0], half)[...] + self.near[0, half] + self.near[1, half]


REDUCE_SEMS = 64


def reduce_kernel(grad, out, a_far, a_near, a_made, a_sum, b_far, b_near, b_made, b_sum,
                  c_far, c_near, c_made, d_far, d_near, d_made,
                  partner, z_in, z_out, send_sems, recv_sems):
    z, y, c, x = position()
    other = 1 - c
    zd = {d: step_of(z, d, NZ) for d in range(-4, 5)}
    cp = Copies(send_sems, recv_sems)

    barrier = pltpu.get_barrier_semaphore()
    peers = [{"y": step_of(y, 1, NY)}, {"y": step_of(y, -1, NY)}, {"x": step_of(x, 1, NX)},
             {"x": step_of(x, -1, NX)}, {"z": zd[1]}, {"z": zd[-1]}, {"core": other}]
    for peer in peers:
        pl.semaphore_signal(barrier, inc=1, device_id=peer, device_id_type=MESH)
    pl.semaphore_wait(barrier, len(peers))

    a = Ring(cp, "a", "y", y, lambda dest, h: grad.at[dest, pl.ds(2 * h, 2), pl.ds(0, 2)], a_far, a_near, a_made)
    b = Ring(cp, "b", "x", x, lambda dest, h: grad.at[pl.ds(2 * h, 2), dest, pl.ds(2, 2)], b_far, b_near, b_made)

    def moved_at(d, cc):
        return PARTS // 2 + zd[d] // 2, lax.rem(zd[d], 2) * NC + cc

    order = [4, 3, -3, 2, -2, 1, -1, 0]
    for d in order:
        cp.start(("p", d), grad.at[moved_at(d, other)], partner.at[zd[d]], {"core": other})
    a.begin()
    b.begin()

    slot = {}
    for s in (1, -1):
        for d in (4, 3, 2, 1):
            for sub in (0, 1):
                if d < 4 or sub == (0 if s > 0 else 1):
                    slot[s, d, sub] = len(slot)

    def mine(d, sub):
        p, s = moved_at(d, c)
        return grad[p, s, pl.ds(2 * sub, 2)] + partner[zd[d], pl.ds(2 * sub, 2)]

    def zsend(s, d, sub, received):
        at = slot[s, d, sub]
        value = mine(s * d if d < 4 else 4, sub)
        if received:
            value = value + z_in[slot[s, d + 1, sub]]
        z_out[at] = value
        cp.start(("z", s, d, sub), z_out.at[at], z_in.at[at], {"z": zd[s]})

    def zgot(s, d, sub):
        cp.arrived(("z", s, d, sub), z_in.at[slot[s, d, sub]], {"z": zd[-s]})

    def from_core(d):
        cp.arrived(("p", d), partner.at[zd[d]], {"core": other})

    lead = {1: 0, -1: 1}
    from_core(4)
    for s in (1, -1):
        zsend(s, 4, lead[s], False)
    for s in (1, -1):
        from_core(3 * s)
        zsend(s, 3, 1 - lead[s], False)
    from_core(2)
    from_core(-2)
    for s in (1, -1):
        zgot(s, 4, lead[s])
        zsend(s, 3, lead[s], True)
    a.pass_on()
    b.pass_on()
    for s in (1, -1):
        zgot(s, 3, 1 - lead[s])
        zsend(s, 2, 1 - lead[s], True)
    for s in (1, -1):
        zgot(s, 3, lead[s])
        zsend(s, 2, lead[s], True)
    from_core(1)
    from_core(-1)
    from_core(0)
    for s in (1, -1):
        zgot(s, 2, 1 - lead[s])
        zsend(s, 1, 1 - lead[s], True)
    for h in (1, 0):
        a_sum[pl.ds(2 * h, 2)] = a.total(h)
        b_sum[pl.ds(2 * h, 2)] = b.total(h)
    second_a = Ring(cp, "c", "x", x, lambda dest, h: a_sum.at[dest, pl.ds(h, 1)], c_far, c_near, c_made)
    second_b = Ring(cp, "d", "y", y, lambda dest, h: b_sum.at[dest, pl.ds(h, 1)], d_far, d_near, d_made)
    second_a.begin()
    second_b.begin()
    for s in (1, -1):
        zgot(s, 2, lead[s])
        zsend(s, 1, lead[s], True)
    second_a.pass_on()
    second_b.pass_on()
    for sub in (0, 1):
        zgot(1, 1, sub)
        zgot(-1, 1, sub)
        value = mine(0, sub) + z_in[slot[1, 1, sub]] + z_in[slot[-1, 1, sub]]
        ring = second_a if sub == 0 else second_b
        for h in (0, 1):
            out[2 * sub + h] = value[h] + ring.total(h)[0]
    cp.drain()


def reduce(grad):
    vmem = pl.BlockSpec(memory_space=pltpu.VMEM)
    tile = (TILE, TILE)
    f32 = jnp.float32

    def ring(blocks):
        return [pltpu.VMEM((2,) + blocks + tile, f32), pltpu.VMEM((2, 2) + blocks + tile, f32),
                pltpu.VMEM((2,) + blocks + tile, f32)]

    first, second = (2, 2), (1,)
    return pl.pallas_call(
        reduce_kernel,
        out_shape=jax.ShapeDtypeStruct((QUARTER,) + tile, f32),
        in_specs=[vmem],
        out_specs=vmem,
        scratch_shapes=ring(first) + [pltpu.VMEM((4, 2) + tile, f32)]
        + ring(first) + [pltpu.VMEM((4, 2) + tile, f32)]
        + ring(second) + ring(second)
        + [
            pltpu.VMEM((NZ, QUARTER) + tile, f32),
            pltpu.VMEM((14, 2) + tile, f32),
            pltpu.VMEM((14, 2) + tile, f32),
            pltpu.SemaphoreType.DMA((REDUCE_SEMS,)),
            pltpu.SemaphoreType.DMA((REDUCE_SEMS,)),
        ],
        compiler_params=pltpu.CompilerParams(
            collective_id=1, has_side_effects=True, vmem_limit_bytes=REDUCE_VMEM
        ),
        name="reduce_rows",
    )(grad)


def body(latent, left_block, right_block, slot_kind, edge_cols):
    edges = edge_cols.reshape(NZ, NY, NC, 2, NBR, TILE)
    ids = [v[0, 0].T.reshape(2, 1, PEERS) for v in (left_block, right_block, slot_kind)]
    high, low, edge, entry = gather(latent, edges, *ids)
    grad = compute(entry, high, low, edge)
    out = reduce(grad)
    return out.reshape(QUARTER * TILE, TILE)


def solution(mesh):
    fine = Mesh(mesh.devices.reshape(NZ, NY, NC, NX), ("z", "y", "core", "x"))
    rows = ("z", "y", "core")
    return jax.shard_map(
        body,
        mesh=fine,
        in_specs=(
            P(rows, None),
            P(rows, "x", None, None),
            P(rows, "x", None, None),
            P(rows, "x", None, None),
            P(rows, "x", None, None, None, None),
        ),
        out_specs=P(("z", "y", "core", "x"), None),
        check_vma=False,
    )
```

```python
import functools

import jax
import jax.numpy as jnp
from jax import lax
from jax.experimental import pallas as pl
from jax.experimental.pallas import tpu as pltpu
from jax.sharding import Mesh
from jax.sharding import PartitionSpec as P

NZ, NY, NC, NX = 8, 4, 2, 4
BLOCKS = 16
QUARTER = 4
TILE = 128
NBR = 8
OWN = NY * BLOCKS
MOVED = NZ * NC * QUARTER
ALL = OWN + MOVED
PLANES = NZ + 1
CAND = PLANES * NY * NC
META = NY + NZ * NC
PARTS = ALL // 16
TRASH = ALL
GROUP = 14
MESH = pl.DeviceIdType.MESH
GATHER_VMEM, SLOT_VMEM, REDUCE_VMEM = 32 << 20, 24 << 20, 28 << 20

NT = (((1,), (1,)), ((), ()))
NN = (((1,), (0,)), ((), ()))


def position():
    return tuple(lax.axis_index(name) for name in ("z", "y", "core", "x"))


def step_of(value, by, size):
    return lax.rem(value + (by + size), size)


class Copies:
    def __init__(self, send_sems, recv_sems):
        self.send_sems, self.recv_sems = send_sems, recv_sems
        self.index = {}
        self.sent = []

    def sems(self, name):
        at = self.index.setdefault(name, len(self.index))
        return self.send_sems.at[at], self.recv_sems.at[at]

    def make(self, name, src, dst, device):
        send, recv = self.sems(name)
        return pltpu.make_async_remote_copy(
            src_ref=src, dst_ref=dst, send_sem=send, recv_sem=recv,
            device_id=device, device_id_type=MESH,
        )

    def start(self, name, src, dst, device, when=None):
        copy = self.make(name, src, dst, device)
        self.sent.append((copy, when))
        if when is None:
            copy.start()
        else:
            pl.when(when)(copy.start)

    def arrived(self, name, landed, device, when=None):
        copy = self.make(name, landed, landed, device)
        if when is None:
            copy.wait_recv()
        else:
            pl.when(when)(copy.wait_recv)

    def drain(self):
        for copy, when in self.sent:
            if when is None:
                copy.wait_send()
            else:
                pl.when(when)(copy.wait_send)


GATHER_SEMS = 128
IDS = 3
ROWS = BLOCKS * TILE
SHARE = 192
HALF_SHARE = SHARE // 2
DIRECT = NX * SHARE
HALF_DIRECT = (ROWS - DIRECT) // 2
SPLIT_FROM = DIRECT // TILE
PEERS = NZ * NY * NC


def entries(meta, entry, z, y, c, x):
    step = NY * NC

    def one(q, carry):
        def write(rows, own_ids, moved_ids, kinds, yo, zc, plane, flip, live):
            cc = zc & 1
            own_at = yo * BLOCKS + own_ids
            moved_at = OWN + zc * QUARTER + moved_ids - x * QUARTER
            left, right = (moved_at, own_at) if flip else (own_at, moved_at)
            where = (q * PLANES + plane) * step + yo * NC + cc
            value = left + right * 256 + where * 65536 + jnp.where(kinds == 2, 1 << 28, 0)
            take = live & ((moved_ids >> 2) == x)
            entry[q, rows, :, pl.ds(0, PEERS)] = jnp.where(take, value + (1 << 30), 0)

        shape = (NY, 1, PEERS)
        s = lax.broadcasted_iota(jnp.int32, shape, 2)
        yo = lax.broadcasted_iota(jnp.int32, shape, 0)
        rows = pl.ds(0, NY)
        lb, rb, kind = [meta[q, rows, v] for v in range(IDS)]
        live = s >= z * step + yo * NC + c
        write(rows, lb, rb, kind, yo, (s >> 3) * NC + (s & 1), s >> 3, False, live)

        shape = (NZ * NC, 1, PEERS)
        s = lax.broadcasted_iota(jnp.int32, shape, 2)
        zc = lax.broadcasted_iota(jnp.int32, shape, 0)
        rows = pl.ds(NY, NZ * NC)
        lb, rb, kind = [meta[q, rows, v] for v in range(IDS)]
        zz = zc >> 1
        live = zz * step + y * NC + (zc & 1) <= s
        write(rows, rb, lb, kind, (s >> 1) & 3, zc, jnp.where(zz == z, NZ, zz), True, live)
        return carry

    lax.fori_loop(0, NX, one, 0)


def gather_kernel(lat, edges, lefts, rights, kinds, high, low, edge, entry, land, meta, ids,
                  send_sems, recv_sems, local_sems, id_sems):
    z, y, c, x = position()
    other = 1 - c
    ys = [step_of(y, d, NY) for d in range(NY)]
    yd = {1: ys[1], -1: ys[3], 2: ys[2]}
    xd = {1: step_of(x, 1, NX), -1: step_of(x, -1, NX), 2: step_of(x, 2, NX)}
    zd = {d: step_of(z, d, NZ) for d in range(-4, NZ)}
    cp = Copies(send_sems, recv_sems)
    cs = [c, other]

    barrier = pltpu.get_barrier_semaphore()
    peers = [{"y": ys[d]} for d in (1, 2, 3)] + [{"x": xd[1]}, {"x": xd[-1]}]
    peers += [{"z": zd[dz], "core": cs[dc]} for dz in range(NZ) for dc in range(NC) if dz or dc]
    for peer in peers:
        pl.semaphore_signal(barrier, inc=1, device_id=peer, device_id_type=MESH)

    local = []

    def here(src, dst, when=None):
        copy = pltpu.make_async_copy(src, dst, local_sems.at[len(local)])
        local.append((copy, when))
        if when is None:
            copy.start()
        else:
            pl.when(when)(copy.start)

    def moved_at(zz, cc):
        return PARTS // 2 + zz // 2, (lax.rem(zz, 2) * NC + cc) * QUARTER

    def rows_of(part, start, count):
        return land.at[part, pl.ds(start, count)]

    def moved_rows(zz, cc):
        p, block = moved_at(zz, cc)
        return rows_of(p, block * TILE, QUARTER * TILE)

    def direct(half):
        return DIRECT + half * HALF_DIRECT

    raw = [pltpu.make_async_copy(ref, ids.at[:, v], id_sems.at[v])
           for v, ref in enumerate((lefts, rights, kinds))]
    for copy in raw:
        copy.start()
    for zp in range(NZ):
        here(edges.at[zp, y, :, 0], edge.at[x, zp, y], zp >= z)
    here(edges.at[z, :, c, 1], edge.at[x, NZ, :, c])
    edge_local = len(local)
    here(lat, land.at[y])
    here(lat.at[pl.ds(x * QUARTER * TILE, QUARTER * TILE)], moved_rows(z, c))

    for copy in raw:
        copy.wait()
    own_ids = [pltpu.make_async_copy(ids.at[0], meta.at[x, y], id_sems.at[0]),
               pltpu.make_async_copy(ids.at[1], meta.at[x, NY + z * NC + c], id_sems.at[1])]
    for copy in own_ids:
        copy.start()
    pl.semaphore_wait(barrier, len(peers))

    def moved_sub(zz, cc, sub):
        p, block = moved_at(zz, cc)
        return rows_of(p, (block + 2 * sub) * TILE, 2 * TILE)

    def zsend(sign, step, sub):
        origin = zd[-(step - 1)] if sign > 0 else zd[step - 1]
        dst = moved_sub(origin, c, sub)
        src = lat.at[pl.ds((x * QUARTER + 2 * sub) * TILE, 2 * TILE)] if step == 1 else dst
        cp.start(("z", sign, step, sub), src, dst, {"z": zd[sign]})

    def zgot(sign, step, sub):
        origin = zd[-step] if sign > 0 else zd[step]
        cp.arrived(("z", sign, step, sub), moved_sub(origin, c, sub), {"z": zd[-sign]})

    def to_core(key, origin, src):
        cp.start(("core", key), src, moved_rows(origin, c), {"core": other})

    def split(part, start, count=QUARTER):
        def one(j, carry):
            at = start + 2 * j
            value = land[part, pl.ds(pl.multiple_of(at * TILE, TILE), 2 * TILE)].reshape(2, TILE, TILE)
            top = value.astype(jnp.bfloat16)
            high[pl.ds(part * BLOCKS + at, 2)] = top
            low[pl.ds(part * BLOCKS + at, 2)] = (value - top.astype(jnp.float32)).astype(jnp.bfloat16)
            return carry

        lax.fori_loop(0, count // 2, one, 0)

    lead = {1: 0, -1: 1}

    for s in (1, -1):
        cp.start(("yx", s), lat.at[pl.ds(x * SHARE, SHARE)], rows_of(y, x * SHARE, SHARE), {"y": yd[s]})
    for d in (1, 2, 3):
        for zp in range(NZ):
            cp.start(("e0", d, zp), edges.at[zp, ys[d], :, 0], edge.at[x, zp, y], {"y": ys[d]}, zp >= z)
        cp.start(("m0", d), ids.at[0], meta.at[x, y], {"y": ys[d]})
    for dz in range(NZ):
        for dc in range(NC):
            if dz or dc:
                zs, cc = zd[dz], cs[dc]
                plane = NZ if dz == 0 else z
                cp.start(("e1", dz, dc), edges.at[zs, :, cc, 1], edge.at[x, plane, :, c],
                         {"z": zs, "core": cc}, zs >= z)
                cp.start(("m1", dz, dc), ids.at[1], meta.at[x, NY + z * NC + c],
                         {"z": zs, "core": cc})
    for s in (1, -1):
        zsend(s, 1, lead[s])
    for s in (1, -1):
        h = lead[s]
        cp.start(("yd", s, h), lat.at[pl.ds(direct(h), HALF_DIRECT)], rows_of(y, direct(h), HALF_DIRECT), {"y": yd[s]})
    for s in (1, -1):
        zsend(s, 1, 1 - lead[s])
    to_core(0, z, lat.at[pl.ds(x * QUARTER * TILE, QUARTER * TILE)])

    for copy, when in local[edge_local:]:
        copy.wait()
    split(y, 0, BLOCKS)
    split(*moved_at(z, c))
    def xpart(row, origin, s, half):
        h = half if s > 0 else 1 - half
        return rows_of(row, origin * SHARE + h * HALF_SHARE, HALF_SHARE)

    def xsend(key, row, half):
        for s in (1, -1):
            ref = xpart(row, x, s, half)
            cp.start(("xo", key, s, half), ref, ref, {"x": xd[s]})

    def xgot(key, row, half, relay):
        for s in (1, -1):
            origin = xd[-s]
            ref = xpart(row, origin, s, half)
            cp.arrived(("xo", key, s, half), ref, {"x": origin})
            if relay:
                cp.start(("xr", key, s), ref, ref, {"x": xd[s]})

    def zstep(step, k):
        for s in (1, -1):
            sub = lead[s] if k == 0 else 1 - lead[s]
            zgot(s, step, sub)
            if step < 3 or (step == 3 and k == 0):
                zsend(s, step + 1, sub)

    def zdone(step):
        for s in (1, -1):
            if step < 4 or s == 1:
                origin = zd[-s * step] if step < 4 else zd[4]
                to_core((s, step), origin, moved_rows(origin, c))

    for s in (1, -1):
        row = yd[-s]
        cp.arrived(("yx", s), rows_of(row, x * SHARE, SHARE), {"y": row})
        ref = xpart(row, x, s, 0)
        cp.start(("yxr", s), ref, ref, {"y": yd[s]})
    for s in (1, -1):
        h = 1 - lead[s]
        cp.start(("yd", s, h), lat.at[pl.ds(direct(h), HALF_DIRECT)], rows_of(y, direct(h), HALF_DIRECT), {"y": yd[s]})
    for half in (0, 1):
        for key in (1, -1):
            xsend(key, yd[key], half)
    zstep(1, 0)

    for copy in own_ids:
        copy.wait()
    for copy, when in local[:edge_local]:
        if when is None:
            copy.wait()
        else:
            pl.when(when)(copy.wait)
    for d in (1, 2, 3):
        src = ys[NY - d]
        for zp in range(NZ):
            cp.arrived(("e0", d, zp), edge.at[x, zp, src], {"y": src}, zp >= z)
        cp.arrived(("m0", d), meta.at[x, src], {"y": src})
    for dz in range(NZ):
        for dc in range(NC):
            if dz or dc:
                zr, cr = zd[(NZ - dz) % NZ], cs[dc]
                plane = NZ if dz == 0 else zr
                cp.arrived(("e1", dz, dc), edge.at[x, plane, :, cr], {"z": zr, "core": cr}, zr <= z)
                cp.arrived(("m1", dz, dc), meta.at[x, NY + zr * NC + cr], {"z": zr, "core": cr})
    pieces = {0: pl.ds(0, 5), 1: pl.ds(5, 4)}
    for s in (1, -1):
        cp.start(("xm", s), meta.at[x], meta.at[x], {"x": xd[s]})
    for k in (0, 1):
        for s in (1, -1):
            h = lead[s] if k == 0 else 1 - lead[s]
            cp.start(("xe", s, h), edge.at[x, pieces[h]], edge.at[x, pieces[h]], {"x": xd[s]})

    zstep(1, 1)
    zdone(1)
    for s in (1, -1):
        h, row = lead[s], yd[-s]
        ref = rows_of(row, direct(h), HALF_DIRECT)
        cp.arrived(("yd", s, h), ref, {"y": row})
        cp.start(("ydr", s), ref, ref, {"y": yd[s]})
    zstep(2, 0)
    for s in (1, -1):
        ref = xpart(yd[2], x, s, 0)
        cp.arrived(("yxr", s), ref, {"y": yd[-s]})
    for half in (0, 1):
        xsend(2, yd[2], half)
    for key in (1, -1):
        xgot(key, yd[key], 0, True)
    zstep(2, 1)
    zdone(2)
    for s in (1, -1):
        h, src = lead[s], xd[-s]
        cp.arrived(("xm", s), meta.at[src], {"x": src})
        if s > 0:
            cp.start(("xmr", s), meta.at[src], meta.at[src], {"x": xd[s]})
        cp.arrived(("xe", s, h), edge.at[src, pieces[h]], {"x": src})
        cp.start(("xer", s), edge.at[src, pieces[h]], edge.at[src, pieces[h]], {"x": xd[s]})
    xgot(2, yd[2], 0, True)
    zstep(3, 0)
    zstep(3, 1)
    zdone(3)
    cp.arrived(("core", 0), moved_rows(z, other), {"core": other})
    split(*moved_at(z, other))
    for step in (1, 2):
        for s in (1, -1):
            origin = zd[-s * step]
            cp.arrived(("core", (s, step)), moved_rows(origin, other), {"core": other})
            split(*moved_at(origin, other))
            split(*moved_at(origin, c))
    for s in (1, -1):
        h, row = 1 - lead[s], yd[-s]
        cp.arrived(("yd", s, h), rows_of(row, direct(h), HALF_DIRECT), {"y": row})
        split(row, SPLIT_FROM, BLOCKS - SPLIT_FROM)
    zstep(4, 0)
    zdone(4)
    for s in (1, -1):
        origin = zd[-s * 3]
        cp.arrived(("core", (s, 3)), moved_rows(origin, other), {"core": other})
        split(*moved_at(origin, other))
        split(*moved_at(origin, c))
    split(*moved_at(zd[4], c))
    for s in (1, -1):
        cp.arrived(("ydr", s), rows_of(yd[2], direct(lead[s]), HALF_DIRECT), {"y": yd[-s]})
    split(yd[2], SPLIT_FROM, BLOCKS - SPLIT_FROM)
    for key in (1, -1, 2):
        xgot(key, yd[key], 1, False)
        for s in (1, -1):
            cp.arrived(("xr", key, s), xpart(yd[key], xd[2], s, 0), {"x": xd[-s]})
        split(yd[key], 0, SPLIT_FROM)
    for s in (1, -1):
        h, src = 1 - lead[s], xd[-s]
        if s > 0:
            cp.arrived(("xmr", s), meta.at[xd[2]], {"x": src})
    entries(meta, entry, z, y, c, x)
    for s in (1, -1):
        h, src = 1 - lead[s], xd[-s]
        cp.arrived(("xe", s, h), edge.at[src, pieces[h]], {"x": src})
        cp.arrived(("xer", s), edge.at[xd[2], pieces[1 - h]], {"x": src})
    cp.arrived(("core", (1, 4)), moved_rows(zd[4], other), {"core": other})
    split(*moved_at(zd[4], other))
    cp.drain()


def gather(lat, edges, lefts, rights, kinds):
    hbm = pl.BlockSpec(memory_space=pltpu.HBM)
    vmem = pl.BlockSpec(memory_space=pltpu.VMEM)
    return pl.pallas_call(
        gather_kernel,
        out_shape=(
            jax.ShapeDtypeStruct((ALL + 1, TILE, TILE), jnp.bfloat16),
            jax.ShapeDtypeStruct((ALL + 1, TILE, TILE), jnp.bfloat16),
            jax.ShapeDtypeStruct((NX, PLANES, NY, NC, NBR, TILE), jnp.int32),
            jax.ShapeDtypeStruct((NX, META, 1, TILE), jnp.int32),
        ),
        in_specs=[hbm] * 5,
        out_specs=(vmem,) * 4,
        scratch_shapes=[
            pltpu.VMEM((PARTS, ROWS, TILE), jnp.float32),
            pltpu.VMEM((NX, META, IDS, 1, PEERS), jnp.int32),
            pltpu.VMEM((NC, IDS, 1, PEERS), jnp.int32),
            pltpu.SemaphoreType.DMA((GATHER_SEMS,)),
            pltpu.SemaphoreType.DMA((GATHER_SEMS,)),
            pltpu.SemaphoreType.DMA((16,)),
            pltpu.SemaphoreType.DMA((IDS,)),
        ],
        compiler_params=pltpu.CompilerParams(
            collective_id=0, has_side_effects=True, vmem_limit_bytes=GATHER_VMEM
        ),
        name="gather_rows",
    )(*[pltpu.with_memory_space_constraint(v, pltpu.HBM) for v in (lat, edges, lefts, rights, kinds)])


def product(x, w, dims):
    left = jnp.concatenate(x, axis=1)
    none = jnp.zeros_like(w[0])
    if dims is NT:
        right = jnp.concatenate(
            [jnp.concatenate([w[0], w[0]], axis=1), jnp.concatenate([w[1], none], axis=1)], axis=0
        )
    else:
        right = jnp.concatenate(
            [jnp.concatenate([w[0], w[1]], axis=1), jnp.concatenate([w[0], none], axis=1)], axis=0
        )
    both = lax.dot_general(left, right, dims, preferred_element_type=jnp.float32)
    return both[:, :TILE] + both[:, TILE:]


def residue(left, right, edges, positive):
    scores = product(right, left, NT)
    bit = jnp.where(positive, lax.shift_left(jnp.ones_like(edges), edges & 31), 0)
    word = edges >> 5
    rows = lax.broadcasted_iota(jnp.int32, (NBR, TILE), 0)
    words, tests = [], []
    for w in range(4):
        have = jnp.where(word == w, bit, 0)
        for shift in (4, 2, 1):
            have = have | pltpu.roll(have, shift, 0)
        words += [have] * 4
        tests.append(lax.shift_left(jnp.ones_like(edges), rows + 8 * w))
    hit = (jnp.concatenate(words, axis=0) & jnp.concatenate(tests * 4, axis=0)) != 0
    value = 1.0 / (1.0 + jnp.exp(-scores)) - jnp.where(hit, 1.0, 0.0)
    top = value.astype(jnp.bfloat16)
    return top, (value - top.astype(jnp.float32)).astype(jnp.bfloat16)


def compute_kernel(entry, high, low, edge, grad, slots, held):
    z, y, c, x = position()

    def put(part, places, count):
        size = 8
        values = [entry[at] for at in places[:size]]
        for k in range(0, len(places), size):
            following = [entry[at] for at in places[k + size : k + 2 * size]]
            grad[part, k // size] = jnp.zeros((4, TILE, TILE), jnp.float32)
            for value in values:
                slots[count] = value
                count = count + (value >> 30)
            values = following
        return count

    def first(zz, count):
        base = zz * (NY * NC) + y * NC
        return put(zz, [base + (q * META + yo) * TILE + cc
                    for q in range(NX) for yo in range(NY) for cc in range(NC)], count)

    def second(zz, count):
        base = zz * (NC * TILE) + z * (NY * NC) + c
        return put(jnp.where(zz == z, NZ, zz), [base + (q * META + NY + cc) * TILE + yo * NC
                    for q in range(NX) for yo in range(NY) for cc in range(NC)], count)

    nothing = TRASH + TRASH * 256
    count = lax.fori_loop(z, NZ, first, 0)
    count = lax.fori_loop(0, z + 1, second, count)
    for k in range(GROUP):
        slots[count + k] = nothing
    steps = jnp.maximum((count + GROUP - 1) // GROUP, 1)

    def parts(value):
        return value & 255, (value >> 8) & 255, (value >> 16) & 4095, (value >> 28) & 1

    def block(at):
        return high[at], low[at]

    def add(at, value):
        p, s, j = at // 16, lax.rem(at // 4, 4), lax.rem(at, 4)
        grad[p, s, j] += value

    def residues(step, k):
        li, ri, where, positive = parts(slots[step * GROUP + k])
        held[k, 0], held[k, 1] = residue(block(li), block(ri), edge[where], positive > 0)

    def gradients(step, k, kept):
        li, ri, _, _ = parts(slots[step * GROUP + k])
        left, right = block(li), block(ri)
        gr = product(kept, left, NN)
        gl = product((kept[0].T, kept[1].T), right, NN)
        return li, ri, gl, gr

    def flush(done):
        for li, ri, gl, gr in done:
            add(li, gl)
            add(ri, gr)

    def work(step, carry):
        done = []
        for k in range(GROUP):
            kept = held[k, 0], held[k, 1]
            residues(step, k)
            done.append(gradients(step - 1, k, kept))
        flush(done)
        return carry

    for k in range(GROUP):
        residues(0, k)
    lax.fori_loop(1, steps, work, 0)
    flush([gradients(steps - 1, k, (held[k, 0], held[k, 1])) for k in range(GROUP)])


def compute(entry, high, low, edges):
    smem = pl.BlockSpec(memory_space=pltpu.SMEM)
    vmem = pl.BlockSpec(memory_space=pltpu.VMEM)
    return pl.pallas_call(
        compute_kernel,
        out_shape=jax.ShapeDtypeStruct((PARTS + 1, 4, 4, TILE, TILE), jnp.float32),
        in_specs=[smem, vmem, vmem, vmem],
        out_specs=vmem,
        scratch_shapes=[
            pltpu.SMEM((NX * CAND + 3 * GROUP,), jnp.int32),
            pltpu.VMEM((GROUP, 2, TILE, TILE), jnp.bfloat16),
        ],
        compiler_params=pltpu.CompilerParams(vmem_limit_bytes=SLOT_VMEM),
        name="slot_gradients",
    )(entry.reshape(NX * META * TILE), high, low,
      edges.reshape(NX * CAND, NBR, TILE))


class Ring:
    def __init__(self, cp, name, axis, at, part, far, near, made):
        self.cp, self.name, self.axis, self.part = cp, name, axis, part
        self.far, self.near, self.made = far, near, made
        self.at = {d: step_of(at, d, 4) for d in (-1, 0, 1, 2)}

    def to(self, sign):
        return {self.axis: self.at[sign]}

    def begin(self):
        for k, s in enumerate((1, -1)):
            self.cp.start((self.name, "far", s), self.part(self.at[2], k), self.far.at[k], self.to(s))
        for k, s in enumerate((1, -1)):
            h = 1 - k
            self.cp.start((self.name, "near", s, h), self.part(self.at[s], h), self.near.at[k, h], self.to(s))

    def pass_on(self):
        for k, s in enumerate((1, -1)):
            self.cp.arrived((self.name, "far", s), self.far.at[k], self.to(-s))
            self.made[k] = self.part(self.at[s], k)[...] + self.far[k]
            self.cp.start((self.name, "near", s, k), self.made.at[k], self.near.at[k, k], self.to(s))

    def total(self, half):
        for k, s in enumerate((1, -1)):
            self.cp.arrived((self.name, "near", s, half), self.near.at[k, half], self.to(-s))
        return self.part(self.at[0], half)[...] + self.near[0, half] + self.near[1, half]


REDUCE_SEMS = 64


def reduce_kernel(grad, out, a_far, a_near, a_made, a_sum, b_far, b_near, b_made, b_sum,
                  c_far, c_near, c_made, d_far, d_near, d_made,
                  partner, z_in, z_out, send_sems, recv_sems):
    z, y, c, x = position()
    other = 1 - c
    zd = {d: step_of(z, d, NZ) for d in range(-4, 5)}
    cp = Copies(send_sems, recv_sems)

    barrier = pltpu.get_barrier_semaphore()
    peers = [{"y": step_of(y, 1, NY)}, {"y": step_of(y, -1, NY)}, {"x": step_of(x, 1, NX)},
             {"x": step_of(x, -1, NX)}, {"z": zd[1]}, {"z": zd[-1]}, {"core": other}]
    for peer in peers:
        pl.semaphore_signal(barrier, inc=1, device_id=peer, device_id_type=MESH)
    pl.semaphore_wait(barrier, len(peers))

    a = Ring(cp, "a", "y", y, lambda dest, h: grad.at[dest, pl.ds(2 * h, 2), pl.ds(0, 2)], a_far, a_near, a_made)
    b = Ring(cp, "b", "x", x, lambda dest, h: grad.at[pl.ds(2 * h, 2), dest, pl.ds(2, 2)], b_far, b_near, b_made)

    def moved_at(d, cc):
        return PARTS // 2 + zd[d] // 2, lax.rem(zd[d], 2) * NC + cc

    order = [4, 3, -3, 2, -2, 1, -1, 0]
    for d in order:
        cp.start(("p", d), grad.at[moved_at(d, other)], partner.at[zd[d]], {"core": other})
    a.begin()
    b.begin()

    slot = {}
    for s in (1, -1):
        for d in (4, 3, 2, 1):
            for sub in (0, 1):
                if d < 4 or sub == (0 if s > 0 else 1):
                    slot[s, d, sub] = len(slot)

    def mine(d, sub):
        p, s = moved_at(d, c)
        return grad[p, s, pl.ds(2 * sub, 2)] + partner[zd[d], pl.ds(2 * sub, 2)]

    def zsend(s, d, sub, received):
        at = slot[s, d, sub]
        value = mine(s * d if d < 4 else 4, sub)
        if received:
            value = value + z_in[slot[s, d + 1, sub]]
        z_out[at] = value
        cp.start(("z", s, d, sub), z_out.at[at], z_in.at[at], {"z": zd[s]})

    def zgot(s, d, sub):
        cp.arrived(("z", s, d, sub), z_in.at[slot[s, d, sub]], {"z": zd[-s]})

    def from_core(d):
        cp.arrived(("p", d), partner.at[zd[d]], {"core": other})

    lead = {1: 0, -1: 1}
    from_core(4)
    for s in (1, -1):
        zsend(s, 4, lead[s], False)
    for s in (1, -1):
        from_core(3 * s)
        zsend(s, 3, 1 - lead[s], False)
    from_core(2)
    from_core(-2)
    for s in (1, -1):
        zgot(s, 4, lead[s])
        zsend(s, 3, lead[s], True)
    a.pass_on()
    b.pass_on()
    for s in (1, -1):
        zgot(s, 3, 1 - lead[s])
        zsend(s, 2, 1 - lead[s], True)
    for s in (1, -1):
        zgot(s, 3, lead[s])
        zsend(s, 2, lead[s], True)
    from_core(1)
    from_core(-1)
    from_core(0)
    for s in (1, -1):
        zgot(s, 2, 1 - lead[s])
        zsend(s, 1, 1 - lead[s], True)
    for h in (1, 0):
        a_sum[pl.ds(2 * h, 2)] = a.total(h)
        b_sum[pl.ds(2 * h, 2)] = b.total(h)
    second_a = Ring(cp, "c", "x", x, lambda dest, h: a_sum.at[dest, pl.ds(h, 1)], c_far, c_near, c_made)
    second_b = Ring(cp, "d", "y", y, lambda dest, h: b_sum.at[dest, pl.ds(h, 1)], d_far, d_near, d_made)
    second_a.begin()
    second_b.begin()
    for s in (1, -1):
        zgot(s, 2, lead[s])
        zsend(s, 1, lead[s], True)
    second_a.pass_on()
    second_b.pass_on()
    for sub in (0, 1):
        zgot(1, 1, sub)
        zgot(-1, 1, sub)
        value = mine(0, sub) + z_in[slot[1, 1, sub]] + z_in[slot[-1, 1, sub]]
        ring = second_a if sub == 0 else second_b
        for h in (0, 1):
            out[2 * sub + h] = value[h] + ring.total(h)[0]
    cp.drain()


def reduce(grad):
    vmem = pl.BlockSpec(memory_space=pltpu.VMEM)
    tile = (TILE, TILE)
    f32 = jnp.float32

    def ring(blocks):
        return [pltpu.VMEM((2,) + blocks + tile, f32), pltpu.VMEM((2, 2) + blocks + tile, f32),
                pltpu.VMEM((2,) + blocks + tile, f32)]

    first, second = (2, 2), (1,)
    return pl.pallas_call(
        reduce_kernel,
        out_shape=jax.ShapeDtypeStruct((QUARTER,) + tile, f32),
        in_specs=[vmem],
        out_specs=vmem,
        scratch_shapes=ring(first) + [pltpu.VMEM((4, 2) + tile, f32)]
        + ring(first) + [pltpu.VMEM((4, 2) + tile, f32)]
        + ring(second) + ring(second)
        + [
            pltpu.VMEM((NZ, QUARTER) + tile, f32),
            pltpu.VMEM((14, 2) + tile, f32),
            pltpu.VMEM((14, 2) + tile, f32),
            pltpu.SemaphoreType.DMA((REDUCE_SEMS,)),
            pltpu.SemaphoreType.DMA((REDUCE_SEMS,)),
        ],
        compiler_params=pltpu.CompilerParams(
            collective_id=1, has_side_effects=True, vmem_limit_bytes=REDUCE_VMEM
        ),
        name="reduce_rows",
    )(grad)


def body(latent, left_block, right_block, slot_kind, edge_cols):
    edges = edge_cols.reshape(NZ, NY, NC, 2, NBR, TILE)
    ids = [v[0, 0].T.reshape(2, 1, PEERS) for v in (left_block, right_block, slot_kind)]
    high, low, edge, entry = gather(latent, edges, *ids)
    grad = compute(entry, high, low, edge)
    out = reduce(grad)
    return out.reshape(QUARTER * TILE, TILE)


def solution(mesh):
    fine = Mesh(mesh.devices.reshape(NZ, NY, NC, NX), ("z", "y", "core", "x"))
    rows = ("z", "y", "core")
    return jax.shard_map(
        body,
        mesh=fine,
        in_specs=(
            P(rows, None),
            P(rows, "x", None, None),
            P(rows, "x", None, None),
            P(rows, "x", None, None),
            P(rows, "x", None, None, None, None),
        ),
        out_specs=P(("z", "y", "core", "x"), None),
        check_vma=False,
    )
```
